256 devices in a mesh: req: 64 (over y, z, x_lo), grp: 4 (over x_hi, core).
Axes of the slice: x: 4 (x_hi: 2, x_lo: 2; x = x_hi * 2 + x_lo), y: 4, z: 8, core: 2. Of those that a mesh axis runs over, the one named last changes fastest.
Arguments:
- suffix_queries: bfloat16 [4, 8192, 1024], P('grp', 'req'), may hold values from -140 to 140
- suffix_keys: bfloat16 [4, 8192, 1024], P('grp', 'req'), may hold values from -6 to 6
- suffix_values: bfloat16 [4, 8192, 1024], P('grp', 'req'), may hold values from -6 to 6
- prefix_cache: bfloat16 [4, 256, 2048], P('grp', 'req'), may hold values from -6 to 6
- residual: bfloat16 [4, 8192, 2048], P('grp', 'req'), may hold values from -6 to 6
- out_weight: bfloat16 [1024, 2048], P(('req', 'grp')), may hold values from -0.1875 to 0.1875
- norm_gain: float32 [2048], replicated, may hold values from 0.5 to 1.5
- routes: int32 [4, 8192, 4], P('grp', 'req'), may hold values from 0 to 63, all different within a row; in each aligned block of 128 rows (0 to 127, 128 to 255, ..., all dimensions but the last counted through in order) at most 10 rows name the same one
- route_weights: float32 [4, 8192, 4], P('grp', 'req'), may hold values from 0.05 to 0.6
- lengths: int32 [4, 16], P('grp'), may hold values from 1 to 1024, 8192 in all within a row
- migrate: int32 [2, 512], P(None, 'req'), may hold values 0 or 1
- expert_gate: bfloat16 [64, 2048, 704], P('req', None, 'grp'), may hold values from -0.125 to 0.125
- expert_up: bfloat16 [64, 2048, 704], P('req', None, 'grp'), may hold values from -0.125 to 0.125
- expert_down: bfloat16 [64, 704, 2048], P('req', 'grp'), may hold values from -0.21875 to 0.21875
- shared_gate: bfloat16 [2048, 2816], P(None, 'grp'), may hold values from -0.125 to 0.125
- shared_up: bfloat16 [2048, 2816], P(None, 'grp'), may hold values from -0.125 to 0.125
- shared_down: bfloat16 [2816, 2048], P('grp'), may hold values from -0.109375 to 0.109375
- shared_router: bfloat16 [2048], replicated, may hold values from -0.125 to 0.125
Outputs:
- hidden_out: bfloat16 [4, 8192, 2048], P('grp', 'req')
- suffix_cache: bfloat16 [4, 8192, 2048], P('grp', 'req')
The draws below stay inside these ranges and needn't reach their ends.
Inputs may be any that keep to these rules, and one draw needn't show every extreme that they name: In each aligned block of 128 tokens no expert is named by more than 10 routes, a bound that some block reaches. Each group's lengths sum to 8192; the longest is exactly 1024.
All inputs are finite; a program needn't handle non-finite values. No bound on the sum of `migrate` on one device may be relied on, other than what follows from the above.
Results may differ from the reference program's by a relative error of at most 0.0069.
Values may be sent and summed in bfloat16 or wider, within the bound.
A program may use at most 128 MiB of HBM per device.

```python
import math
import jax
import jax.numpy as jnp
import numpy as np
from jax import lax

D = 2048
HD = 128
HEADS = 8
EFF = 704
SH = 2816
TOP = 4
PG = 16
REQS = 16
TOK_DEV = 128
EXPERTS = 64
CAP = 10
TOKENS_G = 8192
PREFIX = 256
MAXLEN = 1024
HIST = 8
GROUPS = 4
PAGES = 512


def joint_draw(key):
    base = jax.random.fold_in(key, 17)
    key_first, key_second = jax.random.split(base, 2)
    shape = (GROUPS, TOKENS_G, HEADS * HD)
    key_field = jnp.clip(jax.random.normal(key_first, shape, jnp.float32), -6.0, 6.0)
    query_field = jnp.clip(4.0 * jax.random.normal(key_second, shape, jnp.float32), -24.0, 24.0)
    return (query_field, key_field)


def draw_suffix_queries(key, part):
    return joint_draw(key)[0].astype(jnp.bfloat16)


def draw_suffix_keys(key, part):
    return joint_draw(key)[1].astype(jnp.bfloat16)


def with_ends(array, own_key, low, largest):
    shape = array.shape
    spot = [jax.random.randint(jax.random.fold_in(own_key, axis), (), 0, shape[axis]) for axis in range(len(shape))]
    array = array.at[tuple(spot)].set(low)
    longest = shape.index(max(shape))
    spot[longest] = (spot[longest] + 1) % shape[longest]
    return array.at[tuple(spot)].set(largest)


def block_scale(own_key, dims, cuts, smallest, high):
    loudness = 1.0
    for dim, shards_of in cuts:
        steps = jax.random.uniform(jax.random.fold_in(jax.random.fold_in(own_key, 6), dim), (shards_of,), jnp.float32, smallest / len(cuts), high / len(cuts))
        loudness = loudness * jnp.repeat(jnp.exp(steps), dims[dim] // shards_of).reshape((-1,) + (1,) * (len(dims) - 1 - dim))
    return loudness


def length_profile(count, total, bound, skew):
    loads = [(1 << 20) // math.isqrt(grade ** skew) + 1 for grade in range(2, count + 1)]
    spare, counts = total - bound - (count - 1), [1] * (count - 1)
    while spare > 0:
        movable = [i for i in range(count - 1) if counts[i] < bound]
        pool, left = sum([loads[i] for i in movable]), spare
        for i in movable:
            more = min(bound - counts[i], max(1, left * loads[i] // pool), spare)
            counts[i] = counts[i] + more
            spare = spare - more
    return np.array([bound] + counts)


def ragged_sizes(key, number_of, total, bound, lean):
    if number_of == 2:
        one = jax.random.randint(key, (), max(1, total - bound), min(bound, total - 1) + 1)
        return jnp.stack([one, total - one])
    sizes = jnp.asarray(length_profile(number_of, total, bound, lean), jnp.int32)
    couples = (number_of - 1) // 2
    donor, receiver = sizes[1:1 + 2 * couples:2], sizes[2:2 + 2 * couples:2]
    margin = jnp.minimum(donor - 1, bound - receiver)
    passed = jax.random.randint(jax.random.fold_in(key, 1), (couples,), 0, 1 << 20) % (margin + 1)
    sizes = sizes.at[1:1 + 2 * couples:2].set(donor - passed).at[2:2 + 2 * couples:2].set(receiver + passed)
    return sizes[jax.random.permutation(jax.random.fold_in(key, 2), number_of)]


def assign_block(own_key, own, number, rows, number_of, top, limit, lean):
    ranking = jax.random.permutation(own_key, number_of)
    crowded, usual = load_shares(number_of, rows * top, limit, lean, True), load_shares(number_of, rows * top, limit, lean, False)
    places = jnp.arange(number_of)

    def named(sizes, offset_by):
        used = int((sizes > 0).sum())
        fixed = max(1, used // 4)
        shifted = fixed + (places - fixed + offset_by * (used - fixed)) % max(1, number_of - fixed)
        return jnp.zeros((number_of,), jnp.int32).at[ranking[jnp.where(places < fixed, places, shifted)]].set(jnp.asarray(sizes, jnp.int32))

    sizes = jnp.where(number % 4 == 0, named(crowded, number // 4), named(usual, number - number // 4 - 1))
    mixed = jax.random.permutation(jax.random.fold_in(own, 3), number_of)
    source_of, sink = mixed[0:number_of // 2 * 2:2], mixed[1:number_of // 2 * 2:2]
    slack = jnp.minimum(sizes[source_of] - 1, limit - sizes[sink]) // 2
    slack = jnp.where((source_of == ranking[0]) | (sink == ranking[0]) | (sizes[sink] == 0), 0, jnp.maximum(slack, 0))
    shifted = jax.random.randint(jax.random.fold_in(own, 4), (number_of // 2,), 0, 1 << 20) % (slack + 1)
    sizes = sizes.at[source_of].add(-shifted).at[sink].add(shifted)
    items = jnp.searchsorted(jnp.cumsum(sizes), jnp.arange(rows * top), side="right").astype(jnp.int32)
    listing = items.reshape(top, rows).T
    listing = listing[jax.random.permutation(jax.random.fold_in(own, 1), rows)]
    offset_by = jax.random.randint(jax.random.fold_in(own, 2), (rows, 1), 0, top)
    return jnp.take_along_axis(listing, (jnp.arange(top)[None, :] + offset_by) % top, axis=1)


def load_shares(amount, total, reach, lean, full):
    portions = [(1 << 20) // math.isqrt(grade ** lean) + 1 for grade in range(1, amount + 1)]
    largest = reach if full else min(reach, max(-(-total // amount), total * portions[0] // sum(portions)))
    least = 1 if total - largest >= amount - 1 else 0
    holding, rest = [largest] + [least] * (amount - 1), total - largest - least * (amount - 1)
    while rest > 0:
        free = [i for i in range(1, amount) if holding[i] < largest] or [i for i in range(1, amount) if holding[i] < reach]
        pool, left = sum([portions[i] for i in free]), rest
        for i in free:
            extra = min(reach - holding[i], max(1, left * portions[i] // pool), rest)
            holding[i] = holding[i] + extra
            rest = rest - extra
    return np.array(holding)


def bell_draw(stream_key, extent, spread, bound, cuts=(), kind=jnp.bfloat16):
    level = block_scale(stream_key, extent, cuts, -0.22, 0.18) if cuts else 1.0
    values = jax.random.normal(stream_key, extent, jnp.float32) * spread * level
    return jnp.minimum(jnp.maximum(values, -bound), bound).astype(kind)


def setup_inputs(seed: int = 0) -> dict:
    streams_of = jax.random.split(jax.random.key(seed), 19)
    suffix_queries = draw_suffix_queries(jax.random.fold_in(streams_of[18], 71), 0)
    suffix_keys = draw_suffix_keys(jax.random.fold_in(streams_of[18], 71), 0)
    suffix_values = bell_draw(streams_of[2], (GROUPS, TOKENS_G, HEADS * HD), 1.0, 6.0, ((0, 4), (1, 64)))
    prefix_cache = bell_draw(streams_of[3], (GROUPS, PREFIX, 2 * HEADS * HD), 1.0, 6.0, ((0, 4), (1, 64)))
    residual = bell_draw(streams_of[4], (GROUPS, TOKENS_G, D), 1.0, 6.0, ((0, 4), (1, 64)))
    out_weight = bell_draw(streams_of[5], (HEADS * HD, D), (HEADS * HD) ** -0.5, 0.1875, ((0, 256),))
    norm_gain = jnp.clip(1.0 + 0.1 * jax.random.normal(streams_of[6], (D,), jnp.float32), 0.5, 1.5)
    routes_keys = jax.random.split(jax.random.fold_in(streams_of[7], 1), GROUPS * TOKENS_G // TOK_DEV)
    routes_turns = jax.random.permutation(jax.random.fold_in(streams_of[7], 3), GROUPS * TOKENS_G // TOK_DEV)
    routes = jax.vmap(lambda own, number: assign_block(jax.random.fold_in(streams_of[7], 2), own, number, TOK_DEV, EXPERTS, TOP, CAP, 2))(routes_keys, routes_turns).reshape((GROUPS, TOKENS_G, TOP))
    route_weights = jnp.clip(jnp.exp(math.log(0.6) - 2.4849067 * jax.random.uniform(streams_of[8], (GROUPS, TOKENS_G, TOP), jnp.float32) ** block_scale(streams_of[8], (GROUPS, TOKENS_G, TOP), ((0, 4), (1, 64)), -0.2, 0.2)), 0.05, 0.6)
    lengths = jax.vmap(lambda own: ragged_sizes(own, REQS, TOKENS_G, MAXLEN, 2))(jax.random.split(streams_of[9], GROUPS)).reshape((GROUPS, REQS)).astype(jnp.int32)
    migrate = with_ends((jax.random.randint(streams_of[10], (GROUPS // 2, PAGES), 0, 2) < 1).astype(jnp.int32), jax.random.fold_in(streams_of[10], 1), 0, 1)
    expert_gate = bell_draw(streams_of[11], (EXPERTS, D, EFF), D ** -0.5, 0.125, ((0, 64), (2, 4)))
    expert_up = bell_draw(streams_of[12], (EXPERTS, D, EFF), D ** -0.5, 0.125, ((0, 64), (2, 4)))
    expert_down = bell_draw(streams_of[13], (EXPERTS, EFF, D), EFF ** -0.5, 0.21875, ((0, 64), (1, 4)))
    shared_gate = bell_draw(streams_of[14], (D, SH), D ** -0.5, 0.125, ((1, 4),))
    shared_up = bell_draw(streams_of[15], (D, SH), D ** -0.5, 0.125, ((1, 4),))
    shared_down = bell_draw(streams_of[16], (SH, D), SH ** -0.5, 0.109375, ((0, 4),))
    shared_router = bell_draw(streams_of[17], (D,), D ** -0.5, 0.125)
    return {"suffix_queries": suffix_queries, "suffix_keys": suffix_keys, "suffix_values": suffix_values, "prefix_cache": prefix_cache, "residual": residual, "out_weight": out_weight, "norm_gain": norm_gain, "routes": routes, "route_weights": route_weights, "lengths": lengths, "migrate": migrate, "expert_gate": expert_gate, "expert_up": expert_up, "expert_down": expert_down, "shared_gate": shared_gate, "shared_up": shared_up, "shared_down": shared_down, "shared_router": shared_router}


ROPE_BASE = 1000000.0
EPSILON = 1e-06

def request_index(token_ids, length_row):
    request_ends = jnp.cumsum(length_row).astype(jnp.int32)
    starts = (request_ends - length_row).astype(jnp.int32)
    request = lax.optimization_barrier(jnp.sum((token_ids[:, None] >= request_ends[None, :]).astype(jnp.int32), axis=1)).astype(jnp.int32)
    onehot = request[:, None] == jnp.arange(length_row.shape[0], dtype=jnp.int32)[None, :]
    opening = lax.optimization_barrier(jnp.sum(jnp.where(onehot, starts[None, :], 0), axis=1)).astype(jnp.int32)
    return (request, (token_ids - opening).astype(jnp.int32))

def rope_rows(entries, positions):
    half_size = HD // 2
    indices = jnp.arange(half_size, dtype=jnp.float32)
    inv_freq = jnp.power(ROPE_BASE, -2.0 * indices / HD)
    angles = positions[:, None] * inv_freq[None, :]
    cosine = jnp.cos(angles)[:, None, :]
    sine_part = jnp.sin(angles)[:, None, :]
    per_head = entries.astype(jnp.float32).reshape(entries.shape[0], HEADS, HD)
    first_half = per_head[..., :half_size]
    second = per_head[..., half_size:]
    turned = jnp.concatenate([first_half * cosine - second * sine_part, second * cosine + first_half * sine_part], axis=-1)
    return turned.reshape(entries.shape[0], HEADS * HD).astype(jnp.bfloat16)

def attend(query_block, key_rows, value_rows, allowed):
    count_rows = query_block.shape[0]
    query_heads = query_block.astype(jnp.float32).reshape(count_rows, HEADS, HD)
    key_heads = key_rows.astype(jnp.float32).reshape(key_rows.shape[0], HEADS, HD)
    value_heads = value_rows.astype(jnp.float32).reshape(value_rows.shape[0], HEADS, HD)
    scores = jnp.einsum('qhd,khd->hqk', query_heads, key_heads) * HD ** (-0.5)
    scores = jnp.where(allowed[None], scores, -1e+30)
    highest = lax.optimization_barrier(jnp.max(scores, axis=2, keepdims=True))
    weights = jnp.where(allowed[None], jnp.exp(scores - highest), 0.0)
    totals = lax.optimization_barrier(jnp.sum(weights, axis=2, keepdims=True))
    probabilities = weights.astype(jnp.bfloat16).astype(jnp.float32)
    blended = jnp.einsum('hqk,khd->hqd', probabilities, value_heads) / totals
    return jnp.transpose(blended, (1, 0, 2)).reshape(count_rows, HEADS * HD).astype(jnp.bfloat16)

def expert_outputs(matrix_rows, gate_matrix, up_matrix, down_matrix):
    gate_part = jnp.dot(matrix_rows, gate_matrix, preferred_element_type=jnp.float32)
    up_part = jnp.dot(matrix_rows, up_matrix, preferred_element_type=jnp.float32)
    hidden = (jax.nn.silu(gate_part) * up_part).astype(jnp.bfloat16)
    return jnp.dot(hidden, down_matrix, preferred_element_type=jnp.float32).astype(jnp.bfloat16)

def reference(suffix_queries, suffix_keys, suffix_values, prefix_cache, residual, out_weight, norm_gain, routes, route_weights, lengths, migrate, expert_gate, expert_up, expert_down, shared_gate, shared_up, shared_down, shared_router):
    width_all = HEADS * HD
    span = HIST * TOK_DEV
    attention_groups = []
    cache_groups = []
    for group in range(GROUPS):
        length_row = lengths[group]
        token_ids = jnp.arange(TOKENS_G, dtype=jnp.int32)
        offset = request_index(token_ids, length_row)[1]
        positions = (PREFIX + offset).astype(jnp.float32)
        query_turned = rope_rows(suffix_queries[group], positions)
        key_turned = rope_rows(suffix_keys[group], positions)
        cache_groups.append(jnp.concatenate([key_turned, suffix_values[group]], axis=1))
        padded_keys = jnp.concatenate([jnp.zeros((span, width_all), jnp.bfloat16), key_turned], axis=0)
        padded_values = jnp.concatenate([jnp.zeros((span, width_all), jnp.bfloat16), suffix_values[group]], axis=0)
        prefix_keys = prefix_cache[group, :, :width_all]
        prefix_values = prefix_cache[group, :, width_all:]

        def one_block(block, length_row=length_row, query_turned=query_turned, padded_keys=padded_keys, padded_values=padded_values, prefix_keys=prefix_keys, prefix_values=prefix_values):
            first_row = (block * TOK_DEV).astype(jnp.int32)
            query_block = lax.dynamic_slice_in_dim(query_turned, first_row, TOK_DEV, 0)
            key_block = lax.dynamic_slice_in_dim(padded_keys, first_row, span + TOK_DEV, 0)
            value_block = lax.dynamic_slice_in_dim(padded_values, first_row, span + TOK_DEV, 0)
            query_ids = (first_row + jnp.arange(TOK_DEV, dtype=jnp.int32)).astype(jnp.int32)
            key_ids = (first_row - span + jnp.arange(span + TOK_DEV, dtype=jnp.int32)).astype(jnp.int32)
            query_request = request_index(query_ids, length_row)[0]
            key_request = request_index(jnp.maximum(key_ids, 0), length_row)[0]
            allowed = (key_ids[None, :] >= 0) & (key_request[None, :] == query_request[:, None]) & (key_ids[None, :] <= query_ids[:, None])
            allowed = jnp.concatenate([jnp.ones((TOK_DEV, PREFIX), jnp.bool_), allowed], axis=1)
            key_rows = jnp.concatenate([prefix_keys, key_block], axis=0)
            value_rows = jnp.concatenate([prefix_values, value_block], axis=0)
            return attend(query_block, key_rows, value_rows, allowed)
        outcome = lax.map(one_block, jnp.arange(TOKENS_G // TOK_DEV, dtype=jnp.int32))
        attention_groups.append(outcome.reshape(TOKENS_G, width_all))
    attention = jnp.concatenate(attention_groups, axis=0)
    state = residual.reshape(-1, D).astype(jnp.float32) + jnp.dot(attention, out_weight, preferred_element_type=jnp.float32)
    normed = (state * lax.rsqrt(lax.optimization_barrier(jnp.mean(state * state, axis=1, keepdims=True)) + EPSILON) * norm_gain).astype(jnp.bfloat16)
    quarter = SH // GROUPS
    shared_out = jnp.zeros(state.shape, jnp.float32)
    for block in range(GROUPS):
        gate_part = jnp.dot(normed, shared_gate[:, block * quarter:(block + 1) * quarter], preferred_element_type=jnp.float32)
        up_part = jnp.dot(normed, shared_up[:, block * quarter:(block + 1) * quarter], preferred_element_type=jnp.float32)
        hidden = (jax.nn.silu(gate_part) * up_part).astype(jnp.bfloat16)
        partial_sum = jnp.dot(hidden, shared_down[block * quarter:(block + 1) * quarter], preferred_element_type=jnp.float32).astype(jnp.bfloat16)
        partial_sum = lax.optimization_barrier(partial_sum)
        shared_out = shared_out + partial_sum.astype(jnp.float32)
    shared_scale = jax.nn.sigmoid(jnp.dot(normed, shared_router, preferred_element_type=jnp.float32))
    flat_routes = routes.reshape(-1)
    flat_weights = route_weights.reshape(-1)
    owner_rows = (jnp.arange(flat_routes.shape[0], dtype=jnp.int32) // TOP).astype(jnp.int32)
    slots_total = GROUPS * (TOKENS_G // TOK_DEV) * CAP

    def add_expert(carry, member):
        number, gate_matrix, up_matrix, down_matrix = member
        struck = flat_routes == number
        order = (jnp.cumsum(struck.astype(jnp.int32)) - 1).astype(jnp.int32)
        target = jnp.where(struck, order, slots_total).astype(jnp.int32)
        token_of = jnp.zeros((slots_total,), jnp.int32).at[target].set(owner_rows, mode='drop')
        weight_of = jnp.zeros((slots_total,), jnp.float32).at[target].set(flat_weights, mode='drop')
        outputs = expert_outputs(normed[token_of], gate_matrix, up_matrix, down_matrix)
        carry = carry.at[token_of].add(weight_of[:, None] * outputs.astype(jnp.float32))
        return (carry, None)
    routed = lax.scan(add_expert, jnp.zeros(state.shape, jnp.float32), (jnp.arange(EXPERTS, dtype=jnp.int32), expert_gate, expert_up, expert_down))[0]
    final = state + shared_scale[:, None] * shared_out + routed
    hidden_out = final.astype(jnp.bfloat16).reshape(GROUPS, TOKENS_G, D)
    moved_groups = []
    for group in range(GROUPS):
        pair_row = group // 4 * 2 + group % 2
        page_moved = jnp.repeat(migrate[pair_row], PG) == 1
        moved_groups.append(jnp.where(page_moved[:, None], cache_groups[group ^ 2], cache_groups[group]))
    suffix_cache = jnp.stack(moved_groups, axis=0)
    return (hidden_out, suffix_cache)
```

```python
import jax
import jax.numpy as jnp
from jax import lax
from jax.sharding import PartitionSpec as P

D = 2048
HD = 128
HEADS = 8
TOP = 4
PG = 16

ROPE_BASE = 1000000.0
EPSILON = 1e-06


def request_index(token_ids, length_row):
    request_ends = jnp.cumsum(length_row)
    starts = request_ends - length_row
    request = jnp.sum((token_ids[:, None] >= request_ends[None, :]).astype(jnp.int32), axis=1)
    onehot = request[:, None] == jnp.arange(length_row.shape[0], dtype=jnp.int32)[None, :]
    opening = jnp.sum(jnp.where(onehot, starts[None, :], 0), axis=1)
    return (request, token_ids - opening)


def rope_tables(positions):
    half_size = HD // 2
    indices = jnp.arange(half_size, dtype=jnp.float32)
    inv_freq = jnp.power(ROPE_BASE, -2.0 * indices / HD)
    angles = positions[:, None] * inv_freq[None, :]
    return jnp.cos(angles)[:, None, :], jnp.sin(angles)[:, None, :]


def rope_rows(entries, cosine, sine_part):
    half_size = HD // 2
    per_head = entries.astype(jnp.float32).reshape(entries.shape[0], HEADS, HD)
    first_half = per_head[..., :half_size]
    second = per_head[..., half_size:]
    turned = jnp.concatenate(
        [first_half * cosine - second * sine_part, second * cosine + first_half * sine_part],
        axis=-1,
    )
    return turned.reshape(entries.shape[0], HEADS * HD).astype(jnp.bfloat16)


def expert_outputs(matrix_rows, gate_matrix, up_matrix, down_matrix):
    gate_part = jnp.dot(matrix_rows, gate_matrix, preferred_element_type=jnp.float32)
    up_part = jnp.dot(matrix_rows, up_matrix, preferred_element_type=jnp.float32)
    hidden = (jax.nn.silu(gate_part) * up_part).astype(jnp.bfloat16)
    return jnp.dot(hidden, down_matrix, preferred_element_type=jnp.float32).astype(jnp.bfloat16)


def local(
    suffix_queries,
    suffix_keys,
    suffix_values,
    prefix_cache,
    residual,
    out_weight,
    norm_gain,
    routes,
    route_weights,
    lengths,
    migrate,
    expert_gate,
    expert_up,
    expert_down,
    shared_gate,
    shared_up,
    shared_down,
    shared_router,
):
    rows = suffix_queries.shape[1]
    nreq = lax.axis_size("req")
    ngrp = lax.axis_size("grp")
    me = lax.axis_index("req")
    grp = lax.axis_index("grp")
    prefix_len = prefix_cache.shape[1] * nreq
    width_all = HEADS * HD
    nblk = nreq // HEADS
    in_block = [[b * HEADS + j for j in range(HEADS)] for b in range(nblk)]
    same_head = [[b * HEADS + j for b in range(nblk)] for j in range(HEADS)]

    out_full = lax.all_gather(out_weight, "grp", axis=0, tiled=True)
    out_full = lax.all_gather(
        out_full, "req", axis=0, tiled=True,
        axis_index_groups=[[2 * i, 2 * i + 1] for i in range(nreq // 2)],
    )
    out_full = lax.all_gather(
        out_full, "req", axis=0, tiled=True,
        axis_index_groups=[[y * 16 + z * 2 + x for z in range(8)] for y in range(4) for x in range(2)],
    )
    out_full = lax.all_gather(
        out_full, "req", axis=0, tiled=True,
        axis_index_groups=[[y * 16 + k for y in range(4)] for k in range(16)],
    )

    prefix_rows = lax.all_gather(
        prefix_cache[0], "req", axis=0, tiled=True, axis_index_groups=same_head
    )

    token_ids = me * rows + jnp.arange(rows, dtype=jnp.int32)
    request, offset = request_index(token_ids, lengths[0])
    positions = (prefix_len + offset).astype(jnp.float32)
    cosine, sine_part = rope_tables(positions)
    query_turned = rope_rows(suffix_queries[0], cosine, sine_part)
    key_turned = rope_rows(suffix_keys[0], cosine, sine_part)
    own_cache = jnp.concatenate([key_turned, suffix_values[0]], axis=1)
    partner = lax.ppermute(own_cache, "grp", [(i, i ^ 2) for i in range(ngrp)])
    pair_row = grp // 4 * 2 + grp % 2
    page_flags = jnp.sum(
        jnp.where((jnp.arange(migrate.shape[0], dtype=jnp.int32) == pair_row)[:, None], migrate, 0),
        axis=0,
    )
    page_moved = jnp.repeat(page_flags, PG) == 1
    suffix_cache = jnp.where(page_moved[:, None], partner, own_cache)

    def by_head(a):
        return jnp.transpose(a.reshape(a.shape[0], HEADS, HD), (1, 0, 2))

    def exchange(a):
        return lax.all_to_all(
            a, "req", split_axis=0, concat_axis=0, tiled=True, axis_index_groups=in_block
        )

    pk = prefix_rows[:, :width_all]
    pv = prefix_rows[:, width_all:]
    pr = prefix_rows.shape[0]
    packed = jnp.concatenate(
        [by_head(query_turned), by_head(key_turned), by_head(suffix_values[0]), by_head(pk), by_head(pv)],
        axis=1,
    )
    got = exchange(packed)
    span = rows * HEADS
    q = got[:, :rows].reshape(span, HD)
    k_own = got[:, rows : 2 * rows]
    v_own = got[:, 2 * rows : 3 * rows]
    pk = got[:, 3 * rows : 3 * rows + pr].reshape(prefix_len, HD)
    pv = got[:, 3 * rows + pr :].reshape(prefix_len, HD)
    kv_own = got[:, rows : 3 * rows]
    kv_old = lax.ppermute(
        kv_own, "req", [(i - HEADS, i) for i in range(HEADS, nreq)]
    )
    k_all = jnp.concatenate([pk, kv_old[:, :rows].reshape(span, HD), k_own.reshape(span, HD)], axis=0)
    v_all = jnp.concatenate([pv, kv_old[:, rows:].reshape(span, HD), v_own.reshape(span, HD)], axis=0)

    base = me // HEADS * span
    q_ids = base + jnp.arange(span, dtype=jnp.int32)
    k_ids = base - span + jnp.arange(2 * span, dtype=jnp.int32)
    q_req = request_index(q_ids, lengths[0])[0]
    k_req = request_index(jnp.maximum(k_ids, 0), lengths[0])[0]
    allowed = (
        (k_ids[None, :] >= 0)
        & (k_req[None, :] == q_req[:, None])
        & (k_ids[None, :] <= q_ids[:, None])
    )
    allowed = jnp.concatenate([jnp.ones((span, prefix_len), jnp.bool_), allowed], axis=1)
    scores = jnp.einsum("qd,kd->qk", q, k_all, preferred_element_type=jnp.float32) * HD ** (-0.5)
    scores = jnp.where(allowed, scores, -1e30)
    highest = jnp.max(scores, axis=1, keepdims=True)
    weights = jnp.where(allowed, jnp.exp(scores - highest), 0.0)
    totals = jnp.sum(weights, axis=1, keepdims=True)
    blended = (
        jnp.dot(weights.astype(jnp.bfloat16), v_all, preferred_element_type=jnp.float32) / totals
    ).astype(jnp.bfloat16)
    back = exchange(blended.reshape(HEADS, rows, HD))
    attention = jnp.transpose(back, (1, 0, 2)).reshape(rows, width_all)

    state = residual[0].astype(jnp.float32) + jnp.dot(
        attention, out_full, preferred_element_type=jnp.float32
    )
    normed = (
        state * lax.rsqrt(jnp.mean(state * state, axis=1, keepdims=True) + EPSILON) * norm_gain
    ).astype(jnp.bfloat16)

    capacity = rows * TOP * 5 // (4 * nreq)
    slots = nreq * capacity
    flat_experts = routes[0].reshape(-1)
    onehot = (
        flat_experts[:, None] == jnp.arange(nreq, dtype=jnp.int32)[None, :]
    ).astype(jnp.int32)
    earlier = jnp.cumsum(onehot, axis=0) - onehot
    slot_index = jnp.sum(earlier * onehot, axis=1)
    place = (flat_experts * capacity + slot_index).reshape(rows, TOP)
    hit = place[:, :, None] == jnp.arange(slots, dtype=jnp.int32)[None, None, :]
    spread = jnp.any(hit, axis=1).astype(jnp.bfloat16)
    mix = jnp.sum(jnp.where(hit, route_weights[0][:, :, None], 0.0), axis=1)
    mix_hi = mix.astype(jnp.bfloat16)
    mix_lo = (mix - mix_hi.astype(jnp.float32)).astype(jnp.bfloat16)
    outgoing = lax.dot_general(
        spread, normed, (((0,), (0,)), ((), ())), preferred_element_type=jnp.float32
    ).astype(jnp.bfloat16).reshape(nreq, capacity, D)
    arrived = lax.all_to_all(outgoing, "req", split_axis=0, concat_axis=0, tiled=True)

    shard_rows = lax.all_gather(normed, "grp", axis=0, tiled=True)
    gate_part = jnp.dot(shard_rows, shared_gate, preferred_element_type=jnp.float32)
    up_part = jnp.dot(shard_rows, shared_up, preferred_element_type=jnp.float32)
    shared_hidden = (jax.nn.silu(gate_part) * up_part).astype(jnp.bfloat16)
    shared_out = lax.psum_scatter(
        jnp.dot(shared_hidden, shared_down, preferred_element_type=jnp.float32).astype(
            jnp.bfloat16
        ),
        "grp",
        scatter_dimension=0,
        tiled=True,
    ).astype(jnp.float32)
    shared_scale = jax.nn.sigmoid(
        jnp.dot(normed, shared_router, preferred_element_type=jnp.float32)
    )
    gate_all = lax.all_gather(expert_gate, "grp", axis=2, tiled=True)
    up_all = lax.all_gather(expert_up, "grp", axis=2, tiled=True)
    down_all = lax.all_gather(expert_down, "grp", axis=1, tiled=True)
    finished = expert_outputs(arrived.reshape(-1, D), gate_all[0], up_all[0], down_all[0])
    returned = lax.all_to_all(
        finished.reshape(nreq, capacity, D), "req", split_axis=0, concat_axis=0, tiled=True
    ).reshape(slots, D)
    routed = jnp.dot(mix_hi, returned, preferred_element_type=jnp.float32) + jnp.dot(
        mix_lo, returned, preferred_element_type=jnp.float32
    )
    final = state + shared_scale[:, None] * shared_out + routed
    return (final.astype(jnp.bfloat16)[None], suffix_cache[None])


def solution(mesh):
    placed = (
        P("grp", "req", None),
        P("grp", "req", None),
        P("grp", "req", None),
        P("grp", "req", None),
        P("grp", "req", None),
        P(("req", "grp"), None),
        P(),
        P("grp", "req", None),
        P("grp", "req", None),
        P("grp", None),
        P(None, "req"),
        P("req", None, "grp"),
        P("req", None, "grp"),
        P("req", "grp", None),
        P(None, "grp"),
        P(None, "grp"),
        P("grp", None),
        P(),
    )
    return jax.shard_map(
        local,
        mesh=mesh,
        in_specs=placed,
        out_specs=(P("grp", "req", None), P("grp", "req", None)),
        check_vma=False,
    )
```

```python
import jax
import jax.numpy as jnp
from jax import lax
from jax.experimental import pallas as pl
from jax.experimental.pallas import tpu as pltpu
from jax.sharding import PartitionSpec as P

D = 2048
HD = 128
HEADS = 8
TOP = 4
PG = 16

ROPE_BASE = 1000000.0
EPSILON = 1e-06


def request_index(token_ids, length_row):
    request_ends = jnp.cumsum(length_row)
    starts = request_ends - length_row
    request = jnp.sum((token_ids[:, None] >= request_ends[None, :]).astype(jnp.int32), axis=1)
    onehot = request[:, None] == jnp.arange(length_row.shape[0], dtype=jnp.int32)[None, :]
    opening = jnp.sum(jnp.where(onehot, starts[None, :], 0), axis=1)
    return (request, token_ids - opening)


def rope_tables(positions):
    half_size = HD // 2
    indices = jnp.arange(half_size, dtype=jnp.float32)
    inv_freq = jnp.power(ROPE_BASE, -2.0 * indices / HD)
    angles = positions[:, None] * inv_freq[None, :]
    return jnp.cos(angles)[:, None, :], jnp.sin(angles)[:, None, :]


def rope_rows(entries, cosine, sine_part):
    half_size = HD // 2
    per_head = entries.astype(jnp.float32).reshape(entries.shape[0], HEADS, HD)
    first_half = per_head[..., :half_size]
    second = per_head[..., half_size:]
    turned = jnp.concatenate(
        [first_half * cosine - second * sine_part, second * cosine + first_half * sine_part],
        axis=-1,
    )
    return turned.reshape(entries.shape[0], HEADS * HD).astype(jnp.bfloat16)


def expert_outputs(matrix_rows, gate_matrix, up_matrix, down_matrix):
    gate_part = jnp.dot(matrix_rows, gate_matrix, preferred_element_type=jnp.float32)
    up_part = jnp.dot(matrix_rows, up_matrix, preferred_element_type=jnp.float32)
    hidden = (jax.nn.silu(gate_part) * up_part).astype(jnp.bfloat16)
    return jnp.dot(hidden, down_matrix, preferred_element_type=jnp.float32).astype(jnp.bfloat16)


MESH = pl.DeviceIdType.MESH
QS, KS, VS, HK, HV, PB, PX, GS, XS, ZS, YS, CS, OS, NSEM = (
    0, 8, 16, 24, 32, 40, 48, 56, 60, 61, 69, 73, 74, 82)


def attention_kernel(
    q_ref, kv_ref, pp_ref, wpad_ref, resid_ref, gain_ref, len_ref,
    state_ref, normed_ref,
    qbuf, kvbuf, pbuf, pfx, obuf, osend, gbuf, wbuf, pk, pv,
    send_sem, recv_sem, local_sem,
):
    r = lax.axis_index("req")
    g = lax.axis_index("grp")
    b = r // HEADS
    j = r % HEADS
    c = g % 2
    xlo = r % 2
    z = (r // 2) % 8
    y = r // 16
    width = HEADS * HD
    rows = q_ref.shape[0]

    def flip(v, s):
        out = 0
        bit = 1
        while bit < 8:
            has = (v // bit) % 2
            out = out + bit * ((1 - has) if s & bit else has)
            bit *= 2
        return out

    def copy(src, dst, idx, req, grp):
        return pltpu.make_async_remote_copy(
            src_ref=src, dst_ref=dst, send_sem=send_sem.at[idx], recv_sem=recv_sem.at[idx],
            device_id=(req, grp), device_id_type=MESH)

    def lanes(h):
        return pl.ds(pl.multiple_of(h * HD, HD), HD)

    def vlanes(h):
        return pl.ds(pl.multiple_of(width + h * HD, HD), HD)

    up = (b + 1) % 8
    down = (b + 7) % 8

    barrier = pltpu.get_barrier_semaphore()
    peers = [(b * 8 + flip(j, s), g) for s in range(1, 8)]
    peers += [(up * 8 + s, g) for s in range(8)] + [(down * 8 + s, g) for s in range(8)]
    peers += [(flip(b, s) * 8 + j, g) for s in range(1, 8)]
    peers += [(r, flip(g, s)) for s in range(1, 4)]
    peers += [(y * 16 + flip(z, s) * 2 + xlo, g) for s in range(1, 8)]
    peers += [(flip(y, s) * 16 + z * 2 + xlo, g) for s in range(1, 4)]
    for peer in peers:
        pl.semaphore_signal(barrier, inc=1, device_id=peer, device_id_type=MESH)
    pl.semaphore_wait(barrier, len(peers))

    started = []

    def start(*a):
        d = copy(*a)
        d.start()
        started.append(d)

    for s in range(1, 4):
        og = flip(g, s)
        start(wpad_ref.at[og % 2], gbuf.at[g], GS + s, r, og)
    for s in range(1, 8):
        t = flip(j, s)
        start(pp_ref.at[t], pbuf.at[j], PB + s, b * 8 + t, g)
    for s in range(1, 8):
        t = flip(j, s)
        start(q_ref.at[:, lanes(t)], qbuf.at[j], QS + s, b * 8 + t, g)
        start(kv_ref.at[:, lanes(t)], kvbuf.at[8 + j, pl.ds(0, rows)], KS + s, b * 8 + t, g)
        start(kv_ref.at[:, vlanes(t)], kvbuf.at[8 + j, pl.ds(rows, rows)], VS + s, b * 8 + t, g)
    mine = [
        pltpu.make_async_copy(q_ref.at[:, lanes(j)], qbuf.at[j], local_sem.at[0]),
        pltpu.make_async_copy(kv_ref.at[:, lanes(j)], kvbuf.at[8 + j, pl.ds(0, rows)], local_sem.at[1]),
        pltpu.make_async_copy(kv_ref.at[:, vlanes(j)], kvbuf.at[8 + j, pl.ds(rows, rows)], local_sem.at[2]),
        pltpu.make_async_copy(pp_ref.at[j], pbuf.at[j], local_sem.at[3]),
        pltpu.make_async_copy(wpad_ref.at[c], gbuf.at[g], local_sem.at[4]),
    ]
    for d in mine:
        d.start()

    mine[4].wait()
    for s in range(1, 4):
        og = flip(g, s)
        copy(gbuf.at[og], gbuf.at[og], GS + s, r, og).wait_recv()
    w16 = (gbuf[0].astype(jnp.float32) + gbuf[1].astype(jnp.float32)) + (
        gbuf[2].astype(jnp.float32) + gbuf[3].astype(jnp.float32))
    my16 = pl.ds(pl.multiple_of(r * 16, 16), 16)
    wbuf[c, my16, :] = w16.astype(jnp.bfloat16)
    mine[3].wait()
    for s in range(1, 8):
        t = flip(j, s)
        copy(pp_ref.at[t], pbuf.at[t], PB + s, b * 8 + t, g).wait_recv()
    rx = flip(j, 1) + b * 8
    start(wbuf.at[c, my16], wbuf.at[c, my16], XS, rx, g)
    for s in range(1, 8):
        start(pbuf, pfx.at[b], PX + s, flip(b, s) * 8 + j, g)
    keep = pltpu.make_async_copy(pbuf, pfx.at[b], local_sem.at[5])
    keep.start()
    ox16 = pl.ds(pl.multiple_of(rx * 16, 16), 16)
    copy(wbuf.at[c, ox16], wbuf.at[c, ox16], XS, rx, g).wait_recv()
    my32 = pl.ds(pl.multiple_of((r // 2) * 32, 32), 32)
    for s in range(1, 8):
        start(wbuf.at[c, my32], wbuf.at[c, my32], ZS + s, y * 16 + flip(z, s) * 2 + xlo, g)
    for s in range(8):
        t = flip(j, s)
        start(kv_ref.at[:, lanes(t)], kvbuf.at[j, pl.ds(0, rows)], HK + s, up * 8 + t, g)
        start(kv_ref.at[:, vlanes(t)], kvbuf.at[j, pl.ds(rows, rows)], HV + s, up * 8 + t, g)
    for s in range(1, 8):
        oz = pl.ds(pl.multiple_of((y * 8 + flip(z, s)) * 32, 32), 32)
        copy(wbuf.at[c, oz], wbuf.at[c, oz], ZS + s, r, g).wait_recv()
    my256 = pl.ds(pl.multiple_of(y * 256, 256), 256)
    for s in range(1, 4):
        start(wbuf.at[c, my256], wbuf.at[c, my256], YS + s, flip(y, s) * 16 + z * 2 + xlo, g)

    keep.wait()
    for s in range(1, 8):
        ob = flip(b, s)
        copy(pbuf, pfx.at[ob], PX + s, r, g).wait_recv()
    pieces = pfx[...].reshape(8 * 8 * 16, HD)
    ii = lax.broadcasted_iota(jnp.int32, (256, 1024), 0)
    cc = lax.broadcasted_iota(jnp.int32, (256, 1024), 1)
    at = (ii // 4) * 16 + ii % 4
    pk[...] = jnp.dot((cc == at).astype(jnp.bfloat16), pieces, preferred_element_type=jnp.float32).astype(jnp.bfloat16)
    pv[...] = jnp.dot((cc == at + 4).astype(jnp.bfloat16), pieces, preferred_element_type=jnp.float32).astype(jnp.bfloat16)
    for d in mine[:3]:
        d.wait()
    for s in range(1, 8):
        t = flip(j, s)
        copy(qbuf.at[t], qbuf.at[t], QS + s, r, g).wait_recv()
        copy(kvbuf.at[8 + t, pl.ds(0, rows)], kvbuf.at[8 + t, pl.ds(0, rows)], KS + s, r, g).wait_recv()
        copy(kvbuf.at[8 + t, pl.ds(rows, rows)], kvbuf.at[8 + t, pl.ds(rows, rows)], VS + s, r, g).wait_recv()
    for s in range(8):
        t = flip(j, s)
        copy(kvbuf.at[t, pl.ds(0, rows)], kvbuf.at[t, pl.ds(0, rows)], HK + s, r, g).wait_recv()
        copy(kvbuf.at[t, pl.ds(rows, rows)], kvbuf.at[t, pl.ds(rows, rows)], HV + s, r, g).wait_recv()

    span = rows * HEADS
    nwin = span + rows

    def attend(t):
        q_id = b * span + t * rows + lax.broadcasted_iota(jnp.int32, (rows, 1), 0)
        opening = jnp.zeros((rows, 1), jnp.int32)
        end = 0
        for n in range(len_ref.shape[1]):
            end = end + len_ref[0, n]
            opening = jnp.where(q_id >= end, end, opening)
        first = b * span - span + t * rows
        k_id = first + lax.broadcasted_iota(jnp.int32, (rows, nwin), 1)
        q = qbuf[t]
        kw = kvbuf[pl.ds(t, 9), pl.ds(0, rows), :].reshape(nwin, HD)
        vw = kvbuf[pl.ds(t, 9), pl.ds(rows, rows), :].reshape(nwin, HD)
        dims = (((1,), (1,)), ((), ()))
        s1 = lax.dot_general(q, pk[...], dims, preferred_element_type=jnp.float32) * HD ** (-0.5)
        s2 = lax.dot_general(q, kw, dims, preferred_element_type=jnp.float32) * HD ** (-0.5)
        s2 = jnp.where((k_id >= opening) & (k_id <= q_id), s2, -1e30)
        top = jnp.maximum(jnp.max(s1, axis=1, keepdims=True), jnp.max(s2, axis=1, keepdims=True))
        w1 = jnp.exp(s1 - top)
        w2 = jnp.exp(s2 - top)
        total = jnp.sum(w1, axis=1, keepdims=True) + jnp.sum(w2, axis=1, keepdims=True)
        o = jnp.dot(w1.astype(jnp.bfloat16), pv[...], preferred_element_type=jnp.float32)
        o = o + jnp.dot(w2.astype(jnp.bfloat16), vw, preferred_element_type=jnp.float32)
        return (o / total).astype(jnp.bfloat16)

    for s in range(1, 8):
        if s == 4:
            for q in range(1, 4):
                oy = pl.ds(pl.multiple_of(flip(y, q) * 256, 256), 256)
                copy(wbuf.at[c, oy], wbuf.at[c, oy], YS + q, r, g).wait_recv()
            start(wbuf.at[c], wbuf.at[c], CS, r, flip(g, 1))
        t = flip(j, s)
        osend[t] = attend(t)
        start(osend.at[t], obuf.at[j], OS + s, b * 8 + t, g)
    obuf[j] = attend(j)
    for s in range(1, 8):
        t = flip(j, s)
        copy(obuf.at[t], obuf.at[t], OS + s, r, g).wait_recv()
    copy(wbuf.at[1 - c], wbuf.at[1 - c], CS, r, flip(g, 1)).wait_recv()

    attn = jnp.concatenate([obuf[h] for h in range(HEADS)], axis=1)
    wide = 256
    per = wbuf.shape[2] // wide
    total = jnp.zeros((rows, 1), jnp.float32)
    for n in range(2 * per):
        cols = pl.ds(n * wide, wide)
        part = jnp.dot(attn, wbuf[n // per, :, pl.ds((n % per) * wide, wide)], preferred_element_type=jnp.float32)
        part = resid_ref[:, cols].astype(jnp.float32) + part
        state_ref[:, cols] = part
        total = total + jnp.sum(part * part, axis=1, keepdims=True)
    inv = lax.rsqrt(total / D + EPSILON)
    for n in range(2 * per):
        cols = pl.ds(n * wide, wide)
        normed_ref[:, cols] = (state_ref[:, cols] * inv * gain_ref[:, cols]).astype(jnp.bfloat16)
    for d in started:
        d.wait_send()


def attention_block(q, kv, pp, wpad, resid, gain, lengths):
    rows = q.shape[0]
    vm = pl.BlockSpec(memory_space=pltpu.VMEM)
    bf = jnp.bfloat16
    return pl.pallas_call(
        attention_kernel,
        out_shape=(
            jax.ShapeDtypeStruct((rows, D), jnp.float32),
            jax.ShapeDtypeStruct((rows, D), bf),
        ),
        in_specs=[vm] * 6 + [pl.BlockSpec(memory_space=pltpu.SMEM)],
        out_specs=(vm, vm),
        scratch_shapes=[
            pltpu.VMEM((8, rows, HD), bf),
            pltpu.VMEM((16, 2 * rows, HD), bf),
            pltpu.VMEM((8, 16, HD), bf),
            pltpu.VMEM((8, 8, 16, HD), bf),
            pltpu.VMEM((8, rows, HD), bf),
            pltpu.VMEM((8, rows, HD), bf),
            pltpu.VMEM((4, 16, D // 2), bf),
            pltpu.VMEM((2, HEADS * HD, D // 2), bf),
            pltpu.VMEM((256, HD), bf),
            pltpu.VMEM((256, HD), bf),
            pltpu.SemaphoreType.DMA((NSEM,)),
            pltpu.SemaphoreType.DMA((NSEM,)),
            pltpu.SemaphoreType.DMA((8,)),
        ],
        compiler_params=pltpu.CompilerParams(
            collective_id=0, has_side_effects=True, vmem_limit_bytes=40 << 20
        ),
        cost_estimate=pl.CostEstimate(flops=2_000_000_000, bytes_accessed=150_000_000, transcendentals=1_500_000),
        name="attention_block",
    )(q, kv, pp, wpad, resid, gain, lengths)


def local(
    suffix_queries,
    suffix_keys,
    suffix_values,
    prefix_cache,
    residual,
    out_weight,
    norm_gain,
    routes,
    route_weights,
    lengths,
    migrate,
    expert_gate,
    expert_up,
    expert_down,
    shared_gate,
    shared_up,
    shared_down,
    shared_router,
):
    rows = suffix_queries.shape[1]
    nreq = lax.axis_size("req")
    ngrp = lax.axis_size("grp")
    me = lax.axis_index("req")
    grp = lax.axis_index("grp")
    prefix_len = prefix_cache.shape[1] * nreq
    width_all = HEADS * HD

    token_ids = me * rows + jnp.arange(rows, dtype=jnp.int32)
    request, offset = request_index(token_ids, lengths[0])
    positions = (prefix_len + offset).astype(jnp.float32)
    cosine, sine_part = rope_tables(positions)
    query_turned = rope_rows(suffix_queries[0], cosine, sine_part)
    key_turned = rope_rows(suffix_keys[0], cosine, sine_part)
    own_cache = jnp.concatenate([key_turned, suffix_values[0]], axis=1)
    partner = lax.ppermute(own_cache, "grp", [(i, i ^ 2) for i in range(ngrp)])
    pair_row = grp // 4 * 2 + grp % 2
    page_flags = jnp.sum(
        jnp.where((jnp.arange(migrate.shape[0], dtype=jnp.int32) == pair_row)[:, None], migrate, 0),
        axis=0,
    )
    page_moved = jnp.repeat(page_flags, PG) == 1
    suffix_cache = jnp.where(page_moved[:, None], partner, own_cache)

    few = prefix_cache.shape[1]
    pp = jnp.transpose(prefix_cache[0].reshape(few, 2, HEADS, HD), (2, 1, 0, 3)).reshape(HEADS, 2 * few, HD)
    pp = jnp.pad(pp, ((0, 0), (0, 16 - 2 * few), (0, 0)))
    held = out_weight.shape[0]
    spot = jnp.arange(ngrp, dtype=jnp.int32)[:, None, None] == grp
    wpad = jnp.where(spot, out_weight[None], jnp.zeros((), jnp.bfloat16)).reshape(ngrp * held, D)
    wpad = jnp.transpose(wpad.reshape(ngrp * held, 2, D // 2), (1, 0, 2))
    state, normed = attention_block(
        query_turned, own_cache, pp, wpad, residual[0], norm_gain[None], lengths
    )

    capacity = rows * TOP * 5 // (4 * nreq)
    slots = nreq * capacity
    flat_experts = routes[0].reshape(-1)
    onehot = (
        flat_experts[:, None] == jnp.arange(nreq, dtype=jnp.int32)[None, :]
    ).astype(jnp.int32)
    earlier = jnp.cumsum(onehot, axis=0) - onehot
    slot_index = jnp.sum(earlier * onehot, axis=1)
    place = (flat_experts * capacity + slot_index).reshape(rows, TOP)
    hit = place[:, :, None] == jnp.arange(slots, dtype=jnp.int32)[None, None, :]
    spread = jnp.any(hit, axis=1).astype(jnp.bfloat16)
    mix = jnp.sum(jnp.where(hit, route_weights[0][:, :, None], 0.0), axis=1)
    mix_hi = mix.astype(jnp.bfloat16)
    mix_lo = (mix - mix_hi.astype(jnp.float32)).astype(jnp.bfloat16)
    outgoing = lax.dot_general(
        spread, normed, (((0,), (0,)), ((), ())), preferred_element_type=jnp.float32
    ).astype(jnp.bfloat16).reshape(nreq, capacity, D)
    arrived = lax.all_to_all(outgoing, "req", split_axis=0, concat_axis=0, tiled=True)

    shard_rows = lax.all_gather(normed, "grp", axis=0, tiled=True)
    gate_part = jnp.dot(shard_rows, shared_gate, preferred_element_type=jnp.float32)
    up_part = jnp.dot(shard_rows, shared_up, preferred_element_type=jnp.float32)
    shared_hidden = (jax.nn.silu(gate_part) * up_part).astype(jnp.bfloat16)
    shared_out = lax.psum_scatter(
        jnp.dot(shared_hidden, shared_down, preferred_element_type=jnp.float32).astype(
            jnp.bfloat16
        ),
        "grp",
        scatter_dimension=0,
        tiled=True,
    ).astype(jnp.float32)
    shared_scale = jax.nn.sigmoid(
        jnp.dot(normed, shared_router, preferred_element_type=jnp.float32)
    )
    gate_all = lax.all_gather(expert_gate, "grp", axis=2, tiled=True)
    up_all = lax.all_gather(expert_up, "grp", axis=2, tiled=True)
    down_all = lax.all_gather(expert_down, "grp", axis=1, tiled=True)
    finished = expert_outputs(arrived.reshape(-1, D), gate_all[0], up_all[0], down_all[0])
    returned = lax.all_to_all(
        finished.reshape(nreq, capacity, D), "req", split_axis=0, concat_axis=0, tiled=True
    ).reshape(slots, D)
    routed = jnp.dot(mix_hi, returned, preferred_element_type=jnp.float32) + jnp.dot(
        mix_lo, returned, preferred_element_type=jnp.float32
    )
    final = state + shared_scale[:, None] * shared_out + routed
    return (final.astype(jnp.bfloat16)[None], suffix_cache[None])


def solution(mesh):
    placed = (
        P("grp", "req", None),
        P("grp", "req", None),
        P("grp", "req", None),
        P("grp", "req", None),
        P("grp", "req", None),
        P(("req", "grp"), None),
        P(),
        P("grp", "req", None),
        P("grp", "req", None),
        P("grp", None),
        P(None, "req"),
        P("req", None, "grp"),
        P("req", None, "grp"),
        P("req", "grp", None),
        P(None, "grp"),
        P(None, "grp"),
        P("grp", None),
        P(),
    )
    return jax.shard_map(
        local,
        mesh=mesh,
        in_specs=placed,
        out_specs=(P("grp", "req", None), P("grp", "req", None)),
        check_vma=False,
    )
```

```python
import jax
import jax.numpy as jnp
from jax import lax
from jax.experimental import pallas as pl
from jax.experimental.pallas import tpu as pltpu
from jax.sharding import PartitionSpec as P

D = 2048
HD = 128
HEADS = 8
TOP = 4
PG = 16

ROPE_BASE = 1000000.0
EPSILON = 1e-06


def request_index(token_ids, length_row):
    request_ends = jnp.cumsum(length_row)
    starts = request_ends - length_row
    request = jnp.sum((token_ids[:, None] >= request_ends[None, :]).astype(jnp.int32), axis=1)
    onehot = request[:, None] == jnp.arange(length_row.shape[0], dtype=jnp.int32)[None, :]
    opening = jnp.sum(jnp.where(onehot, starts[None, :], 0), axis=1)
    return (request, token_ids - opening)


def rope_tables(positions):
    half_size = HD // 2
    indices = jnp.arange(half_size, dtype=jnp.float32)
    inv_freq = jnp.power(ROPE_BASE, -2.0 * indices / HD)
    angles = positions[:, None] * inv_freq[None, :]
    return jnp.cos(angles)[:, None, :], jnp.sin(angles)[:, None, :]


def rope_rows(entries, cosine, sine_part):
    half_size = HD // 2
    per_head = entries.astype(jnp.float32).reshape(entries.shape[0], HEADS, HD)
    first_half = per_head[..., :half_size]
    second = per_head[..., half_size:]
    turned = jnp.concatenate(
        [first_half * cosine - second * sine_part, second * cosine + first_half * sine_part],
        axis=-1,
    )
    return turned.reshape(entries.shape[0], HEADS * HD).astype(jnp.bfloat16)


MESH = pl.DeviceIdType.MESH
QS, KS, VS, HK, HV, PB, PX, GS, XS, ZS, YS, CS, OS, NSEM = (
    0, 8, 16, 24, 32, 40, 48, 56, 60, 61, 69, 73, 74, 82)


def attention_kernel(
    q_ref, kv_ref, pp_ref, wpad_ref, resid_ref, gain_ref, len_ref,
    state_ref, normed_ref,
    qbuf, kvbuf, pbuf, pfx, obuf, osend, gbuf, wbuf, pk, pv,
    send_sem, recv_sem, local_sem,
):
    r = lax.axis_index("req")
    g = lax.axis_index("grp")
    b = r // HEADS
    j = r % HEADS
    c = g % 2
    xlo = r % 2
    z = (r // 2) % 8
    y = r // 16
    width = HEADS * HD
    rows = q_ref.shape[0]

    def flip(v, s):
        out = 0
        bit = 1
        while bit < 8:
            has = (v // bit) % 2
            out = out + bit * ((1 - has) if s & bit else has)
            bit *= 2
        return out

    def copy(src, dst, idx, req, grp):
        return pltpu.make_async_remote_copy(
            src_ref=src, dst_ref=dst, send_sem=send_sem.at[idx], recv_sem=recv_sem.at[idx],
            device_id=(req, grp), device_id_type=MESH)

    def lanes(h):
        return pl.ds(pl.multiple_of(h * HD, HD), HD)

    def vlanes(h):
        return pl.ds(pl.multiple_of(width + h * HD, HD), HD)

    up = (b + 1) % 8
    down = (b + 7) % 8

    barrier = pltpu.get_barrier_semaphore()
    peers = [(b * 8 + flip(j, s), g) for s in range(1, 8)]
    peers += [(up * 8 + s, g) for s in range(8)] + [(down * 8 + s, g) for s in range(8)]
    peers += [(flip(b, s) * 8 + j, g) for s in range(1, 8)]
    peers += [(r, flip(g, s)) for s in range(1, 4)]
    peers += [(y * 16 + flip(z, s) * 2 + xlo, g) for s in range(1, 8)]
    peers += [(flip(y, s) * 16 + z * 2 + xlo, g) for s in range(1, 4)]
    for peer in peers:
        pl.semaphore_signal(barrier, inc=1, device_id=peer, device_id_type=MESH)
    pl.semaphore_wait(barrier, len(peers))

    started = []

    def start(*a):
        d = copy(*a)
        d.start()
        started.append(d)

    for s in range(1, 4):
        og = flip(g, s)
        start(wpad_ref.at[og % 2], gbuf.at[g], GS + s, r, og)
    for s in range(1, 8):
        t = flip(j, s)
        start(pp_ref.at[t], pbuf.at[j], PB + s, b * 8 + t, g)
    for s in range(1, 8):
        t = flip(j, s)
        start(q_ref.at[:, lanes(t)], qbuf.at[j], QS + s, b * 8 + t, g)
        start(kv_ref.at[:, lanes(t)], kvbuf.at[8 + j, pl.ds(0, rows)], KS + s, b * 8 + t, g)
        start(kv_ref.at[:, vlanes(t)], kvbuf.at[8 + j, pl.ds(rows, rows)], VS + s, b * 8 + t, g)
    mine = [
        pltpu.make_async_copy(q_ref.at[:, lanes(j)], qbuf.at[j], local_sem.at[0]),
        pltpu.make_async_copy(kv_ref.at[:, lanes(j)], kvbuf.at[8 + j, pl.ds(0, rows)], local_sem.at[1]),
        pltpu.make_async_copy(kv_ref.at[:, vlanes(j)], kvbuf.at[8 + j, pl.ds(rows, rows)], local_sem.at[2]),
        pltpu.make_async_copy(pp_ref.at[j], pbuf.at[j], local_sem.at[3]),
        pltpu.make_async_copy(wpad_ref.at[c], gbuf.at[g], local_sem.at[4]),
    ]
    for d in mine:
        d.start()

    mine[4].wait()
    for s in range(1, 4):
        og = flip(g, s)
        copy(gbuf.at[og], gbuf.at[og], GS + s, r, og).wait_recv()
    w16 = (gbuf[0].astype(jnp.float32) + gbuf[1].astype(jnp.float32)) + (
        gbuf[2].astype(jnp.float32) + gbuf[3].astype(jnp.float32))
    my16 = pl.ds(pl.multiple_of(r * 16, 16), 16)
    wbuf[c, my16, :] = w16.astype(jnp.bfloat16)
    mine[3].wait()
    for s in range(1, 8):
        t = flip(j, s)
        copy(pp_ref.at[t], pbuf.at[t], PB + s, b * 8 + t, g).wait_recv()
    rx = flip(j, 1) + b * 8
    start(wbuf.at[c, my16], wbuf.at[c, my16], XS, rx, g)
    for s in range(1, 8):
        start(pbuf, pfx.at[b], PX + s, flip(b, s) * 8 + j, g)
    keep = pltpu.make_async_copy(pbuf, pfx.at[b], local_sem.at[5])
    keep.start()
    ox16 = pl.ds(pl.multiple_of(rx * 16, 16), 16)
    copy(wbuf.at[c, ox16], wbuf.at[c, ox16], XS, rx, g).wait_recv()
    my32 = pl.ds(pl.multiple_of((r // 2) * 32, 32), 32)
    for s in range(1, 8):
        start(wbuf.at[c, my32], wbuf.at[c, my32], ZS + s, y * 16 + flip(z, s) * 2 + xlo, g)
    for s in range(8):
        t = flip(j, s)
        start(kv_ref.at[:, lanes(t)], kvbuf.at[j, pl.ds(0, rows)], HK + s, up * 8 + t, g)
        start(kv_ref.at[:, vlanes(t)], kvbuf.at[j, pl.ds(rows, rows)], HV + s, up * 8 + t, g)
    for s in range(1, 8):
        oz = pl.ds(pl.multiple_of((y * 8 + flip(z, s)) * 32, 32), 32)
        copy(wbuf.at[c, oz], wbuf.at[c, oz], ZS + s, r, g).wait_recv()
    my256 = pl.ds(pl.multiple_of(y * 256, 256), 256)
    for s in range(1, 4):
        start(wbuf.at[c, my256], wbuf.at[c, my256], YS + s, flip(y, s) * 16 + z * 2 + xlo, g)

    keep.wait()
    for s in range(1, 8):
        ob = flip(b, s)
        copy(pbuf, pfx.at[ob], PX + s, r, g).wait_recv()
    pieces = pfx[...].reshape(8 * 8 * 16, HD)
    ii = lax.broadcasted_iota(jnp.int32, (256, 1024), 0)
    cc = lax.broadcasted_iota(jnp.int32, (256, 1024), 1)
    at = (ii // 4) * 16 + ii % 4
    pk[...] = jnp.dot((cc == at).astype(jnp.bfloat16), pieces, preferred_element_type=jnp.float32).astype(jnp.bfloat16)
    pv[...] = jnp.dot((cc == at + 4).astype(jnp.bfloat16), pieces, preferred_element_type=jnp.float32).astype(jnp.bfloat16)
    for d in mine[:3]:
        d.wait()
    for s in range(1, 8):
        t = flip(j, s)
        copy(qbuf.at[t], qbuf.at[t], QS + s, r, g).wait_recv()
        copy(kvbuf.at[8 + t, pl.ds(0, rows)], kvbuf.at[8 + t, pl.ds(0, rows)], KS + s, r, g).wait_recv()
        copy(kvbuf.at[8 + t, pl.ds(rows, rows)], kvbuf.at[8 + t, pl.ds(rows, rows)], VS + s, r, g).wait_recv()
    for s in range(8):
        t = flip(j, s)
        copy(kvbuf.at[t, pl.ds(0, rows)], kvbuf.at[t, pl.ds(0, rows)], HK + s, r, g).wait_recv()
        copy(kvbuf.at[t, pl.ds(rows, rows)], kvbuf.at[t, pl.ds(rows, rows)], HV + s, r, g).wait_recv()

    span = rows * HEADS
    nwin = span + rows

    def attend(t):
        q_id = b * span + t * rows + lax.broadcasted_iota(jnp.int32, (rows, 1), 0)
        opening = jnp.zeros((rows, 1), jnp.int32)
        end = 0
        for n in range(len_ref.shape[1]):
            end = end + len_ref[0, n]
            opening = jnp.where(q_id >= end, end, opening)
        first = b * span - span + t * rows
        k_id = first + lax.broadcasted_iota(jnp.int32, (rows, nwin), 1)
        q = qbuf[t]
        kw = kvbuf[pl.ds(t, 9), pl.ds(0, rows), :].reshape(nwin, HD)
        vw = kvbuf[pl.ds(t, 9), pl.ds(rows, rows), :].reshape(nwin, HD)
        dims = (((1,), (1,)), ((), ()))
        s1 = lax.dot_general(q, pk[...], dims, preferred_element_type=jnp.float32) * HD ** (-0.5)
        s2 = lax.dot_general(q, kw, dims, preferred_element_type=jnp.float32) * HD ** (-0.5)
        s2 = jnp.where((k_id >= opening) & (k_id <= q_id), s2, -1e30)
        top = jnp.maximum(jnp.max(s1, axis=1, keepdims=True), jnp.max(s2, axis=1, keepdims=True))
        w1 = jnp.exp(s1 - top)
        w2 = jnp.exp(s2 - top)
        total = jnp.sum(w1, axis=1, keepdims=True) + jnp.sum(w2, axis=1, keepdims=True)
        o = jnp.dot(w1.astype(jnp.bfloat16), pv[...], preferred_element_type=jnp.float32)
        o = o + jnp.dot(w2.astype(jnp.bfloat16), vw, preferred_element_type=jnp.float32)
        return (o / total).astype(jnp.bfloat16)

    for s in range(1, 8):
        if s == 4:
            for q in range(1, 4):
                oy = pl.ds(pl.multiple_of(flip(y, q) * 256, 256), 256)
                copy(wbuf.at[c, oy], wbuf.at[c, oy], YS + q, r, g).wait_recv()
            start(wbuf.at[c], wbuf.at[c], CS, r, flip(g, 1))
        t = flip(j, s)
        osend[t] = attend(t)
        start(osend.at[t], obuf.at[j], OS + s, b * 8 + t, g)
    obuf[j] = attend(j)
    for s in range(1, 8):
        t = flip(j, s)
        copy(obuf.at[t], obuf.at[t], OS + s, r, g).wait_recv()
    copy(wbuf.at[1 - c], wbuf.at[1 - c], CS, r, flip(g, 1)).wait_recv()

    attn = jnp.concatenate([obuf[h] for h in range(HEADS)], axis=1)
    wide = 256
    per = wbuf.shape[2] // wide
    total = jnp.zeros((rows, 1), jnp.float32)
    for n in range(2 * per):
        cols = pl.ds(n * wide, wide)
        part = jnp.dot(attn, wbuf[n // per, :, pl.ds((n % per) * wide, wide)], preferred_element_type=jnp.float32)
        part = resid_ref[:, cols].astype(jnp.float32) + part
        state_ref[:, cols] = part
        total = total + jnp.sum(part * part, axis=1, keepdims=True)
    inv = lax.rsqrt(total / D + EPSILON)
    for n in range(2 * per):
        cols = pl.ds(n * wide, wide)
        normed_ref[:, cols] = (state_ref[:, cols] * inv * gain_ref[:, cols]).astype(jnp.bfloat16)
    for d in started:
        d.wait_send()


def attention_block(q, kv, pp, wpad, resid, gain, lengths):
    rows = q.shape[0]
    vm = pl.BlockSpec(memory_space=pltpu.VMEM)
    bf = jnp.bfloat16
    return pl.pallas_call(
        attention_kernel,
        out_shape=(
            jax.ShapeDtypeStruct((rows, D), jnp.float32),
            jax.ShapeDtypeStruct((rows, D), bf),
        ),
        in_specs=[vm] * 6 + [pl.BlockSpec(memory_space=pltpu.SMEM)],
        out_specs=(vm, vm),
        scratch_shapes=[
            pltpu.VMEM((8, rows, HD), bf),
            pltpu.VMEM((16, 2 * rows, HD), bf),
            pltpu.VMEM((8, 16, HD), bf),
            pltpu.VMEM((8, 8, 16, HD), bf),
            pltpu.VMEM((8, rows, HD), bf),
            pltpu.VMEM((8, rows, HD), bf),
            pltpu.VMEM((4, 16, D // 2), bf),
            pltpu.VMEM((2, HEADS * HD, D // 2), bf),
            pltpu.VMEM((256, HD), bf),
            pltpu.VMEM((256, HD), bf),
            pltpu.SemaphoreType.DMA((NSEM,)),
            pltpu.SemaphoreType.DMA((NSEM,)),
            pltpu.SemaphoreType.DMA((8,)),
        ],
        compiler_params=pltpu.CompilerParams(
            collective_id=0, has_side_effects=True, vmem_limit_bytes=40 << 20
        ),
        cost_estimate=pl.CostEstimate(flops=2_000_000_000, bytes_accessed=150_000_000, transcendentals=1_500_000),
        name="attention_block",
    )(q, kv, pp, wpad, resid, gain, lengths)


MAIN = 8
MORE = 2
NREQ = 64
PLANE = 16 * (MAIN + MORE)


def moe_kernel(
    normed_ref, state_ref, routes_ref, rcols_ref, rw_ref, router_ref,
    egate_ref, eup_ref, edown_ref, sgate_ref, sup_ref, sdown_ref,
    out_ref,
    hit_t, mix_hi, mix_lo, outb, outc, arrb, arrc, finb, finc, retb, retc, shard, part, parts, acc,
    wg, wu, wd, sg, su, sd,
    send_sem, recv_sem, grp_send, grp_recv, local_sem,
):
    r = lax.axis_index("req")
    g = lax.axis_index("grp")
    y = r // 16
    low = r % 16
    rows = normed_ref.shape[0]
    bf = jnp.bfloat16
    f32 = jnp.float32

    def slot_maps(shape, axis, p):
        i = lax.broadcasted_iota(jnp.int32, shape, axis)
        first = i < 16 * MAIN
        rest = i - 16 * MAIN
        return (p * 16 + jnp.where(first, i // MAIN, rest // MORE),
                jnp.where(first, i % MAIN, MAIN + rest % MORE))

    def xor(a, b, bits):
        out = 0
        bit = 1
        for _ in range(bits):
            out = out + bit * (((a // bit) % 2 + (b // bit) % 2) % 2)
            bit *= 2
        return out

    loads = [
        pltpu.make_async_copy(src, dst, local_sem.at[n])
        for n, (src, dst) in enumerate(
            [(egate_ref, wg), (eup_ref, wu), (edown_ref, wd), (sgate_ref, sg), (sup_ref, su), (sdown_ref, sd)]
        )
    ]
    for d in loads:
        d.start()
    barrier = pltpu.get_barrier_semaphore()

    def greet(s, _):
        peer = xor(y, s // 16, 2) * 16 + xor(low, s % 16, 4)
        pl.semaphore_signal(barrier, inc=1, device_id=(peer, g), device_id_type=MESH)
        return 0

    lax.fori_loop(1, NREQ, greet, 0)
    for s in range(1, 4):
        pl.semaphore_signal(barrier, inc=1, device_id=(r, xor(g, s, 2)), device_id_type=MESH)

    ei = lax.broadcasted_iota(jnp.int32, (NREQ, rows), 0)
    named_t = jnp.zeros((NREQ, rows), f32)
    for k in range(TOP):
        named_t = named_t + (rcols_ref[k : k + 1, :] == ei).astype(f32)
    ti = lax.broadcasted_iota(jnp.int32, (rows, rows), 0)
    tj = lax.broadcasted_iota(jnp.int32, (rows, rows), 1)
    slot_t = jnp.dot(named_t.astype(bf), (ti < tj).astype(bf), preferred_element_type=f32)
    for p in range(4):
        expert_of = slot_maps((PLANE, NREQ), 0, p)[0]
        widen_t = (expert_of == lax.broadcasted_iota(jnp.int32, (PLANE, NREQ), 1)).astype(bf)
        mine = jnp.dot(widen_t, named_t.astype(bf), preferred_element_type=f32)
        spot = jnp.dot(widen_t, slot_t.astype(bf), preferred_element_type=f32)
        want = slot_maps((PLANE, rows), 0, p)[1].astype(f32)
        hit_t[p] = jnp.where(spot == want, mine, 0.0).astype(bf)

    pl.semaphore_wait(barrier, NREQ - 1 + 3)

    def rcopy(src, dst, idx, req):
        return pltpu.make_async_remote_copy(
            src_ref=src, dst_ref=dst, send_sem=send_sem.at[idx], recv_sem=recv_sem.at[idx],
            device_id=(req, g), device_id_type=MESH)

    def gcopy(src, dst, idx, grp):
        return pltpu.make_async_remote_copy(
            src_ref=src, dst_ref=dst, send_sem=grp_send.at[idx], recv_sem=grp_recv.at[idx],
            device_id=(r, grp), device_id_type=MESH)

    def pair(b8, b2, i, to8, to2, o, idx, req):
        return (rcopy(b8.at[i], to8.at[o], idx, req), rcopy(b2.at[i], to2.at[o], idx + NREQ, req))

    def halves(v):
        cut = 16 * MAIN
        return v[:cut].reshape(16, MAIN, v.shape[1]), v[cut:].reshape(16, MORE, v.shape[1])

    def dispatch(k, _):
        plane = xor(y, k, 2)
        put = hit_t[plane]
        for n in range(4):
            cols = pl.ds(n * 512, 512)
            block = jnp.dot(put, normed_ref[:, cols], preferred_element_type=f32).astype(bf)
            outb[pl.ds(plane * 16, 16), :, cols], outc[pl.ds(plane * 16, 16), :, cols] = halves(block)

        def one(m, _):
            e = plane * 16 + xor(low, m, 4)
            for d in pair(outb, outc, e, arrb, arrc, r, k * 16 + m, e):
                d.start()
            return 0

        lax.fori_loop(jnp.where(k == 0, 1, 0), 16, one, 0)
        return 0

    dispatch(0, 0)
    own = [
        pltpu.make_async_copy(outb.at[r], arrb.at[r], local_sem.at[6]),
        pltpu.make_async_copy(outc.at[r], arrc.at[r], local_sem.at[10]),
    ]
    for d in own:
        d.start()
    for s in range(1, 4):
        gcopy(normed_ref, shard.at[g], s, xor(g, s, 2)).start()
    keep = pltpu.make_async_copy(normed_ref, shard.at[g], local_sem.at[7])
    keep.start()
    lax.fori_loop(1, 4, dispatch, 0)

    ej = lax.broadcasted_iota(jnp.int32, (rows, NREQ), 1)
    named = jnp.zeros((rows, NREQ), f32)
    heft = jnp.zeros((rows, NREQ), f32)
    for k in range(TOP):
        same = routes_ref[:, k : k + 1] == ej
        named = named + same.astype(f32)
        heft = heft + jnp.where(same, rw_ref[:, k : k + 1], 0.0)
    slot = jnp.dot((tj < ti).astype(bf), named.astype(bf), preferred_element_type=f32)
    heft_hi = heft.astype(bf)
    heft_lo = (heft - heft_hi.astype(f32)).astype(bf)
    for p in range(4):
        expert_of = slot_maps((NREQ, PLANE), 1, p)[0]
        widen = (expert_of == lax.broadcasted_iota(jnp.int32, (NREQ, PLANE), 0)).astype(bf)
        spot = jnp.dot(slot.astype(bf), widen, preferred_element_type=f32)
        hit = spot == slot_maps((rows, PLANE), 1, p)[1].astype(f32)
        mix_hi[p] = jnp.where(hit, jnp.dot(heft_hi, widen, preferred_element_type=f32), 0.0).astype(bf)
        mix_lo[p] = jnp.where(hit, jnp.dot(heft_lo, widen, preferred_element_type=f32), 0.0).astype(bf)
    scale = jax.nn.sigmoid(
        jnp.sum(normed_ref[...].astype(f32) * router_ref[...].astype(f32), axis=1, keepdims=True)
    )
    for d in loads[:3]:
        d.wait()
    for d in own:
        d.wait()
    nt = (((1,), (1,)), ((), ()))

    def expert(k, _):
        plane = xor(y, k, 2)

        def got(m, _):
            e = plane * 16 + xor(low, m, 4)
            for d in pair(arrb, arrc, e, arrb, arrc, e, k * 16 + m, e):
                d.wait_recv()
            return 0

        lax.fori_loop(jnp.where(k == 0, 1, 0), 16, got, 0)
        x = jnp.concatenate(
            [arrb[pl.ds(plane * 16, 16)].reshape(16 * MAIN, D), arrc[pl.ds(plane * 16, 16)].reshape(16 * MORE, D)],
            axis=0,
        )
        gate = lax.dot_general(x, wg[...], nt, preferred_element_type=f32)
        up = lax.dot_general(x, wu[...], nt, preferred_element_type=f32)
        hidden = (jax.nn.silu(gate) * up).astype(bf)
        for n in range(4):
            cols = pl.ds(n * 512, 512)
            o = jnp.dot(hidden, wd[:, cols], preferred_element_type=f32).astype(bf)
            finb[pl.ds(plane * 16, 16), :, cols], finc[pl.ds(plane * 16, 16), :, cols] = halves(o)

        def back(m, _):
            e = plane * 16 + xor(low, m, 4)
            for d in pair(finb, finc, e, retb, retc, r, 128 + k * 16 + m, e):
                d.start()
            return 0

        lax.fori_loop(jnp.where(k == 0, 1, 0), 16, back, 0)
        return 0

    lax.fori_loop(0, 2, expert, 0)
    home = [
        pltpu.make_async_copy(finb.at[r], retb.at[r], local_sem.at[8]),
        pltpu.make_async_copy(finc.at[r], retc.at[r], local_sem.at[11]),
    ]
    for d in home:
        d.start()

    for d in loads[3:]:
        d.wait()
    keep.wait()
    for s in range(1, 4):
        og = xor(g, s, 2)
        gcopy(shard.at[og], shard.at[og], s, og).wait_recv()
    for h in range(2):
        x = shard[2 * h : 2 * h + 2].reshape(2 * rows, D)
        gate = lax.dot_general(x, sg[...], nt, preferred_element_type=f32)
        up = lax.dot_general(x, su[...], nt, preferred_element_type=f32)
        hidden = (jax.nn.silu(gate) * up).astype(bf)
        for n in range(4):
            cols = pl.ds(n * 512, 512)
            o = jnp.dot(hidden, sd[:, cols], preferred_element_type=f32).astype(bf)
            part[2 * h : 2 * h + 2, :, cols] = o.reshape(2, rows, 512)
    for s in range(1, 4):
        og = xor(g, s, 2)
        gcopy(part.at[og], parts.at[g], 4 + s, og).start()
    own_part = pltpu.make_async_copy(part.at[g], parts.at[g], local_sem.at[9])
    own_part.start()

    lax.fori_loop(2, 4, expert, 0)
    for d in home:
        d.wait()
    own_part.wait()
    for s in range(1, 4):
        og = xor(g, s, 2)
        gcopy(parts.at[og], parts.at[og], 4 + s, og).wait_recv()
    for n in range(4):
        cols = pl.ds(n * 512, 512)
        total = (parts[0, :, cols].astype(f32) + parts[1, :, cols].astype(f32)) + (
            parts[2, :, cols].astype(f32) + parts[3, :, cols].astype(f32))
        acc[:, cols] = state_ref[:, cols] + scale * total

    def gather(k, _):
        plane = xor(y, k, 2)

        def got(m, _):
            e = plane * 16 + xor(low, m, 4)
            for d in pair(retb, retc, e, retb, retc, e, 128 + k * 16 + m, e):
                d.wait_recv()
            return 0

        lax.fori_loop(jnp.where(k == 0, 1, 0), 16, got, 0)
        hi = mix_hi[plane]
        lo = mix_lo[plane]
        for n in range(4):
            cols = pl.ds(n * 512, 512)
            v = jnp.concatenate(
                [retb[pl.ds(plane * 16, 16), :, cols].reshape(16 * MAIN, 512),
                 retc[pl.ds(plane * 16, 16), :, cols].reshape(16 * MORE, 512)],
                axis=0,
            )
            acc[:, cols] += jnp.dot(hi, v, preferred_element_type=f32) + jnp.dot(lo, v, preferred_element_type=f32)
        return 0

    lax.fori_loop(0, 4, gather, 0)
    out_ref[...] = acc[...].astype(bf)

    def sent(s, _):
        for d in pair(outb, outc, 0, arrb, arrc, 0, s, r) + pair(finb, finc, 0, retb, retc, 0, 128 + s, r):
            d.wait_send()
        return 0

    lax.fori_loop(1, NREQ, sent, 0)
    for s in range(1, 4):
        gcopy(normed_ref, shard.at[g], s, g).wait_send()
        gcopy(part.at[0], parts.at[g], 4 + s, g).wait_send()


def moe_block(normed, state, routes, rcols, rw, router, eg, eu, ed, sg, su, sd):
    rows = normed.shape[0]
    vm = pl.BlockSpec(memory_space=pltpu.VMEM)
    hb = pl.BlockSpec(memory_space=pl.ANY)
    bf = jnp.bfloat16
    return pl.pallas_call(
        moe_kernel,
        out_shape=jax.ShapeDtypeStruct((rows, D), bf),
        in_specs=[vm] * 6 + [hb] * 6,
        out_specs=vm,
        scratch_shapes=[
            pltpu.VMEM((4, PLANE, rows), bf),
            pltpu.VMEM((4, rows, PLANE), bf),
            pltpu.VMEM((4, rows, PLANE), bf),
        ] + [
            pltpu.VMEM((NREQ, few, D), bf) for _ in range(4) for few in (MAIN, MORE)
        ] + [
            pltpu.VMEM((4, rows, D), bf),
            pltpu.VMEM((4, rows, D), bf),
            pltpu.VMEM((4, rows, D), bf),
            pltpu.VMEM((rows, D), jnp.float32),
            pltpu.VMEM(eg.shape, bf),
            pltpu.VMEM(eu.shape, bf),
            pltpu.VMEM(ed.shape, bf),
            pltpu.VMEM(sg.shape, bf),
            pltpu.VMEM(su.shape, bf),
            pltpu.VMEM(sd.shape, bf),
            pltpu.SemaphoreType.DMA((4 * NREQ,)),
            pltpu.SemaphoreType.DMA((4 * NREQ,)),
            pltpu.SemaphoreType.DMA((8,)),
            pltpu.SemaphoreType.DMA((8,)),
            pltpu.SemaphoreType.DMA((12,)),
        ],
        compiler_params=pltpu.CompilerParams(
            collective_id=1, has_side_effects=True, vmem_limit_bytes=60 << 20
        ),
        cost_estimate=pl.CostEstimate(flops=14_000_000_000, bytes_accessed=300_000_000, transcendentals=1_500_000),
        name="moe_block",
    )(normed, state, routes, rcols, rw, router, eg, eu, ed, sg, su, sd)


def local(
    suffix_queries,
    suffix_keys,
    suffix_values,
    prefix_cache,
    residual,
    out_weight,
    norm_gain,
    routes,
    route_weights,
    lengths,
    migrate,
    expert_gate,
    expert_up,
    expert_down,
    shared_gate,
    shared_up,
    shared_down,
    shared_router,
):
    rows = suffix_queries.shape[1]
    nreq = lax.axis_size("req")
    ngrp = lax.axis_size("grp")
    me = lax.axis_index("req")
    grp = lax.axis_index("grp")
    prefix_len = prefix_cache.shape[1] * nreq
    width_all = HEADS * HD

    token_ids = me * rows + jnp.arange(rows, dtype=jnp.int32)
    request, offset = request_index(token_ids, lengths[0])
    positions = (prefix_len + offset).astype(jnp.float32)
    cosine, sine_part = rope_tables(positions)
    query_turned = rope_rows(suffix_queries[0], cosine, sine_part)
    key_turned = rope_rows(suffix_keys[0], cosine, sine_part)
    own_cache = jnp.concatenate([key_turned, suffix_values[0]], axis=1)
    partner = lax.ppermute(own_cache, "grp", [(i, i ^ 2) for i in range(ngrp)])
    pair_row = grp // 4 * 2 + grp % 2
    page_flags = jnp.sum(
        jnp.where((jnp.arange(migrate.shape[0], dtype=jnp.int32) == pair_row)[:, None], migrate, 0),
        axis=0,
    )
    page_moved = jnp.repeat(page_flags, PG) == 1
    suffix_cache = jnp.where(page_moved[:, None], partner, own_cache)

    few = prefix_cache.shape[1]
    pp = jnp.transpose(prefix_cache[0].reshape(few, 2, HEADS, HD), (2, 1, 0, 3)).reshape(HEADS, 2 * few, HD)
    pp = jnp.pad(pp, ((0, 0), (0, 16 - 2 * few), (0, 0)))
    held = out_weight.shape[0]
    spot = jnp.arange(ngrp, dtype=jnp.int32)[:, None, None] == grp
    wpad = jnp.where(spot, out_weight[None], jnp.zeros((), jnp.bfloat16)).reshape(ngrp * held, D)
    wpad = jnp.transpose(wpad.reshape(ngrp * held, 2, D // 2), (1, 0, 2))
    state, normed = attention_block(
        query_turned, own_cache, pp, wpad, residual[0], norm_gain[None], lengths
    )

    gate_all = lax.all_gather(jnp.swapaxes(expert_gate[0], 0, 1), "grp", axis=0, tiled=True)
    up_all = lax.all_gather(jnp.swapaxes(expert_up[0], 0, 1), "grp", axis=0, tiled=True)
    down_all = lax.all_gather(expert_down[0], "grp", axis=0, tiled=True)
    final = moe_block(
        normed, state, routes[0], routes[0].T, route_weights[0], shared_router[None],
        gate_all, up_all, down_all, shared_gate.T, shared_up.T, shared_down,
    )
    return (final[None], suffix_cache[None])


def solution(mesh):
    placed = (
        P("grp", "req", None),
        P("grp", "req", None),
        P("grp", "req", None),
        P("grp", "req", None),
        P("grp", "req", None),
        P(("req", "grp"), None),
        P(),
        P("grp", "req", None),
        P("grp", "req", None),
        P("grp", None),
        P(None, "req"),
        P("req", None, "grp"),
        P("req", None, "grp"),
        P("req", "grp", None),
        P(None, "grp"),
        P(None, "grp"),
        P("grp", None),
        P(),
    )
    return jax.shard_map(
        local,
        mesh=mesh,
        in_specs=placed,
        out_specs=(P("grp", "req", None), P("grp", "req", None)),
        check_vma=False,
    )
```

```python
import jax
import jax.numpy as jnp
from jax import lax
from jax.experimental import pallas as pl
from jax.experimental.pallas import tpu as pltpu
from jax.sharding import PartitionSpec as P

D = 2048
HD = 128
HEADS = 8
TOP = 4
PG = 16

ROPE_BASE = 1000000.0
EPSILON = 1e-06


def request_index(token_ids, length_row):
    request_ends = jnp.cumsum(length_row)
    starts = request_ends - length_row
    request = jnp.sum((token_ids[:, None] >= request_ends[None, :]).astype(jnp.int32), axis=1)
    onehot = request[:, None] == jnp.arange(length_row.shape[0], dtype=jnp.int32)[None, :]
    opening = jnp.sum(jnp.where(onehot, starts[None, :], 0), axis=1)
    return (request, token_ids - opening)


def rope_tables(positions):
    half_size = HD // 2
    indices = jnp.arange(half_size, dtype=jnp.float32)
    inv_freq = jnp.power(ROPE_BASE, -2.0 * indices / HD)
    angles = positions[:, None] * inv_freq[None, :]
    return jnp.cos(angles)[:, None, :], jnp.sin(angles)[:, None, :]


def rope_rows(entries, cosine, sine_part):
    half_size = HD // 2
    per_head = entries.astype(jnp.float32).reshape(entries.shape[0], HEADS, HD)
    first_half = per_head[..., :half_size]
    second = per_head[..., half_size:]
    turned = jnp.concatenate(
        [first_half * cosine - second * sine_part, second * cosine + first_half * sine_part],
        axis=-1,
    )
    return turned.reshape(entries.shape[0], HEADS * HD).astype(jnp.bfloat16)


MESH = pl.DeviceIdType.MESH
QS, KS, VS, HK, HV, PB, PX, GS, XS, ZS, YS, CS, OS, WR, WP, WF, NSEM = (
    0, 8, 16, 24, 32, 40, 48, 56, 60, 61, 69, 73, 77, 85, 88, 91, 94)


def attention_kernel(
    q_ref, kv_ref, pp_ref, wpad_ref, resid_ref, gain_ref, len_ref, eg_ref, eu_ref, ed_ref,
    state_ref, normed_ref, wg_ref, wu_ref, wd_ref,
    hold, qbuf, kvbuf, pbuf, pfx, obuf, osend, gbuf, wbuf, pk, pv,
    send_sem, recv_sem, local_sem,
):
    r = lax.axis_index("req")
    g = lax.axis_index("grp")
    b = r // HEADS
    j = r % HEADS
    c = g % 2
    xlo = r % 2
    z = (r // 2) % 8
    y = r // 16
    width = HEADS * HD
    rows = q_ref.shape[0]

    def flip(v, s):
        out = 0
        bit = 1
        while bit < 8:
            has = (v // bit) % 2
            out = out + bit * ((1 - has) if s & bit else has)
            bit *= 2
        return out

    def copy(src, dst, idx, req, grp):
        return pltpu.make_async_remote_copy(
            src_ref=src, dst_ref=dst, send_sem=send_sem.at[idx], recv_sem=recv_sem.at[idx],
            device_id=(req, grp), device_id_type=MESH)

    def lanes(h):
        return pl.ds(pl.multiple_of(h * HD, HD), HD)

    def vlanes(h):
        return pl.ds(pl.multiple_of(width + h * HD, HD), HD)

    up = (b + 1) % 8
    down = (b + 7) % 8

    barrier = pltpu.get_barrier_semaphore()
    peers = [(b * 8 + flip(j, s), g) for s in range(1, 8)]
    peers += [(up * 8 + s, g) for s in range(8)] + [(down * 8 + s, g) for s in range(8)]
    peers += [(flip(b, s) * 8 + j, g) for s in range(1, 8)]
    peers += [(r, flip(g, s)) for s in range(1, 4)]
    peers += [(y * 16 + flip(z, s) * 2 + xlo, g) for s in range(1, 8)]
    peers += [(flip(y, s) * 16 + z * 2 + xlo, g) for s in range(1, 4)]
    for peer in peers:
        pl.semaphore_signal(barrier, inc=1, device_id=peer, device_id_type=MESH)
    pl.semaphore_wait(barrier, len(peers))

    started = []

    def start(*a):
        d = copy(*a)
        d.start()
        started.append(d)

    for s in range(1, 4):
        og = flip(g, s)
        start(wpad_ref.at[og % 2], gbuf.at[g], GS + s, r, og)
    for s in range(1, 8):
        t = flip(j, s)
        start(pp_ref.at[t], pbuf.at[j], PB + s, b * 8 + t, g)
    mine = [
        pltpu.make_async_copy(q_ref.at[:, lanes(j)], qbuf.at[j], local_sem.at[0]),
        pltpu.make_async_copy(kv_ref.at[:, lanes(j)], kvbuf.at[8 + j, pl.ds(0, rows)], local_sem.at[1]),
        pltpu.make_async_copy(kv_ref.at[:, vlanes(j)], kvbuf.at[8 + j, pl.ds(rows, rows)], local_sem.at[2]),
        pltpu.make_async_copy(pp_ref.at[j], pbuf.at[j], local_sem.at[3]),
        pltpu.make_async_copy(wpad_ref.at[c], gbuf.at[g], local_sem.at[4]),
    ]
    for d in mine:
        d.start()
    shards = (eg_ref, eu_ref, ed_ref)
    wholes = (wg_ref, wu_ref, wd_ref)
    take = [pltpu.make_async_copy(shards[n], hold.at[n], local_sem.at[6 + n]) for n in range(3)]
    for d in take:
        d.start()

    def piece(owner):
        return pl.ds(pl.multiple_of(owner * hold.shape[1], 16), hold.shape[1])

    mine[4].wait()
    for s in range(1, 4):
        og = flip(g, s)
        copy(gbuf.at[og], gbuf.at[og], GS + s, r, og).wait_recv()
    w16 = (gbuf[0].astype(jnp.float32) + gbuf[1].astype(jnp.float32)) + (
        gbuf[2].astype(jnp.float32) + gbuf[3].astype(jnp.float32))
    my16 = pl.ds(pl.multiple_of(r * 16, 16), 16)
    wbuf[c, my16, :] = w16.astype(jnp.bfloat16)
    mine[3].wait()
    for s in range(1, 8):
        t = flip(j, s)
        copy(pp_ref.at[t], pbuf.at[t], PB + s, b * 8 + t, g).wait_recv()
    rx = flip(j, 1) + b * 8
    start(wbuf.at[c, my16], wbuf.at[c, my16], XS, rx, g)
    for s in range(1, 8):
        start(pbuf, pfx.at[b], PX + s, flip(b, s) * 8 + j, g)
    keep = pltpu.make_async_copy(pbuf, pfx.at[b], local_sem.at[5])
    keep.start()
    ox16 = pl.ds(pl.multiple_of(rx * 16, 16), 16)
    copy(wbuf.at[c, ox16], wbuf.at[c, ox16], XS, rx, g).wait_recv()
    my32 = pl.ds(pl.multiple_of((r // 2) * 32, 32), 32)
    for s in range(1, 8):
        start(wbuf.at[c, my32], wbuf.at[c, my32], ZS + s, y * 16 + flip(z, s) * 2 + xlo, g)
    for s in range(8):
        t = flip(j, s)
        start(kv_ref.at[:, lanes(t)], kvbuf.at[j, pl.ds(0, rows)], HK + s, up * 8 + t, g)
        start(kv_ref.at[:, vlanes(t)], kvbuf.at[j, pl.ds(rows, rows)], HV + s, up * 8 + t, g)
    for s in range(1, 8):
        t = flip(j, s)
        start(q_ref.at[:, lanes(t)], qbuf.at[j], QS + s, b * 8 + t, g)
        start(kv_ref.at[:, lanes(t)], kvbuf.at[8 + j, pl.ds(0, rows)], KS + s, b * 8 + t, g)
        start(kv_ref.at[:, vlanes(t)], kvbuf.at[8 + j, pl.ds(rows, rows)], VS + s, b * 8 + t, g)
    put = []
    for n in range(3):
        take[n].wait()
        start(hold.at[n], wholes[n].at[piece(g)], WR + n, r, flip(g, 2))
        start(hold.at[n], wholes[n].at[piece(g)], WP + n, r, flip(g, 1))
        d = pltpu.make_async_copy(hold.at[n], wholes[n].at[piece(g)], local_sem.at[6 + n])
        d.start()
        put.append(d)
    for s in range(1, 8):
        oz = pl.ds(pl.multiple_of((y * 8 + flip(z, s)) * 32, 32), 32)
        copy(wbuf.at[c, oz], wbuf.at[c, oz], ZS + s, r, g).wait_recv()
    my256 = pl.ds(pl.multiple_of(y * 256, 256), 256)
    for s in range(1, 4):
        start(wbuf.at[c, my256], wbuf.at[c, my256], YS + s, flip(y, s) * 16 + z * 2 + xlo, g)
    start(wbuf.at[c, my256], wbuf.at[c, my256], CS, r, flip(g, 1))

    def hand_over(q):
        oy = pl.ds(pl.multiple_of(flip(y, q) * 256, 256), 256)
        copy(wbuf.at[c, oy], wbuf.at[c, oy], YS + q, r, g).wait_recv()
        start(wbuf.at[c, oy], wbuf.at[c, oy], CS + q, r, flip(g, 1))

    def pass_on(n):
        far = piece(flip(g, 2))
        copy(wholes[n].at[far], wholes[n].at[far], WR + n, r, g).wait_recv()
        start(wholes[n].at[far], wholes[n].at[far], WF + n, r, flip(g, 1))

    keep.wait()
    for s in range(1, 8):
        ob = flip(b, s)
        copy(pbuf, pfx.at[ob], PX + s, r, g).wait_recv()
    pieces = pfx[...].reshape(8 * 8 * 16, HD)
    ii = lax.broadcasted_iota(jnp.int32, (256, 1024), 0)
    cc = lax.broadcasted_iota(jnp.int32, (256, 1024), 1)
    at = (ii // 4) * 16 + ii % 4
    pk[...] = jnp.dot((cc == at).astype(jnp.bfloat16), pieces, preferred_element_type=jnp.float32).astype(jnp.bfloat16)
    pv[...] = jnp.dot((cc == at + 4).astype(jnp.bfloat16), pieces, preferred_element_type=jnp.float32).astype(jnp.bfloat16)
    for d in mine[:3]:
        d.wait()
    for s in range(1, 8):
        t = flip(j, s)
        copy(qbuf.at[t], qbuf.at[t], QS + s, r, g).wait_recv()
        copy(kvbuf.at[8 + t, pl.ds(0, rows)], kvbuf.at[8 + t, pl.ds(0, rows)], KS + s, r, g).wait_recv()
        copy(kvbuf.at[8 + t, pl.ds(rows, rows)], kvbuf.at[8 + t, pl.ds(rows, rows)], VS + s, r, g).wait_recv()
    for s in range(8):
        t = flip(j, s)
        copy(kvbuf.at[t, pl.ds(0, rows)], kvbuf.at[t, pl.ds(0, rows)], HK + s, r, g).wait_recv()
        copy(kvbuf.at[t, pl.ds(rows, rows)], kvbuf.at[t, pl.ds(rows, rows)], HV + s, r, g).wait_recv()

    span = rows * HEADS
    nwin = span + rows

    def attend(t):
        q_id = b * span + t * rows + lax.broadcasted_iota(jnp.int32, (rows, 1), 0)
        opening = jnp.zeros((rows, 1), jnp.int32)
        end = 0
        for n in range(len_ref.shape[1]):
            end = end + len_ref[0, n]
            opening = jnp.where(q_id >= end, end, opening)
        first = b * span - span + t * rows
        k_id = first + lax.broadcasted_iota(jnp.int32, (rows, nwin), 1)
        q = qbuf[t]
        kw = kvbuf[pl.ds(t, 9), pl.ds(0, rows), :].reshape(nwin, HD)
        vw = kvbuf[pl.ds(t, 9), pl.ds(rows, rows), :].reshape(nwin, HD)
        dims = (((1,), (1,)), ((), ()))
        s1 = lax.dot_general(q, pk[...], dims, preferred_element_type=jnp.float32) * HD ** (-0.5)
        s2 = lax.dot_general(q, kw, dims, preferred_element_type=jnp.float32) * HD ** (-0.5)
        s2 = jnp.where((k_id >= opening) & (k_id <= q_id), s2, -1e30)
        top = jnp.maximum(jnp.max(s1, axis=1, keepdims=True), jnp.max(s2, axis=1, keepdims=True))
        w1 = jnp.exp(s1 - top)
        w2 = jnp.exp(s2 - top)
        total = jnp.sum(w1, axis=1, keepdims=True) + jnp.sum(w2, axis=1, keepdims=True)
        o = jnp.dot(w1.astype(jnp.bfloat16), pv[...], preferred_element_type=jnp.float32)
        o = o + jnp.dot(w2.astype(jnp.bfloat16), vw, preferred_element_type=jnp.float32)
        return (o / total).astype(jnp.bfloat16)

    for s in range(1, 8):
        if s in (5, 6, 7):
            hand_over(s - 4)
        t = flip(j, s)
        osend[t] = attend(t)
        start(osend.at[t], obuf.at[j], OS + s, b * 8 + t, g)
    obuf[j] = attend(j)
    for s in range(1, 8):
        t = flip(j, s)
        copy(obuf.at[t], obuf.at[t], OS + s, r, g).wait_recv()
    pass_on(0)
    for q in range(4):
        oy = pl.ds(pl.multiple_of(flip(y, q) * 256, 256), 256)
        copy(wbuf.at[1 - c, oy], wbuf.at[1 - c, oy], CS + q, r, g).wait_recv()

    attn = jnp.concatenate([obuf[h] for h in range(HEADS)], axis=1)
    wide = 256
    per = wbuf.shape[2] // wide
    total = jnp.zeros((rows, 1), jnp.float32)
    for n in range(2 * per):
        cols = pl.ds(n * wide, wide)
        part = jnp.dot(attn, wbuf[n // per, :, pl.ds((n % per) * wide, wide)], preferred_element_type=jnp.float32)
        part = resid_ref[:, cols].astype(jnp.float32) + part
        state_ref[:, cols] = part
        total = total + jnp.sum(part * part, axis=1, keepdims=True)
    inv = lax.rsqrt(total / D + EPSILON)
    for n in range(2 * per):
        cols = pl.ds(n * wide, wide)
        normed_ref[:, cols] = (state_ref[:, cols] * inv * gain_ref[:, cols]).astype(jnp.bfloat16)
    pass_on(1)
    pass_on(2)
    for n in range(3):
        near = piece(flip(g, 1))
        copy(wholes[n].at[near], wholes[n].at[near], WP + n, r, g).wait_recv()
        last = piece(flip(g, 3))
        copy(wholes[n].at[last], wholes[n].at[last], WF + n, r, g).wait_recv()
        put[n].wait()
    for d in started:
        d.wait_send()


def attention_block(q, kv, pp, wpad, resid, gain, lengths, eg, eu, ed):
    rows = q.shape[0]
    vm = pl.BlockSpec(memory_space=pltpu.VMEM)
    hb = pl.BlockSpec(memory_space=pltpu.HBM)
    bf = jnp.bfloat16
    return pl.pallas_call(
        attention_kernel,
        out_shape=(
            jax.ShapeDtypeStruct((rows, D), jnp.float32),
            jax.ShapeDtypeStruct((rows, D), bf),
        ) + (jax.ShapeDtypeStruct((4 * eg.shape[0], D), bf),) * 3,
        in_specs=[vm] * 6 + [pl.BlockSpec(memory_space=pltpu.SMEM)] + [hb] * 3,
        out_specs=(vm, vm, hb, hb, hb),
        scratch_shapes=[
            pltpu.VMEM((3,) + eg.shape, bf),
            pltpu.VMEM((8, rows, HD), bf),
            pltpu.VMEM((16, 2 * rows, HD), bf),
            pltpu.VMEM((8, 16, HD), bf),
            pltpu.VMEM((8, 8, 16, HD), bf),
            pltpu.VMEM((8, rows, HD), bf),
            pltpu.VMEM((8, rows, HD), bf),
            pltpu.VMEM((4, 16, D // 2), bf),
            pltpu.VMEM((2, HEADS * HD, D // 2), bf),
            pltpu.VMEM((256, HD), bf),
            pltpu.VMEM((256, HD), bf),
            pltpu.SemaphoreType.DMA((NSEM,)),
            pltpu.SemaphoreType.DMA((NSEM,)),
            pltpu.SemaphoreType.DMA((9,)),
        ],
        compiler_params=pltpu.CompilerParams(
            collective_id=0, has_side_effects=True, vmem_limit_bytes=40 << 20
        ),
        cost_estimate=pl.CostEstimate(flops=2_000_000_000, bytes_accessed=150_000_000, transcendentals=1_500_000),
        name="attention_block",
    )(q, kv, pp, wpad, resid, gain, lengths, eg, eu, ed)


MAIN = 8
MORE = 2
NREQ = 64
PLANE = 16 * (MAIN + MORE)


def moe_kernel(
    normed_ref, state_ref, routes_ref, rcols_ref, rw_ref, router_ref,
    egate_ref, eup_ref, edown_ref, sgate_ref, sup_ref, sdown_ref,
    out_ref,
    hit_t, mix_hi, mix_lo, outb, outc, arrb, arrc, finb, finc, retb, retc, shard, part, parts, acc,
    wg, wu, wd, sg, su, sd,
    send_sem, recv_sem, grp_send, grp_recv, local_sem,
):
    r = lax.axis_index("req")
    g = lax.axis_index("grp")
    y = r // 16
    low = r % 16
    rows = normed_ref.shape[0]
    bf = jnp.bfloat16
    f32 = jnp.float32

    def slot_maps(shape, axis, p):
        i = lax.broadcasted_iota(jnp.int32, shape, axis)
        first = i < 16 * MAIN
        rest = i - 16 * MAIN
        return (p * 16 + jnp.where(first, i // MAIN, rest // MORE),
                jnp.where(first, i % MAIN, MAIN + rest % MORE))

    def xor(a, b, bits):
        out = 0
        bit = 1
        for _ in range(bits):
            out = out + bit * (((a // bit) % 2 + (b // bit) % 2) % 2)
            bit *= 2
        return out

    loads = [
        pltpu.make_async_copy(src, dst, local_sem.at[n])
        for n, (src, dst) in enumerate(
            [(egate_ref, wg), (eup_ref, wu), (edown_ref, wd), (sgate_ref, sg), (sup_ref, su), (sdown_ref, sd)]
        )
    ]
    for d in loads:
        d.start()
    barrier = pltpu.get_barrier_semaphore()

    def greet(s, _):
        peer = xor(y, s // 16, 2) * 16 + xor(low, s % 16, 4)
        pl.semaphore_signal(barrier, inc=1, device_id=(peer, g), device_id_type=MESH)
        return 0

    lax.fori_loop(1, NREQ, greet, 0)
    for s in range(1, 4):
        pl.semaphore_signal(barrier, inc=1, device_id=(r, xor(g, s, 2)), device_id_type=MESH)

    ei = lax.broadcasted_iota(jnp.int32, (NREQ, rows), 0)
    named_t = jnp.zeros((NREQ, rows), f32)
    for k in range(TOP):
        named_t = named_t + (rcols_ref[k : k + 1, :] == ei).astype(f32)
    ti = lax.broadcasted_iota(jnp.int32, (rows, rows), 0)
    tj = lax.broadcasted_iota(jnp.int32, (rows, rows), 1)
    slot_t = jnp.dot(named_t.astype(bf), (ti < tj).astype(bf), preferred_element_type=f32)
    for p in range(4):
        expert_of = slot_maps((PLANE, NREQ), 0, p)[0]
        widen_t = (expert_of == lax.broadcasted_iota(jnp.int32, (PLANE, NREQ), 1)).astype(bf)
        mine = jnp.dot(widen_t, named_t.astype(bf), preferred_element_type=f32)
        spot = jnp.dot(widen_t, slot_t.astype(bf), preferred_element_type=f32)
        want = slot_maps((PLANE, rows), 0, p)[1].astype(f32)
        hit_t[p] = jnp.where(spot == want, mine, 0.0).astype(bf)

    pl.semaphore_wait(barrier, NREQ - 1 + 3)

    def rcopy(src, dst, idx, req):
        return pltpu.make_async_remote_copy(
            src_ref=src, dst_ref=dst, send_sem=send_sem.at[idx], recv_sem=recv_sem.at[idx],
            device_id=(req, g), device_id_type=MESH)

    def gcopy(src, dst, idx, grp):
        return pltpu.make_async_remote_copy(
            src_ref=src, dst_ref=dst, send_sem=grp_send.at[idx], recv_sem=grp_recv.at[idx],
            device_id=(r, grp), device_id_type=MESH)

    def pair(b8, b2, i, to8, to2, o, idx, req):
        return (rcopy(b8.at[i], to8.at[o], idx, req), rcopy(b2.at[i], to2.at[o], idx + NREQ, req))

    def halves(v):
        cut = 16 * MAIN
        return v[:cut].reshape(16, MAIN, v.shape[1]), v[cut:].reshape(16, MORE, v.shape[1])

    def dispatch(k, _):
        plane = xor(y, k, 2)
        put = hit_t[plane]
        for n in range(4):
            cols = pl.ds(n * 512, 512)
            block = jnp.dot(put, normed_ref[:, cols], preferred_element_type=f32).astype(bf)
            outb[pl.ds(plane * 16, 16), :, cols], outc[pl.ds(plane * 16, 16), :, cols] = halves(block)

        def one(m, _):
            e = plane * 16 + xor(low, m, 4)
            for d in pair(outb, outc, e, arrb, arrc, r, k * 16 + m, e):
                d.start()
            return 0

        lax.fori_loop(jnp.where(k == 0, 1, 0), 16, one, 0)
        return 0

    dispatch(0, 0)
    own = [
        pltpu.make_async_copy(outb.at[r], arrb.at[r], local_sem.at[6]),
        pltpu.make_async_copy(outc.at[r], arrc.at[r], local_sem.at[10]),
    ]
    for d in own:
        d.start()
    gcopy(normed_ref, shard.at[g], 2, xor(g, 2, 2)).start()
    gcopy(normed_ref, shard.at[g], 1, xor(g, 1, 2)).start()
    keep = pltpu.make_async_copy(normed_ref, shard.at[g], local_sem.at[7])
    keep.start()
    lax.fori_loop(1, 4, dispatch, 0)

    ej = lax.broadcasted_iota(jnp.int32, (rows, NREQ), 1)
    named = jnp.zeros((rows, NREQ), f32)
    heft = jnp.zeros((rows, NREQ), f32)
    for k in range(TOP):
        same = routes_ref[:, k : k + 1] == ej
        named = named + same.astype(f32)
        heft = heft + jnp.where(same, rw_ref[:, k : k + 1], 0.0)
    slot = jnp.dot((tj < ti).astype(bf), named.astype(bf), preferred_element_type=f32)
    heft_hi = heft.astype(bf)
    heft_lo = (heft - heft_hi.astype(f32)).astype(bf)
    for p in range(4):
        expert_of = slot_maps((NREQ, PLANE), 1, p)[0]
        widen = (expert_of == lax.broadcasted_iota(jnp.int32, (NREQ, PLANE), 0)).astype(bf)
        spot = jnp.dot(slot.astype(bf), widen, preferred_element_type=f32)
        hit = spot == slot_maps((rows, PLANE), 1, p)[1].astype(f32)
        mix_hi[p] = jnp.where(hit, jnp.dot(heft_hi, widen, preferred_element_type=f32), 0.0).astype(bf)
        mix_lo[p] = jnp.where(hit, jnp.dot(heft_lo, widen, preferred_element_type=f32), 0.0).astype(bf)
    scale = jax.nn.sigmoid(
        jnp.sum(normed_ref[...].astype(f32) * router_ref[...].astype(f32), axis=1, keepdims=True)
    )
    far = xor(g, 2, 2)
    gcopy(shard.at[far], shard.at[far], 2, far).wait_recv()
    gcopy(shard.at[far], shard.at[far], 3, xor(g, 1, 2)).start()
    for d in loads[:3]:
        d.wait()
    for d in own:
        d.wait()
    nt = (((1,), (1,)), ((), ()))

    def expert(k, _):
        plane = xor(y, k, 2)

        def got(m, _):
            e = plane * 16 + xor(low, m, 4)
            for d in pair(arrb, arrc, e, arrb, arrc, e, k * 16 + m, e):
                d.wait_recv()
            return 0

        lax.fori_loop(jnp.where(k == 0, 1, 0), 16, got, 0)
        x = jnp.concatenate(
            [arrb[pl.ds(plane * 16, 16)].reshape(16 * MAIN, D), arrc[pl.ds(plane * 16, 16)].reshape(16 * MORE, D)],
            axis=0,
        )
        gate = lax.dot_general(x, wg[...], nt, preferred_element_type=f32)
        up = lax.dot_general(x, wu[...], nt, preferred_element_type=f32)
        hidden = (jax.nn.silu(gate) * up).astype(bf)
        for n in range(4):
            cols = pl.ds(n * 512, 512)
            o = jnp.dot(hidden, wd[:, cols], preferred_element_type=f32).astype(bf)
            finb[pl.ds(plane * 16, 16), :, cols], finc[pl.ds(plane * 16, 16), :, cols] = halves(o)

        def back(m, _):
            e = plane * 16 + xor(low, m, 4)
            for d in pair(finb, finc, e, retb, retc, r, 128 + k * 16 + m, e):
                d.start()
            return 0

        lax.fori_loop(jnp.where(k == 0, 1, 0), 16, back, 0)
        return 0

    lax.fori_loop(0, 2, expert, 0)
    home = [
        pltpu.make_async_copy(finb.at[r], retb.at[r], local_sem.at[8]),
        pltpu.make_async_copy(finc.at[r], retc.at[r], local_sem.at[11]),
    ]
    for d in home:
        d.start()

    for d in loads[3:]:
        d.wait()
    keep.wait()
    for s in (1, 3):
        og = xor(g, s, 2)
        gcopy(shard.at[og], shard.at[og], s, og).wait_recv()
    for h in range(2):
        x = shard[2 * h : 2 * h + 2].reshape(2 * rows, D)
        gate = lax.dot_general(x, sg[...], nt, preferred_element_type=f32)
        up = lax.dot_general(x, su[...], nt, preferred_element_type=f32)
        hidden = (jax.nn.silu(gate) * up).astype(bf)
        for n in range(4):
            cols = pl.ds(n * 512, 512)
            o = jnp.dot(hidden, sd[:, cols], preferred_element_type=f32).astype(bf)
            part[2 * h : 2 * h + 2, :, cols] = o.reshape(2, rows, 512)
    other = xor(g, 1, 2)
    gcopy(part.at[xor(g, 3, 2)], parts.at[3], 6, other).start()
    gcopy(part.at[other], parts.at[1], 5, other).start()

    lax.fori_loop(2, 3, expert, 0)
    gcopy(parts.at[3], parts.at[3], 6, other).wait_recv()
    parts[0] = (part[far].astype(f32) + parts[3].astype(f32)).astype(bf)
    lax.fori_loop(3, 4, expert, 0)
    gcopy(parts.at[0], parts.at[2], 7, far).start()
    for d in home:
        d.wait()
    for s in (1, 2):
        gcopy(parts.at[s], parts.at[s], 4 + s if s == 1 else 7, other).wait_recv()
    for n in range(4):
        cols = pl.ds(n * 512, 512)
        total = (part[g, :, cols].astype(f32) + parts[1, :, cols].astype(f32)) + parts[2, :, cols].astype(f32)
        acc[:, cols] = state_ref[:, cols] + scale * total

    def gather(k, _):
        plane = xor(y, k, 2)

        def got(m, _):
            e = plane * 16 + xor(low, m, 4)
            for d in pair(retb, retc, e, retb, retc, e, 128 + k * 16 + m, e):
                d.wait_recv()
            return 0

        lax.fori_loop(jnp.where(k == 0, 1, 0), 16, got, 0)
        hi = mix_hi[plane]
        lo = mix_lo[plane]
        for n in range(4):
            cols = pl.ds(n * 512, 512)
            v = jnp.concatenate(
                [retb[pl.ds(plane * 16, 16), :, cols].reshape(16 * MAIN, 512),
                 retc[pl.ds(plane * 16, 16), :, cols].reshape(16 * MORE, 512)],
                axis=0,
            )
            acc[:, cols] += jnp.dot(hi, v, preferred_element_type=f32) + jnp.dot(lo, v, preferred_element_type=f32)
        return 0

    lax.fori_loop(0, 4, gather, 0)
    out_ref[...] = acc[...].astype(bf)

    def sent(s, _):
        for d in pair(outb, outc, 0, arrb, arrc, 0, s, r) + pair(finb, finc, 0, retb, retc, 0, 128 + s, r):
            d.wait_send()
        return 0

    lax.fori_loop(1, NREQ, sent, 0)
    for s in range(1, 4):
        gcopy(normed_ref, shard.at[g], s, g).wait_send()
        gcopy(part.at[0], parts.at[g], 4 + s, g).wait_send()


def moe_block(normed, state, routes, rcols, rw, router, eg, eu, ed, sg, su, sd):
    rows = normed.shape[0]
    vm = pl.BlockSpec(memory_space=pltpu.VMEM)
    hb = pl.BlockSpec(memory_space=pl.ANY)
    bf = jnp.bfloat16
    return pl.pallas_call(
        moe_kernel,
        out_shape=jax.ShapeDtypeStruct((rows, D), bf),
        in_specs=[vm] * 6 + [hb] * 6,
        out_specs=vm,
        scratch_shapes=[
            pltpu.VMEM((4, PLANE, rows), bf),
            pltpu.VMEM((4, rows, PLANE), bf),
            pltpu.VMEM((4, rows, PLANE), bf),
        ] + [
            pltpu.VMEM((NREQ, few, D), bf) for _ in range(4) for few in (MAIN, MORE)
        ] + [
            pltpu.VMEM((4, rows, D), bf),
            pltpu.VMEM((4, rows, D), bf),
            pltpu.VMEM((4, rows, D), bf),
            pltpu.VMEM((rows, D), jnp.float32),
            pltpu.VMEM(eg.shape, bf),
            pltpu.VMEM(eu.shape, bf),
            pltpu.VMEM(ed.shape, bf),
            pltpu.VMEM(sg.shape, bf),
            pltpu.VMEM(su.shape, bf),
            pltpu.VMEM(sd.shape, bf),
            pltpu.SemaphoreType.DMA((4 * NREQ,)),
            pltpu.SemaphoreType.DMA((4 * NREQ,)),
            pltpu.SemaphoreType.DMA((8,)),
            pltpu.SemaphoreType.DMA((8,)),
            pltpu.SemaphoreType.DMA((12,)),
        ],
        compiler_params=pltpu.CompilerParams(
            collective_id=1, has_side_effects=True, vmem_limit_bytes=60 << 20
        ),
        cost_estimate=pl.CostEstimate(flops=14_000_000_000, bytes_accessed=300_000_000, transcendentals=1_500_000),
        name="moe_block",
    )(normed, state, routes, rcols, rw, router, eg, eu, ed, sg, su, sd)


def local(
    suffix_queries,
    suffix_keys,
    suffix_values,
    prefix_cache,
    residual,
    out_weight,
    norm_gain,
    routes,
    route_weights,
    lengths,
    migrate,
    expert_gate,
    expert_up,
    expert_down,
    shared_gate,
    shared_up,
    shared_down,
    shared_router,
):
    rows = suffix_queries.shape[1]
    nreq = lax.axis_size("req")
    ngrp = lax.axis_size("grp")
    me = lax.axis_index("req")
    grp = lax.axis_index("grp")
    prefix_len = prefix_cache.shape[1] * nreq
    width_all = HEADS * HD

    token_ids = me * rows + jnp.arange(rows, dtype=jnp.int32)
    request, offset = request_index(token_ids, lengths[0])
    positions = (prefix_len + offset).astype(jnp.float32)
    cosine, sine_part = rope_tables(positions)
    query_turned = rope_rows(suffix_queries[0], cosine, sine_part)
    key_turned = rope_rows(suffix_keys[0], cosine, sine_part)
    own_cache = jnp.concatenate([key_turned, suffix_values[0]], axis=1)
    partner = lax.ppermute(own_cache, "grp", [(i, i ^ 2) for i in range(ngrp)])
    pair_row = grp // 4 * 2 + grp % 2
    page_flags = jnp.sum(
        jnp.where((jnp.arange(migrate.shape[0], dtype=jnp.int32) == pair_row)[:, None], migrate, 0),
        axis=0,
    )
    page_moved = jnp.repeat(page_flags, PG) == 1
    suffix_cache = jnp.where(page_moved[:, None], partner, own_cache)

    few = prefix_cache.shape[1]
    pp = jnp.transpose(prefix_cache[0].reshape(few, 2, HEADS, HD), (2, 1, 0, 3)).reshape(HEADS, 2 * few, HD)
    pp = jnp.pad(pp, ((0, 0), (0, 16 - 2 * few), (0, 0)))
    held = out_weight.shape[0]
    spot = jnp.arange(ngrp, dtype=jnp.int32)[:, None, None] == grp
    wpad = jnp.where(spot, out_weight[None], jnp.zeros((), jnp.bfloat16)).reshape(ngrp * held, D)
    wpad = jnp.transpose(wpad.reshape(ngrp * held, 2, D // 2), (1, 0, 2))
    state, normed, gate_all, up_all, down_all = attention_block(
        query_turned, own_cache, pp, wpad, residual[0], norm_gain[None], lengths,
        jnp.swapaxes(expert_gate[0], 0, 1), jnp.swapaxes(expert_up[0], 0, 1), expert_down[0],
    )

    final = moe_block(
        normed, state, routes[0], routes[0].T, route_weights[0], shared_router[None],
        gate_all, up_all, down_all, shared_gate.T, shared_up.T, shared_down,
    )
    return (final[None], suffix_cache[None])


def solution(mesh):
    placed = (
        P("grp", "req", None),
        P("grp", "req", None),
        P("grp", "req", None),
        P("grp", "req", None),
        P("grp", "req", None),
        P(("req", "grp"), None),
        P(),
        P("grp", "req", None),
        P("grp", "req", None),
        P("grp", None),
        P(None, "req"),
        P("req", None, "grp"),
        P("req", None, "grp"),
        P("req", "grp", None),
        P(None, "grp"),
        P(None, "grp"),
        P("grp", None),
        P(),
    )
    return jax.shard_map(
        local,
        mesh=mesh,
        in_specs=placed,
        out_specs=(P("grp", "req", None), P("grp", "req", None)),
        check_vma=False,
    )
```

```python
import jax
import jax.numpy as jnp
from jax import lax
from jax.experimental import pallas as pl
from jax.experimental.pallas import tpu as pltpu
from jax.sharding import PartitionSpec as P

D = 2048
HD = 128
HEADS = 8
TOP = 4
PG = 16

ROPE_BASE = 1000000.0
EPSILON = 1e-06


def request_index(token_ids, length_row):
    request_ends = jnp.cumsum(length_row)
    starts = request_ends - length_row
    request = jnp.sum((token_ids[:, None] >= request_ends[None, :]).astype(jnp.int32), axis=1)
    onehot = request[:, None] == jnp.arange(length_row.shape[0], dtype=jnp.int32)[None, :]
    opening = jnp.sum(jnp.where(onehot, starts[None, :], 0), axis=1)
    return (request, token_ids - opening)


def rope_tables(positions):
    half_size = HD // 2
    indices = jnp.arange(half_size, dtype=jnp.float32)
    inv_freq = jnp.power(ROPE_BASE, -2.0 * indices / HD)
    angles = positions[:, None] * inv_freq[None, :]
    return jnp.cos(angles)[:, None, :], jnp.sin(angles)[:, None, :]


def rope_rows(entries, cosine, sine_part):
    half_size = HD // 2
    per_head = entries.astype(jnp.float32).reshape(entries.shape[0], HEADS, HD)
    first_half = per_head[..., :half_size]
    second = per_head[..., half_size:]
    turned = jnp.concatenate(
        [first_half * cosine - second * sine_part, second * cosine + first_half * sine_part],
        axis=-1,
    )
    return turned.reshape(entries.shape[0], HEADS * HD).astype(jnp.bfloat16)


MESH = pl.DeviceIdType.MESH
QS, KS, VS, HK, HV, PB, PX, GS, XS, ZS, YS, CS, OS, WR, WP, WF, NSEM = (
    0, 8, 16, 24, 32, 40, 48, 56, 60, 61, 69, 73, 77, 85, 88, 91, 94)


def attention_kernel(
    q_ref, kv_ref, px_ref, ow_ref, resid_ref, gain_ref, len_ref, eg_ref, eu_ref,
    state_ref, normed_ref, wg_ref, wu_ref,
    hold, pp_ref, wpad_ref, qbuf, kvbuf, pbuf, pfx, obuf, osend, gbuf, wbuf, pk, pv,
    send_sem, recv_sem, local_sem,
):
    r = lax.axis_index("req")
    g = lax.axis_index("grp")
    b = r // HEADS
    j = r % HEADS
    c = g % 2
    xlo = r % 2
    z = (r // 2) % 8
    y = r // 16
    width = HEADS * HD
    rows = q_ref.shape[0]

    def flip(v, s):
        out = 0
        bit = 1
        while bit < 8:
            has = (v // bit) % 2
            out = out + bit * ((1 - has) if s & bit else has)
            bit *= 2
        return out

    def copy(src, dst, idx, req, grp):
        return pltpu.make_async_remote_copy(
            src_ref=src, dst_ref=dst, send_sem=send_sem.at[idx], recv_sem=recv_sem.at[idx],
            device_id=(req, grp), device_id_type=MESH)

    def lanes(h):
        return pl.ds(pl.multiple_of(h * HD, HD), HD)

    def vlanes(h):
        return pl.ds(pl.multiple_of(width + h * HD, HD), HD)

    up = (b + 1) % 8
    down = (b + 7) % 8

    at = lax.broadcasted_iota(jnp.int32, (16, width), 0)
    few = px_ref.shape[0]
    pieces = jnp.zeros((16, width), jnp.float32)
    left = jnp.zeros((16, width), jnp.float32)
    right = jnp.zeros((16, width), jnp.float32)
    for n in range(few):
        pieces = jnp.where(at == n, px_ref[n : n + 1, :width].astype(jnp.float32), pieces)
        pieces = jnp.where(at == few + n, px_ref[n : n + 1, width:].astype(jnp.float32), pieces)
        left = jnp.where(at == few * g + n, ow_ref[n : n + 1, :width].astype(jnp.float32), left)
        right = jnp.where(at == few * g + n, ow_ref[n : n + 1, width:].astype(jnp.float32), right)
    for h in range(HEADS):
        pp_ref[h] = pieces[:, h * HD : (h + 1) * HD].astype(jnp.bfloat16)
    wpad_ref[0] = left.astype(jnp.bfloat16)
    wpad_ref[1] = right.astype(jnp.bfloat16)

    barrier = pltpu.get_barrier_semaphore()
    peers = [(b * 8 + flip(j, s), g) for s in range(1, 8)]
    peers += [(up * 8 + s, g) for s in range(8)] + [(down * 8 + s, g) for s in range(8)]
    peers += [(flip(b, s) * 8 + j, g) for s in range(1, 8)]
    peers += [(r, flip(g, s)) for s in range(1, 4)]
    peers += [(y * 16 + flip(z, s) * 2 + xlo, g) for s in range(1, 8)]
    peers += [(flip(y, s) * 16 + z * 2 + xlo, g) for s in range(1, 4)]
    for peer in peers:
        pl.semaphore_signal(barrier, inc=1, device_id=peer, device_id_type=MESH)
    pl.semaphore_wait(barrier, len(peers))

    started = []

    def start(*a):
        d = copy(*a)
        d.start()
        started.append(d)

    for s in range(1, 4):
        og = flip(g, s)
        start(wpad_ref.at[og % 2], gbuf.at[g], GS + s, r, og)
    for s in range(1, 8):
        t = flip(j, s)
        start(pp_ref.at[t], pbuf.at[j], PB + s, b * 8 + t, g)
    mine = [
        pltpu.make_async_copy(q_ref.at[:, lanes(j)], qbuf.at[j], local_sem.at[0]),
        pltpu.make_async_copy(kv_ref.at[:, lanes(j)], kvbuf.at[8 + j, pl.ds(0, rows)], local_sem.at[1]),
        pltpu.make_async_copy(kv_ref.at[:, vlanes(j)], kvbuf.at[8 + j, pl.ds(rows, rows)], local_sem.at[2]),
        pltpu.make_async_copy(pp_ref.at[j], pbuf.at[j], local_sem.at[3]),
        pltpu.make_async_copy(wpad_ref.at[c], gbuf.at[g], local_sem.at[4]),
    ]
    for d in mine:
        d.start()
    shards = (eg_ref, eu_ref)
    wholes = (wg_ref, wu_ref)
    take = [pltpu.make_async_copy(shards[n], hold.at[n], local_sem.at[6 + n]) for n in range(2)]
    for d in take:
        d.start()

    def piece(owner):
        return pl.ds(pl.multiple_of(owner * hold.shape[1], 16), hold.shape[1])

    mine[4].wait()
    for s in range(1, 4):
        og = flip(g, s)
        copy(gbuf.at[og], gbuf.at[og], GS + s, r, og).wait_recv()
    w16 = (gbuf[0].astype(jnp.float32) + gbuf[1].astype(jnp.float32)) + (
        gbuf[2].astype(jnp.float32) + gbuf[3].astype(jnp.float32))
    my16 = pl.ds(pl.multiple_of(r * 16, 16), 16)
    wbuf[c, my16, :] = w16.astype(jnp.bfloat16)
    mine[3].wait()
    for s in range(1, 8):
        t = flip(j, s)
        copy(pp_ref.at[t], pbuf.at[t], PB + s, b * 8 + t, g).wait_recv()
    rx = flip(j, 1) + b * 8
    start(wbuf.at[c, my16], wbuf.at[c, my16], XS, rx, g)
    for s in range(1, 8):
        start(pbuf, pfx.at[b], PX + s, flip(b, s) * 8 + j, g)
    keep = pltpu.make_async_copy(pbuf, pfx.at[b], local_sem.at[5])
    keep.start()
    ox16 = pl.ds(pl.multiple_of(rx * 16, 16), 16)
    copy(wbuf.at[c, ox16], wbuf.at[c, ox16], XS, rx, g).wait_recv()
    my32 = pl.ds(pl.multiple_of((r // 2) * 32, 32), 32)
    for s in range(1, 8):
        start(wbuf.at[c, my32], wbuf.at[c, my32], ZS + s, y * 16 + flip(z, s) * 2 + xlo, g)
    for s in range(8):
        t = flip(j, s)
        start(kv_ref.at[:, lanes(t)], kvbuf.at[j, pl.ds(0, rows)], HK + s, up * 8 + t, g)
        start(kv_ref.at[:, vlanes(t)], kvbuf.at[j, pl.ds(rows, rows)], HV + s, up * 8 + t, g)
    for s in range(1, 8):
        t = flip(j, s)
        start(q_ref.at[:, lanes(t)], qbuf.at[j], QS + s, b * 8 + t, g)
        start(kv_ref.at[:, lanes(t)], kvbuf.at[8 + j, pl.ds(0, rows)], KS + s, b * 8 + t, g)
        start(kv_ref.at[:, vlanes(t)], kvbuf.at[8 + j, pl.ds(rows, rows)], VS + s, b * 8 + t, g)
    put = []
    for n in range(2):
        take[n].wait()
        start(hold.at[n], wholes[n].at[piece(g)], WR + n, r, flip(g, 2))
        start(hold.at[n], wholes[n].at[piece(g)], WP + n, r, flip(g, 1))
        d = pltpu.make_async_copy(hold.at[n], wholes[n].at[piece(g)], local_sem.at[6 + n])
        d.start()
        put.append(d)
    for s in range(1, 8):
        oz = pl.ds(pl.multiple_of((y * 8 + flip(z, s)) * 32, 32), 32)
        copy(wbuf.at[c, oz], wbuf.at[c, oz], ZS + s, r, g).wait_recv()
    my256 = pl.ds(pl.multiple_of(y * 256, 256), 256)
    for s in range(1, 4):
        start(wbuf.at[c, my256], wbuf.at[c, my256], YS + s, flip(y, s) * 16 + z * 2 + xlo, g)
    start(wbuf.at[c, my256], wbuf.at[c, my256], CS, r, flip(g, 1))

    def hand_over(q):
        oy = pl.ds(pl.multiple_of(flip(y, q) * 256, 256), 256)
        copy(wbuf.at[c, oy], wbuf.at[c, oy], YS + q, r, g).wait_recv()
        start(wbuf.at[c, oy], wbuf.at[c, oy], CS + q, r, flip(g, 1))

    def pass_on(n):
        far = piece(flip(g, 2))
        copy(wholes[n].at[far], wholes[n].at[far], WR + n, r, g).wait_recv()
        start(wholes[n].at[far], wholes[n].at[far], WF + n, r, flip(g, 1))

    keep.wait()
    for s in range(1, 8):
        ob = flip(b, s)
        copy(pbuf, pfx.at[ob], PX + s, r, g).wait_recv()
    pieces = pfx[...].reshape(8 * 8 * 16, HD)
    ii = lax.broadcasted_iota(jnp.int32, (256, 1024), 0)
    cc = lax.broadcasted_iota(jnp.int32, (256, 1024), 1)
    at = (ii // 4) * 16 + ii % 4
    pk[...] = jnp.dot((cc == at).astype(jnp.bfloat16), pieces, preferred_element_type=jnp.float32).astype(jnp.bfloat16)
    pv[...] = jnp.dot((cc == at + 4).astype(jnp.bfloat16), pieces, preferred_element_type=jnp.float32).astype(jnp.bfloat16)
    for d in mine[:3]:
        d.wait()
    for s in range(1, 8):
        t = flip(j, s)
        copy(qbuf.at[t], qbuf.at[t], QS + s, r, g).wait_recv()
        copy(kvbuf.at[8 + t, pl.ds(0, rows)], kvbuf.at[8 + t, pl.ds(0, rows)], KS + s, r, g).wait_recv()
        copy(kvbuf.at[8 + t, pl.ds(rows, rows)], kvbuf.at[8 + t, pl.ds(rows, rows)], VS + s, r, g).wait_recv()
    for s in range(8):
        t = flip(j, s)
        copy(kvbuf.at[t, pl.ds(0, rows)], kvbuf.at[t, pl.ds(0, rows)], HK + s, r, g).wait_recv()
        copy(kvbuf.at[t, pl.ds(rows, rows)], kvbuf.at[t, pl.ds(rows, rows)], HV + s, r, g).wait_recv()

    span = rows * HEADS
    nwin = span + rows

    def attend(t):
        q_id = b * span + t * rows + lax.broadcasted_iota(jnp.int32, (rows, 1), 0)
        opening = jnp.zeros((rows, 1), jnp.int32)
        end = 0
        for n in range(len_ref.shape[1]):
            end = end + len_ref[0, n]
            opening = jnp.where(q_id >= end, end, opening)
        first = b * span - span + t * rows
        k_id = first + lax.broadcasted_iota(jnp.int32, (rows, nwin), 1)
        q = qbuf[t]
        kw = kvbuf[pl.ds(t, 9), pl.ds(0, rows), :].reshape(nwin, HD)
        vw = kvbuf[pl.ds(t, 9), pl.ds(rows, rows), :].reshape(nwin, HD)
        dims = (((1,), (1,)), ((), ()))
        s1 = lax.dot_general(q, pk[...], dims, preferred_element_type=jnp.float32) * HD ** (-0.5)
        s2 = lax.dot_general(q, kw, dims, preferred_element_type=jnp.float32) * HD ** (-0.5)
        s2 = jnp.where((k_id >= opening) & (k_id <= q_id), s2, -1e30)
        top = jnp.maximum(jnp.max(s1, axis=1, keepdims=True), jnp.max(s2, axis=1, keepdims=True))
        w1 = jnp.exp(s1 - top)
        w2 = jnp.exp(s2 - top)
        total = jnp.sum(w1, axis=1, keepdims=True) + jnp.sum(w2, axis=1, keepdims=True)
        o = jnp.dot(w1.astype(jnp.bfloat16), pv[...], preferred_element_type=jnp.float32)
        o = o + jnp.dot(w2.astype(jnp.bfloat16), vw, preferred_element_type=jnp.float32)
        return (o / total).astype(jnp.bfloat16)

    for s in range(1, 8):
        if s in (5, 6, 7):
            hand_over(s - 4)
        t = flip(j, s)
        osend[t] = attend(t)
        start(osend.at[t], obuf.at[j], OS + s, b * 8 + t, g)
    obuf[j] = attend(j)
    for s in range(1, 8):
        t = flip(j, s)
        copy(obuf.at[t], obuf.at[t], OS + s, r, g).wait_recv()
    pass_on(0)
    for q in range(4):
        oy = pl.ds(pl.multiple_of(flip(y, q) * 256, 256), 256)
        copy(wbuf.at[1 - c, oy], wbuf.at[1 - c, oy], CS + q, r, g).wait_recv()

    attn = jnp.concatenate([obuf[h] for h in range(HEADS)], axis=1)
    wide = 256
    per = wbuf.shape[2] // wide
    total = jnp.zeros((rows, 1), jnp.float32)
    for n in range(2 * per):
        cols = pl.ds(n * wide, wide)
        part = jnp.dot(attn, wbuf[n // per, :, pl.ds((n % per) * wide, wide)], preferred_element_type=jnp.float32)
        part = resid_ref[:, cols].astype(jnp.float32) + part
        state_ref[:, cols] = part
        total = total + jnp.sum(part * part, axis=1, keepdims=True)
    inv = lax.rsqrt(total / D + EPSILON)
    for n in range(2 * per):
        cols = pl.ds(n * wide, wide)
        normed_ref[:, cols] = (state_ref[:, cols] * inv * gain_ref[:, cols]).astype(jnp.bfloat16)
    pass_on(1)
    for n in range(2):
        near = piece(flip(g, 1))
        copy(wholes[n].at[near], wholes[n].at[near], WP + n, r, g).wait_recv()
        last = piece(flip(g, 3))
        copy(wholes[n].at[last], wholes[n].at[last], WF + n, r, g).wait_recv()
        put[n].wait()
    for d in started:
        d.wait_send()


def attention_block(q, kv, px, ow, resid, gain, lengths, eg, eu):
    rows = q.shape[0]
    vm = pl.BlockSpec(memory_space=pltpu.VMEM)
    hb = pl.BlockSpec(memory_space=pltpu.HBM)
    bf = jnp.bfloat16
    return pl.pallas_call(
        attention_kernel,
        out_shape=(
            jax.ShapeDtypeStruct((rows, D), jnp.float32),
            jax.ShapeDtypeStruct((rows, D), bf),
        ) + (jax.ShapeDtypeStruct((4 * eg.shape[0], D), bf),) * 2,
        in_specs=[vm] * 6 + [pl.BlockSpec(memory_space=pltpu.SMEM)] + [hb] * 2,
        out_specs=(vm, vm, hb, hb),
        scratch_shapes=[
            pltpu.VMEM((2,) + eg.shape, bf),
            pltpu.VMEM((8, 16, HD), bf),
            pltpu.VMEM((2, 16, D // 2), bf),
            pltpu.VMEM((8, rows, HD), bf),
            pltpu.VMEM((16, 2 * rows, HD), bf),
            pltpu.VMEM((8, 16, HD), bf),
            pltpu.VMEM((8, 8, 16, HD), bf),
            pltpu.VMEM((8, rows, HD), bf),
            pltpu.VMEM((8, rows, HD), bf),
            pltpu.VMEM((4, 16, D // 2), bf),
            pltpu.VMEM((2, HEADS * HD, D // 2), bf),
            pltpu.VMEM((256, HD), bf),
            pltpu.VMEM((256, HD), bf),
            pltpu.SemaphoreType.DMA((NSEM,)),
            pltpu.SemaphoreType.DMA((NSEM,)),
            pltpu.SemaphoreType.DMA((9,)),
        ],
        compiler_params=pltpu.CompilerParams(
            collective_id=0, has_side_effects=True, vmem_limit_bytes=63 << 20
        ),
        cost_estimate=pl.CostEstimate(flops=2_000_000_000, bytes_accessed=150_000_000, transcendentals=1_500_000),
        name="attention_block",
    )(q, kv, px, ow, resid, gain, lengths, eg, eu)


MAIN = 8
MORE = 2
NREQ = 64
PLANE = 16 * (MAIN + MORE)


def moe_kernel(
    normed_ref, state_ref, rcols_ref, rw_ref, router_ref,
    egate_ref, eup_ref, edown_ref, sgate_ref, sup_ref, sdown_ref, cache_ref,
    out_ref, partner_ref,
    hit_t, mix_hi, mix_lo, outb, outc, arrb, arrc, finb, finc, retb, retc, shard, part, parts, acc,
    wg, wu, wd, sg, su, sd,
    send_sem, recv_sem, grp_send, grp_recv, local_sem,
):
    r = lax.axis_index("req")
    g = lax.axis_index("grp")
    y = r // 16
    low = r % 16
    rows = normed_ref.shape[0]
    bf = jnp.bfloat16
    f32 = jnp.float32

    def slot_maps(shape, axis, p):
        i = lax.broadcasted_iota(jnp.int32, shape, axis)
        first = i < 16 * MAIN
        rest = i - 16 * MAIN
        return (p * 16 + jnp.where(first, i // MAIN, rest // MORE),
                jnp.where(first, i % MAIN, MAIN + rest % MORE))

    def xor(a, b, bits):
        out = 0
        bit = 1
        for _ in range(bits):
            out = out + bit * (((a // bit) % 2 + (b // bit) % 2) % 2)
            bit *= 2
        return out

    span = edown_ref.shape[0]

    def piece(owner):
        return pl.ds(pl.multiple_of(owner * span, 16), span)

    loads = [
        pltpu.make_async_copy(src, dst, local_sem.at[n])
        for n, (src, dst) in enumerate(
            [(egate_ref, wg), (eup_ref, wu), (edown_ref, wd.at[piece(g)]), (sgate_ref, sg), (sup_ref, su), (sdown_ref, sd)]
        )
    ]
    for d in loads:
        d.start()
    barrier = pltpu.get_barrier_semaphore()

    def greet(s, _):
        peer = xor(y, s // 16, 2) * 16 + xor(low, s % 16, 4)
        pl.semaphore_signal(barrier, inc=1, device_id=(peer, g), device_id_type=MESH)
        return 0

    lax.fori_loop(1, NREQ, greet, 0)
    for s in range(1, 4):
        pl.semaphore_signal(barrier, inc=1, device_id=(r, xor(g, s, 2)), device_id_type=MESH)

    ei = lax.broadcasted_iota(jnp.int32, (NREQ, rows), 0)
    named_t = jnp.zeros((NREQ, rows), f32)
    for k in range(TOP):
        named_t = named_t + (rcols_ref[k : k + 1, :] == ei).astype(f32)
    ti = lax.broadcasted_iota(jnp.int32, (rows, rows), 0)
    tj = lax.broadcasted_iota(jnp.int32, (rows, rows), 1)
    slot_t = jnp.dot(named_t.astype(bf), (ti < tj).astype(bf), preferred_element_type=f32)
    for p in range(4):
        expert_of = slot_maps((PLANE, NREQ), 0, p)[0]
        widen_t = (expert_of == lax.broadcasted_iota(jnp.int32, (PLANE, NREQ), 1)).astype(bf)
        mine = jnp.dot(widen_t, named_t.astype(bf), preferred_element_type=f32)
        spot = jnp.dot(widen_t, slot_t.astype(bf), preferred_element_type=f32)
        want = slot_maps((PLANE, rows), 0, p)[1].astype(f32)
        hit_t[p] = jnp.where(spot == want, mine, 0.0).astype(bf)

    pl.semaphore_wait(barrier, NREQ - 1 + 3)

    def rcopy(src, dst, idx, req):
        return pltpu.make_async_remote_copy(
            src_ref=src, dst_ref=dst, send_sem=send_sem.at[idx], recv_sem=recv_sem.at[idx],
            device_id=(req, g), device_id_type=MESH)

    def gcopy(src, dst, idx, grp):
        return pltpu.make_async_remote_copy(
            src_ref=src, dst_ref=dst, send_sem=grp_send.at[idx], recv_sem=grp_recv.at[idx],
            device_id=(r, grp), device_id_type=MESH)

    def pair(b8, b2, i, to8, to2, o, idx, req):
        return (rcopy(b8.at[i], to8.at[o], idx, req), rcopy(b2.at[i], to2.at[o], idx + NREQ, req))

    def halves(v):
        cut = 16 * MAIN
        return v[:cut].reshape(16, MAIN, v.shape[1]), v[cut:].reshape(16, MORE, v.shape[1])

    def dispatch(k, _):
        plane = xor(y, k, 2)
        put = hit_t[plane]
        for n in range(4):
            cols = pl.ds(n * 512, 512)
            block = jnp.dot(put, normed_ref[:, cols], preferred_element_type=f32).astype(bf)
            outb[pl.ds(plane * 16, 16), :, cols], outc[pl.ds(plane * 16, 16), :, cols] = halves(block)

        def one(m, _):
            e = plane * 16 + xor(low, m, 4)
            for d in pair(outb, outc, e, arrb, arrc, r, k * 16 + m, e):
                d.start()
            return 0

        lax.fori_loop(jnp.where(k == 0, 1, 0), 16, one, 0)
        return 0

    lax.fori_loop(0, 2, dispatch, 0)
    far = xor(g, 2, 2)
    other = xor(g, 1, 2)
    loads[2].wait()
    gcopy(wd.at[piece(g)], wd.at[piece(g)], 8, far).start()
    gcopy(wd.at[piece(g)], wd.at[piece(g)], 9, other).start()
    own = [
        pltpu.make_async_copy(outb.at[r], arrb.at[r], local_sem.at[6]),
        pltpu.make_async_copy(outc.at[r], arrc.at[r], local_sem.at[10]),
    ]
    for d in own:
        d.start()
    gcopy(normed_ref, shard.at[g], 2, xor(g, 2, 2)).start()
    gcopy(normed_ref, shard.at[g], 1, xor(g, 1, 2)).start()
    keep = pltpu.make_async_copy(normed_ref, shard.at[g], local_sem.at[7])
    keep.start()
    lax.fori_loop(2, 4, dispatch, 0)

    heft = jnp.zeros((NREQ, rows), f32)
    for k in range(TOP):
        heft = heft + jnp.where(rcols_ref[k : k + 1, :] == ei, rw_ref[k : k + 1, :], 0.0)
    heft_hi = heft.astype(bf)
    heft_lo = (heft - heft_hi.astype(f32)).astype(bf)
    tn = (((0,), (0,)), ((), ()))
    for p in range(4):
        expert_of = slot_maps((NREQ, PLANE), 1, p)[0]
        widen = (expert_of == lax.broadcasted_iota(jnp.int32, (NREQ, PLANE), 0)).astype(bf)
        spot = lax.dot_general(slot_t.astype(bf), widen, tn, preferred_element_type=f32)
        hit = spot == slot_maps((rows, PLANE), 1, p)[1].astype(f32)
        mix_hi[p] = jnp.where(hit, lax.dot_general(heft_hi, widen, tn, preferred_element_type=f32), 0.0).astype(bf)
        mix_lo[p] = jnp.where(hit, lax.dot_general(heft_lo, widen, tn, preferred_element_type=f32), 0.0).astype(bf)
    scale = jax.nn.sigmoid(
        jnp.sum(normed_ref[...].astype(f32) * router_ref[...].astype(f32), axis=1, keepdims=True)
    )
    gcopy(wd.at[piece(far)], wd.at[piece(far)], 8, far).wait_recv()
    gcopy(wd.at[piece(far)], wd.at[piece(far)], 10, other).start()
    gcopy(shard.at[far], shard.at[far], 2, far).wait_recv()
    gcopy(shard.at[far], shard.at[far], 3, other).start()
    for d in loads[:2]:
        d.wait()
    gcopy(wd.at[piece(other)], wd.at[piece(other)], 9, other).wait_recv()
    last = piece(xor(g, 3, 2))
    gcopy(wd.at[last], wd.at[last], 10, other).wait_recv()
    for d in own:
        d.wait()
    nt = (((1,), (1,)), ((), ()))

    def expert(k, _):
        plane = xor(y, k, 2)

        def got(m, _):
            e = plane * 16 + xor(low, m, 4)
            for d in pair(arrb, arrc, e, arrb, arrc, e, k * 16 + m, e):
                d.wait_recv()
            return 0

        lax.fori_loop(jnp.where(k == 0, 1, 0), 16, got, 0)
        x = jnp.concatenate(
            [arrb[pl.ds(plane * 16, 16)].reshape(16 * MAIN, D), arrc[pl.ds(plane * 16, 16)].reshape(16 * MORE, D)],
            axis=0,
        )
        gate = lax.dot_general(x, wg[...], nt, preferred_element_type=f32)
        up = lax.dot_general(x, wu[...], nt, preferred_element_type=f32)
        hidden = (jax.nn.silu(gate) * up).astype(bf)
        for n in range(4):
            cols = pl.ds(n * 512, 512)
            o = jnp.dot(hidden, wd[:, cols], preferred_element_type=f32).astype(bf)
            finb[pl.ds(plane * 16, 16), :, cols], finc[pl.ds(plane * 16, 16), :, cols] = halves(o)

        def back(m, _):
            e = plane * 16 + xor(low, m, 4)
            for d in pair(finb, finc, e, retb, retc, r, 128 + k * 16 + m, e):
                d.start()
            return 0

        lax.fori_loop(jnp.where(k == 0, 1, 0), 16, back, 0)
        return 0

    lax.fori_loop(0, 2, expert, 0)
    home = [
        pltpu.make_async_copy(finb.at[r], retb.at[r], local_sem.at[8]),
        pltpu.make_async_copy(finc.at[r], retc.at[r], local_sem.at[11]),
    ]
    for d in home:
        d.start()

    for d in loads[3:]:
        d.wait()
    keep.wait()
    for s in (1, 3):
        og = xor(g, s, 2)
        gcopy(shard.at[og], shard.at[og], s, og).wait_recv()
    for h in range(2):
        x = shard[2 * h : 2 * h + 2].reshape(2 * rows, D)
        gate = lax.dot_general(x, sg[...], nt, preferred_element_type=f32)
        up = lax.dot_general(x, su[...], nt, preferred_element_type=f32)
        hidden = (jax.nn.silu(gate) * up).astype(bf)
        for n in range(4):
            cols = pl.ds(n * 512, 512)
            o = jnp.dot(hidden, sd[:, cols], preferred_element_type=f32).astype(bf)
            part[2 * h : 2 * h + 2, :, cols] = o.reshape(2, rows, 512)
    gcopy(part.at[xor(g, 3, 2)], parts.at[3], 6, other).start()
    gcopy(part.at[other], parts.at[1], 5, other).start()

    lax.fori_loop(2, 3, expert, 0)
    gcopy(parts.at[3], parts.at[3], 6, other).wait_recv()
    parts[0] = (part[far].astype(f32) + parts[3].astype(f32)).astype(bf)
    lax.fori_loop(3, 4, expert, 0)
    gcopy(parts.at[0], parts.at[2], 7, far).start()
    gcopy(cache_ref, partner_ref, 11, far).start()
    for d in home:
        d.wait()
    for s in (1, 2):
        gcopy(parts.at[s], parts.at[s], 4 + s if s == 1 else 7, other).wait_recv()
    for n in range(4):
        cols = pl.ds(n * 512, 512)
        total = (part[g, :, cols].astype(f32) + parts[1, :, cols].astype(f32)) + parts[2, :, cols].astype(f32)
        acc[:, cols] = state_ref[:, cols] + scale * total

    def gather(k, _):
        plane = xor(y, k, 2)

        def got(m, _):
            e = plane * 16 + xor(low, m, 4)
            for d in pair(retb, retc, e, retb, retc, e, 128 + k * 16 + m, e):
                d.wait_recv()
            return 0

        lax.fori_loop(jnp.where(k == 0, 1, 0), 16, got, 0)
        hi = mix_hi[plane]
        lo = mix_lo[plane]
        for n in range(4):
            cols = pl.ds(n * 512, 512)
            v = jnp.concatenate(
                [retb[pl.ds(plane * 16, 16), :, cols].reshape(16 * MAIN, 512),
                 retc[pl.ds(plane * 16, 16), :, cols].reshape(16 * MORE, 512)],
                axis=0,
            )
            acc[:, cols] += jnp.dot(hi, v, preferred_element_type=f32) + jnp.dot(lo, v, preferred_element_type=f32)
        return 0

    lax.fori_loop(0, 4, gather, 0)
    out_ref[...] = acc[...].astype(bf)

    def sent(s, _):
        for d in pair(outb, outc, 0, arrb, arrc, 0, s, r) + pair(finb, finc, 0, retb, retc, 0, 128 + s, r):
            d.wait_send()
        return 0

    lax.fori_loop(1, NREQ, sent, 0)
    for s in range(1, 4):
        gcopy(normed_ref, shard.at[g], s, g).wait_send()
        gcopy(part.at[0], parts.at[g], 4 + s, g).wait_send()
        gcopy(wd.at[piece(g)], wd.at[piece(g)], 7 + s, g).wait_send()
    gcopy(cache_ref, partner_ref, 11, far).wait()


def moe_block(normed, state, rcols, rw, router, eg, eu, ed, sg, su, sd, cache):
    rows = normed.shape[0]
    vm = pl.BlockSpec(memory_space=pltpu.VMEM)
    hb = pl.BlockSpec(memory_space=pl.ANY)
    bf = jnp.bfloat16
    return pl.pallas_call(
        moe_kernel,
        out_shape=(jax.ShapeDtypeStruct((rows, D), bf), jax.ShapeDtypeStruct(cache.shape, bf)),
        in_specs=[vm] * 5 + [hb] * 7,
        out_specs=(vm, hb),
        scratch_shapes=[
            pltpu.VMEM((4, PLANE, rows), bf),
            pltpu.VMEM((4, rows, PLANE), bf),
            pltpu.VMEM((4, rows, PLANE), bf),
        ] + [
            pltpu.VMEM((NREQ, few, D), bf) for _ in range(4) for few in (MAIN, MORE)
        ] + [
            pltpu.VMEM((4, rows, D), bf),
            pltpu.VMEM((4, rows, D), bf),
            pltpu.VMEM((4, rows, D), bf),
            pltpu.VMEM((rows, D), jnp.float32),
            pltpu.VMEM(eg.shape, bf),
            pltpu.VMEM(eu.shape, bf),
            pltpu.VMEM(eg.shape, bf),
            pltpu.VMEM(sg.shape, bf),
            pltpu.VMEM(su.shape, bf),
            pltpu.VMEM(sd.shape, bf),
            pltpu.SemaphoreType.DMA((4 * NREQ,)),
            pltpu.SemaphoreType.DMA((4 * NREQ,)),
            pltpu.SemaphoreType.DMA((12,)),
            pltpu.SemaphoreType.DMA((12,)),
            pltpu.SemaphoreType.DMA((12,)),
        ],
        compiler_params=pltpu.CompilerParams(
            collective_id=1, has_side_effects=True, vmem_limit_bytes=60 << 20
        ),
        cost_estimate=pl.CostEstimate(flops=14_000_000_000, bytes_accessed=300_000_000, transcendentals=1_500_000),
        name="moe_block",
    )(normed, state, rcols, rw, router, eg, eu, ed, sg, su, sd, cache)


def local(
    suffix_queries,
    suffix_keys,
    suffix_values,
    prefix_cache,
    residual,
    out_weight,
    norm_gain,
    routes,
    route_weights,
    lengths,
    migrate,
    expert_gate,
    expert_up,
    expert_down,
    shared_gate,
    shared_up,
    shared_down,
    shared_router,
):
    rows = suffix_queries.shape[1]
    nreq = lax.axis_size("req")
    me = lax.axis_index("req")
    grp = lax.axis_index("grp")
    prefix_len = prefix_cache.shape[1] * nreq
    width_all = HEADS * HD

    token_ids = me * rows + jnp.arange(rows, dtype=jnp.int32)
    request, offset = request_index(token_ids, lengths[0])
    positions = (prefix_len + offset).astype(jnp.float32)
    cosine, sine_part = rope_tables(positions)
    query_turned = rope_rows(suffix_queries[0], cosine, sine_part)
    key_turned = rope_rows(suffix_keys[0], cosine, sine_part)
    own_cache = jnp.concatenate([key_turned, suffix_values[0]], axis=1)
    pair_row = grp // 4 * 2 + grp % 2
    page_flags = jnp.sum(
        jnp.where((jnp.arange(migrate.shape[0], dtype=jnp.int32) == pair_row)[:, None], migrate, 0),
        axis=0,
    )
    page_moved = jnp.repeat(page_flags, PG) == 1

    state, normed, gate_all, up_all = attention_block(
        query_turned, own_cache, prefix_cache[0], out_weight, residual[0], norm_gain[None], lengths,
        jnp.swapaxes(expert_gate[0], 0, 1), jnp.swapaxes(expert_up[0], 0, 1),
    )

    final, partner = moe_block(
        normed, state, routes[0].T, route_weights[0].T, shared_router[None],
        gate_all, up_all, expert_down[0], shared_gate.T, shared_up.T, shared_down, own_cache,
    )
    suffix_cache = jnp.where(page_moved[:, None], partner, own_cache)
    return (final[None], suffix_cache[None])


def solution(mesh):
    placed = (
        P("grp", "req", None),
        P("grp", "req", None),
        P("grp", "req", None),
        P("grp", "req", None),
        P("grp", "req", None),
        P(("req", "grp"), None),
        P(),
        P("grp", "req", None),
        P("grp", "req", None),
        P("grp", None),
        P(None, "req"),
        P("req", None, "grp"),
        P("req", None, "grp"),
        P("req", "grp", None),
        P(None, "grp"),
        P(None, "grp"),
        P("grp", None),
        P(),
    )
    return jax.shard_map(
        local,
        mesh=mesh,
        in_specs=placed,
        out_specs=(P("grp", "req", None), P("grp", "req", None)),
        check_vma=False,
    )
```

```python
import jax
import jax.numpy as jnp
from jax import lax
from jax.experimental import pallas as pl
from jax.experimental.pallas import tpu as pltpu
from jax.sharding import PartitionSpec as P

D = 2048
HD = 128
HEADS = 8
TOP = 4
PG = 16

ROPE_BASE = 1000000.0
EPSILON = 1e-06


MAIN = 8
MORE = 2
NREQ = 64
PLANE = 16 * (MAIN + MORE)
MESH = pl.DeviceIdType.MESH
QS, KS, VS, HK, HV, PB, PX, GS, XS, ZS, YS, CS, OS, WR, WP, WF, NSEM = (
    0, 8, 16, 24, 32, 40, 48, 56, 60, 61, 69, 73, 77, 85, 88, 91, 94)


def attention_part(
    meanwhile, raw_q, raw_k, v_ref, px_ref, ow_ref, resid_ref, gain_ref, len_ref, freq_ref, eg_ref, eu_ref,
    cache_ref, state_ref, normed_ref, wg_ref, wu_ref,
    q_ref, k_ref, pp_ref, wpad_ref, qbuf, kvbuf, pbuf, pfx, obuf, osend, gbuf, wbuf, pk, pv,
    send_sem, recv_sem, local_sem,
):
    r = lax.axis_index("req")
    g = lax.axis_index("grp")
    b = r // HEADS
    j = r % HEADS
    c = g % 2
    xlo = r % 2
    z = (r // 2) % 8
    y = r // 16
    width = HEADS * HD
    rows = q_ref.shape[0]

    def flip(v, s):
        out = 0
        bit = 1
        while bit < 8:
            has = (v // bit) % 2
            out = out + bit * ((1 - has) if s & bit else has)
            bit *= 2
        return out

    def copy(src, dst, idx, req, grp):
        return pltpu.make_async_remote_copy(
            src_ref=src, dst_ref=dst, send_sem=send_sem.at[idx], recv_sem=recv_sem.at[idx],
            device_id=(req, grp), device_id_type=MESH)

    def lanes(h):
        return pl.ds(pl.multiple_of(h * HD, HD), HD)

    up = (b + 1) % 8

    at = lax.broadcasted_iota(jnp.int32, (16, width), 0)
    at8 = lax.broadcasted_iota(jnp.int32, (8, width), 0)
    few = px_ref.shape[0]
    pieces = jnp.zeros((8, width), jnp.float32)
    left = jnp.zeros((16, width), jnp.float32)
    right = jnp.zeros((16, width), jnp.float32)
    for n in range(few):
        pieces = jnp.where(at8 == n, px_ref[n : n + 1, :width].astype(jnp.float32), pieces)
        pieces = jnp.where(at8 == few + n, px_ref[n : n + 1, width:].astype(jnp.float32), pieces)
        left = jnp.where(at == few * g + n, ow_ref[n : n + 1, :width].astype(jnp.float32), left)
        right = jnp.where(at == few * g + n, ow_ref[n : n + 1, width:].astype(jnp.float32), right)
    for h in range(HEADS):
        pp_ref[h] = pieces[:, h * HD : (h + 1) * HD].astype(jnp.bfloat16)
    wpad_ref[0] = left.astype(jnp.bfloat16)
    wpad_ref[1] = right.astype(jnp.bfloat16)

    def openings(ids):
        opening = jnp.zeros(ids.shape, jnp.int32)
        end = 0
        for n in range(len_ref.shape[1]):
            end = end + len_ref[0, n]
            opening = jnp.where(ids >= end, end, opening)
        return opening

    ids = r * rows + lax.broadcasted_iota(jnp.int32, (rows, 1), 0)
    position = (few * NREQ + ids - openings(ids)).astype(jnp.float32)
    angle = position * freq_ref[...]
    cosine = jnp.cos(angle)
    sine = jnp.sin(angle)
    sine = jnp.where(lax.broadcasted_iota(jnp.int32, (rows, HD), 1) < HD // 2, -sine, sine)
    for raw, turned in ((raw_k, k_ref), (raw_q, q_ref)):
        for h in range(HEADS):
            part = raw[:, h * HD : (h + 1) * HD].astype(jnp.float32)
            turned[:, h * HD : (h + 1) * HD] = (
                part * cosine + pltpu.roll(part, HD // 2, 1) * sine
            ).astype(jnp.bfloat16)
    kept = [
        pltpu.make_async_copy(k_ref, cache_ref.at[:, pl.ds(0, width)], local_sem.at[8]),
        pltpu.make_async_copy(v_ref, cache_ref.at[:, pl.ds(width, width)], local_sem.at[9]),
    ]
    for d in kept:
        d.start()
    meanwhile()

    pl.semaphore_wait(pltpu.get_barrier_semaphore(), NREQ - 1 + 3)

    started = []

    def start(*a):
        d = copy(*a)
        d.start()
        started.append(d)

    for s in range(1, 4):
        og = flip(g, s)
        start(wpad_ref.at[og % 2], gbuf.at[g], GS + s, r, og)
    for s in range(1, 8):
        t = flip(j, s)
        start(pp_ref.at[t], pbuf.at[j], PB + s, b * 8 + t, g)
    mine = [
        pltpu.make_async_copy(q_ref.at[:, lanes(j)], qbuf.at[j], local_sem.at[0]),
        pltpu.make_async_copy(k_ref.at[:, lanes(j)], kvbuf.at[8 + j, pl.ds(0, rows)], local_sem.at[1]),
        pltpu.make_async_copy(v_ref.at[:, lanes(j)], kvbuf.at[8 + j, pl.ds(rows, rows)], local_sem.at[2]),
        pltpu.make_async_copy(pp_ref.at[j], pbuf.at[j], local_sem.at[3]),
        pltpu.make_async_copy(wpad_ref.at[c], gbuf.at[g], local_sem.at[4]),
    ]
    for d in mine:
        d.start()
    shards = (eg_ref, eu_ref)
    wholes = (wg_ref, wu_ref)

    def piece(owner):
        return pl.ds(pl.multiple_of(owner * eg_ref.shape[0], 16), eg_ref.shape[0])

    take = [pltpu.make_async_copy(shards[n], wholes[n].at[piece(g)], local_sem.at[6 + n]) for n in range(2)]
    for d in take:
        d.start()

    mine[4].wait()
    for s in range(1, 4):
        og = flip(g, s)
        copy(gbuf.at[og], gbuf.at[og], GS + s, r, og).wait_recv()
    w16 = (gbuf[0].astype(jnp.float32) + gbuf[1].astype(jnp.float32)) + (
        gbuf[2].astype(jnp.float32) + gbuf[3].astype(jnp.float32))
    my16 = pl.ds(pl.multiple_of(r * 16, 16), 16)
    wbuf[c, my16, :] = w16.astype(jnp.bfloat16)
    mine[3].wait()
    for s in range(1, 8):
        t = flip(j, s)
        copy(pp_ref.at[t], pbuf.at[t], PB + s, b * 8 + t, g).wait_recv()
    rx = flip(j, 1) + b * 8
    start(wbuf.at[c, my16], wbuf.at[c, my16], XS, rx, g)
    for s in range(1, 8):
        start(pbuf, pfx.at[b], PX + s, flip(b, s) * 8 + j, g)
    keep = pltpu.make_async_copy(pbuf, pfx.at[b], local_sem.at[5])
    keep.start()
    ox16 = pl.ds(pl.multiple_of(rx * 16, 16), 16)
    copy(wbuf.at[c, ox16], wbuf.at[c, ox16], XS, rx, g).wait_recv()
    my32 = pl.ds(pl.multiple_of((r // 2) * 32, 32), 32)
    for s in range(1, 8):
        start(wbuf.at[c, my32], wbuf.at[c, my32], ZS + s, y * 16 + flip(z, s) * 2 + xlo, g)
    for s in range(8):
        t = flip(j, s)
        start(k_ref.at[:, lanes(t)], kvbuf.at[j, pl.ds(0, rows)], HK + s, up * 8 + t, g)
        start(v_ref.at[:, lanes(t)], kvbuf.at[j, pl.ds(rows, rows)], HV + s, up * 8 + t, g)
    for s in range(1, 8):
        t = flip(j, s)
        start(q_ref.at[:, lanes(t)], qbuf.at[j], QS + s, b * 8 + t, g)
        start(k_ref.at[:, lanes(t)], kvbuf.at[8 + j, pl.ds(0, rows)], KS + s, b * 8 + t, g)
        start(v_ref.at[:, lanes(t)], kvbuf.at[8 + j, pl.ds(rows, rows)], VS + s, b * 8 + t, g)
    for n in range(2):
        take[n].wait()
        mypiece = wholes[n].at[piece(g)]
        start(mypiece, mypiece, WR + n, r, flip(g, 2))
        start(mypiece, mypiece, WP + n, r, flip(g, 1))
    for s in range(1, 8):
        oz = pl.ds(pl.multiple_of((y * 8 + flip(z, s)) * 32, 32), 32)
        copy(wbuf.at[c, oz], wbuf.at[c, oz], ZS + s, r, g).wait_recv()
    my256 = pl.ds(pl.multiple_of(y * 256, 256), 256)
    for s in range(1, 4):
        start(wbuf.at[c, my256], wbuf.at[c, my256], YS + s, flip(y, s) * 16 + z * 2 + xlo, g)
    start(wbuf.at[c, my256], wbuf.at[c, my256], CS, r, flip(g, 1))

    def hand_over(q):
        oy = pl.ds(pl.multiple_of(flip(y, q) * 256, 256), 256)
        copy(wbuf.at[c, oy], wbuf.at[c, oy], YS + q, r, g).wait_recv()
        start(wbuf.at[c, oy], wbuf.at[c, oy], CS + q, r, flip(g, 1))

    def pass_on(n):
        far = piece(flip(g, 2))
        copy(wholes[n].at[far], wholes[n].at[far], WR + n, r, g).wait_recv()
        start(wholes[n].at[far], wholes[n].at[far], WF + n, r, flip(g, 1))

    keep.wait()
    for s in range(1, 8):
        ob = flip(b, s)
        copy(pbuf, pfx.at[ob], PX + s, r, g).wait_recv()
    pieces = pfx[...].reshape(8 * 8 * 8, HD)
    ii = lax.broadcasted_iota(jnp.int32, (256, 512), 0)
    cc = lax.broadcasted_iota(jnp.int32, (256, 512), 1)
    at = (ii // 4) * 8 + ii % 4
    pk[...] = jnp.dot((cc == at).astype(jnp.bfloat16), pieces, preferred_element_type=jnp.float32).astype(jnp.bfloat16)
    pv[...] = jnp.dot((cc == at + 4).astype(jnp.bfloat16), pieces, preferred_element_type=jnp.float32).astype(jnp.bfloat16)
    for d in mine[:3]:
        d.wait()
    for s in range(1, 8):
        t = flip(j, s)
        copy(qbuf.at[t], qbuf.at[t], QS + s, r, g).wait_recv()
        copy(kvbuf.at[8 + t, pl.ds(0, rows)], kvbuf.at[8 + t, pl.ds(0, rows)], KS + s, r, g).wait_recv()
        copy(kvbuf.at[8 + t, pl.ds(rows, rows)], kvbuf.at[8 + t, pl.ds(rows, rows)], VS + s, r, g).wait_recv()
    for s in range(8):
        t = flip(j, s)
        copy(kvbuf.at[t, pl.ds(0, rows)], kvbuf.at[t, pl.ds(0, rows)], HK + s, r, g).wait_recv()
        copy(kvbuf.at[t, pl.ds(rows, rows)], kvbuf.at[t, pl.ds(rows, rows)], HV + s, r, g).wait_recv()

    span = rows * HEADS
    nwin = span + rows

    def attend(t):
        q_id = b * span + t * rows + lax.broadcasted_iota(jnp.int32, (rows, 1), 0)
        opening = openings(q_id)
        first = b * span - span + t * rows
        k_id = first + lax.broadcasted_iota(jnp.int32, (rows, nwin), 1)
        q = qbuf[t]
        kw = kvbuf[pl.ds(t, 9), pl.ds(0, rows), :].reshape(nwin, HD)
        vw = kvbuf[pl.ds(t, 9), pl.ds(rows, rows), :].reshape(nwin, HD)
        dims = (((1,), (1,)), ((), ()))
        s1 = lax.dot_general(q, pk[...], dims, preferred_element_type=jnp.float32) * HD ** (-0.5)
        s2 = lax.dot_general(q, kw, dims, preferred_element_type=jnp.float32) * HD ** (-0.5)
        s2 = jnp.where((k_id >= opening) & (k_id <= q_id), s2, -1e30)
        top = jnp.maximum(jnp.max(s1, axis=1, keepdims=True), jnp.max(s2, axis=1, keepdims=True))
        w1 = jnp.exp(s1 - top)
        w2 = jnp.exp(s2 - top)
        total = jnp.sum(w1, axis=1, keepdims=True) + jnp.sum(w2, axis=1, keepdims=True)
        o = jnp.dot(w1.astype(jnp.bfloat16), pv[...], preferred_element_type=jnp.float32)
        o = o + jnp.dot(w2.astype(jnp.bfloat16), vw, preferred_element_type=jnp.float32)
        return (o / total).astype(jnp.bfloat16)

    for s in range(1, 8):
        if s in (5, 6, 7):
            hand_over(s - 4)
        t = flip(j, s)
        osend[t] = attend(t)
        start(osend.at[t], obuf.at[j], OS + s, b * 8 + t, g)
    obuf[j] = attend(j)
    for s in range(1, 8):
        t = flip(j, s)
        copy(obuf.at[t], obuf.at[t], OS + s, r, g).wait_recv()
    pass_on(0)
    for q in range(4):
        oy = pl.ds(pl.multiple_of(flip(y, q) * 256, 256), 256)
        copy(wbuf.at[1 - c, oy], wbuf.at[1 - c, oy], CS + q, r, g).wait_recv()

    attn = jnp.concatenate([obuf[h] for h in range(HEADS)], axis=1)
    wide = 256
    per = wbuf.shape[2] // wide
    total = jnp.zeros((rows, 1), jnp.float32)
    for n in range(2 * per):
        cols = pl.ds(n * wide, wide)
        part = jnp.dot(attn, wbuf[n // per, :, pl.ds((n % per) * wide, wide)], preferred_element_type=jnp.float32)
        part = resid_ref[:, cols].astype(jnp.float32) + part
        state_ref[:, cols] = part
        total = total + jnp.sum(part * part, axis=1, keepdims=True)
    inv = lax.rsqrt(total / D + EPSILON)
    for n in range(2 * per):
        cols = pl.ds(n * wide, wide)
        normed_ref[:, cols] = (state_ref[:, cols] * inv * gain_ref[:, cols]).astype(jnp.bfloat16)
    pass_on(1)

    def weights_in():
        for n in range(2):
            near = piece(flip(g, 1))
            copy(wholes[n].at[near], wholes[n].at[near], WP + n, r, g).wait_recv()
            last = piece(flip(g, 3))
            copy(wholes[n].at[last], wholes[n].at[last], WF + n, r, g).wait_recv()

    def finish():
        for d in kept:
            d.wait()
        for d in started:
            d.wait_send()

    return weights_in, finish


def layer_kernel(
    raw_q, raw_k, v_ref, px_ref, ow_ref, resid_ref, gain_ref, freq_ref,
    rcols_ref, rw_ref, router_ref, len_ref,
    egate_ref, eup_ref, edown_ref, sgate_ref, sup_ref, sdown_ref,
    out_ref, cache_ref, partner_ref,
    state_ref, normed_ref,
    hit_t, mix_hi, mix_lo, outb, outc, arrb, arrc, finb, finc, retb, retc, shard, part, parts, acc,
    wg, wu, wd, sg, su, sd,
    send_sem, recv_sem, grp_send, grp_recv, local_sem,
    k_turned, *attention_scratch,
):
    r = lax.axis_index("req")
    g = lax.axis_index("grp")
    y = r // 16
    low = r % 16
    rows = normed_ref.shape[0]
    bf = jnp.bfloat16
    f32 = jnp.float32

    def slot_maps(shape, axis, p):
        i = lax.broadcasted_iota(jnp.int32, shape, axis)
        first = i < 16 * MAIN
        rest = i - 16 * MAIN
        return (p * 16 + jnp.where(first, i // MAIN, rest // MORE),
                jnp.where(first, i % MAIN, MAIN + rest % MORE))

    def xor(a, b, bits):
        out = 0
        bit = 1
        for _ in range(bits):
            out = out + bit * (((a // bit) % 2 + (b // bit) % 2) % 2)
            bit *= 2
        return out

    span = edown_ref.shape[0]

    def piece(owner):
        return pl.ds(pl.multiple_of(owner * span, 16), span)

    barrier = pltpu.get_barrier_semaphore()

    def greet(s, _):
        peer = xor(y, s // 16, 2) * 16 + xor(low, s % 16, 4)
        pl.semaphore_signal(barrier, inc=1, device_id=(peer, g), device_id_type=MESH)
        return 0

    lax.fori_loop(1, NREQ, greet, 0)
    for s in range(1, 4):
        pl.semaphore_signal(barrier, inc=1, device_id=(r, xor(g, s, 2)), device_id_type=MESH)

    loads = [
        pltpu.make_async_copy(src, dst, local_sem.at[n])
        for n, (src, dst) in enumerate(
            [(edown_ref, wd.at[piece(g)]), (sgate_ref, sg), (sup_ref, su), (sdown_ref, sd)]
        )
    ]
    for d in loads:
        d.start()
    maps = []

    def places():
        ei = lax.broadcasted_iota(jnp.int32, (NREQ, rows), 0)
        named_t = jnp.zeros((NREQ, rows), f32)
        for k in range(TOP):
            named_t = named_t + (rcols_ref[k : k + 1, :] == ei).astype(f32)
        ti = lax.broadcasted_iota(jnp.int32, (rows, rows), 0)
        tj = lax.broadcasted_iota(jnp.int32, (rows, rows), 1)
        slot_t = jnp.dot(named_t.astype(bf), (ti < tj).astype(bf), preferred_element_type=f32)
        for p in range(4):
            expert_of = slot_maps((PLANE, NREQ), 0, p)[0]
            widen_t = (expert_of == lax.broadcasted_iota(jnp.int32, (PLANE, NREQ), 1)).astype(bf)
            mine = jnp.dot(widen_t, named_t.astype(bf), preferred_element_type=f32)
            spot = jnp.dot(widen_t, slot_t.astype(bf), preferred_element_type=f32)
            want = slot_maps((PLANE, rows), 0, p)[1].astype(f32)
            hit_t[p] = jnp.where(spot == want, mine, 0.0).astype(bf)
        maps.extend((ei, ti, slot_t))

    weights_in, finish = attention_part(
        places, raw_q, raw_k, v_ref, px_ref, ow_ref, resid_ref, gain_ref, len_ref, freq_ref, egate_ref, eup_ref,
        cache_ref, state_ref, normed_ref, wg, wu,
        attention_scratch[0], k_turned, *attention_scratch[1:],
    )
    ei, ti, slot_t = maps

    def rcopy(src, dst, idx, req):
        return pltpu.make_async_remote_copy(
            src_ref=src, dst_ref=dst, send_sem=send_sem.at[idx], recv_sem=recv_sem.at[idx],
            device_id=(req, g), device_id_type=MESH)

    def gcopy(src, dst, idx, grp):
        return pltpu.make_async_remote_copy(
            src_ref=src, dst_ref=dst, send_sem=grp_send.at[idx], recv_sem=grp_recv.at[idx],
            device_id=(r, grp), device_id_type=MESH)

    def pair(b8, b2, i, to8, to2, o, idx, req):
        return (rcopy(b8.at[i], to8.at[o], idx, req), rcopy(b2.at[i], to2.at[o], idx + NREQ, req))

    def halves(v):
        cut = 16 * MAIN
        return v[:cut].reshape(16, MAIN, v.shape[1]), v[cut:].reshape(16, MORE, v.shape[1])

    def dispatch(k, _):
        plane = xor(y, k, 2)
        put = hit_t[plane]
        for n in range(4):
            cols = pl.ds(n * 512, 512)
            block = jnp.dot(put, normed_ref[:, cols], preferred_element_type=f32).astype(bf)
            outb[pl.ds(plane * 16, 16), :, cols], outc[pl.ds(plane * 16, 16), :, cols] = halves(block)

        def one(m, _):
            e = plane * 16 + xor(low, m, 4)
            for d in pair(outb, outc, e, arrb, arrc, r, k * 16 + m, e):
                d.start()
            return 0

        lax.fori_loop(jnp.where(k == 0, 1, 0), 16, one, 0)
        return 0

    lax.fori_loop(0, 2, dispatch, 0)
    far = xor(g, 2, 2)
    other = xor(g, 1, 2)
    loads[0].wait()
    gcopy(wd.at[piece(g)], wd.at[piece(g)], 8, far).start()
    gcopy(wd.at[piece(g)], wd.at[piece(g)], 9, other).start()
    own = [
        pltpu.make_async_copy(outb.at[r], arrb.at[r], local_sem.at[6]),
        pltpu.make_async_copy(outc.at[r], arrc.at[r], local_sem.at[10]),
    ]
    for d in own:
        d.start()
    gcopy(normed_ref, shard.at[g], 2, xor(g, 2, 2)).start()
    gcopy(normed_ref, shard.at[g], 1, xor(g, 1, 2)).start()
    keep = pltpu.make_async_copy(normed_ref, shard.at[g], local_sem.at[7])
    keep.start()
    lax.fori_loop(2, 4, dispatch, 0)

    heft = jnp.zeros((NREQ, rows), f32)
    for k in range(TOP):
        heft = heft + jnp.where(rcols_ref[k : k + 1, :] == ei, rw_ref[k : k + 1, :], 0.0)
    heft_hi = heft.astype(bf)
    heft_lo = (heft - heft_hi.astype(f32)).astype(bf)
    tn = (((0,), (0,)), ((), ()))
    for p in range(4):
        expert_of = slot_maps((NREQ, PLANE), 1, p)[0]
        widen = (expert_of == lax.broadcasted_iota(jnp.int32, (NREQ, PLANE), 0)).astype(bf)
        spot = lax.dot_general(slot_t.astype(bf), widen, tn, preferred_element_type=f32)
        hit = spot == slot_maps((rows, PLANE), 1, p)[1].astype(f32)
        mix_hi[p] = jnp.where(hit, lax.dot_general(heft_hi, widen, tn, preferred_element_type=f32), 0.0).astype(bf)
        mix_lo[p] = jnp.where(hit, lax.dot_general(heft_lo, widen, tn, preferred_element_type=f32), 0.0).astype(bf)
    scale = jax.nn.sigmoid(
        jnp.sum(normed_ref[...].astype(f32) * router_ref[...].astype(f32), axis=1, keepdims=True)
    )
    gcopy(wd.at[piece(far)], wd.at[piece(far)], 8, far).wait_recv()
    gcopy(wd.at[piece(far)], wd.at[piece(far)], 10, other).start()
    gcopy(shard.at[far], shard.at[far], 2, far).wait_recv()
    gcopy(shard.at[far], shard.at[far], 3, other).start()
    weights_in()
    gcopy(wd.at[piece(other)], wd.at[piece(other)], 9, other).wait_recv()
    last = piece(xor(g, 3, 2))
    gcopy(wd.at[last], wd.at[last], 10, other).wait_recv()
    for d in own:
        d.wait()
    nt = (((1,), (1,)), ((), ()))

    def expert(k, _):
        plane = xor(y, k, 2)

        def got(m, _):
            e = plane * 16 + xor(low, m, 4)
            for d in pair(arrb, arrc, e, arrb, arrc, e, k * 16 + m, e):
                d.wait_recv()
            return 0

        lax.fori_loop(jnp.where(k == 0, 1, 0), 16, got, 0)
        x = jnp.concatenate(
            [arrb[pl.ds(plane * 16, 16)].reshape(16 * MAIN, D), arrc[pl.ds(plane * 16, 16)].reshape(16 * MORE, D)],
            axis=0,
        )
        gate = lax.dot_general(x, wg[...], nt, preferred_element_type=f32)
        up = lax.dot_general(x, wu[...], nt, preferred_element_type=f32)
        hidden = (jax.nn.silu(gate) * up).astype(bf)
        for n in range(4):
            cols = pl.ds(n * 512, 512)
            o = jnp.dot(hidden, wd[:, cols], preferred_element_type=f32).astype(bf)
            finb[pl.ds(plane * 16, 16), :, cols], finc[pl.ds(plane * 16, 16), :, cols] = halves(o)

        def back(m, _):
            e = plane * 16 + xor(low, m, 4)
            for d in pair(finb, finc, e, retb, retc, r, 128 + k * 16 + m, e):
                d.start()
            return 0

        lax.fori_loop(jnp.where(k == 0, 1, 0), 16, back, 0)
        return 0

    lax.fori_loop(0, 2, expert, 0)
    home = [
        pltpu.make_async_copy(finb.at[r], retb.at[r], local_sem.at[8]),
        pltpu.make_async_copy(finc.at[r], retc.at[r], local_sem.at[11]),
    ]
    for d in home:
        d.start()

    for d in loads[1:]:
        d.wait()
    keep.wait()
    for s in (1, 3):
        og = xor(g, s, 2)
        gcopy(shard.at[og], shard.at[og], s, og).wait_recv()
    for h in range(2):
        x = shard[2 * h : 2 * h + 2].reshape(2 * rows, D)
        gate = lax.dot_general(x, sg[...], nt, preferred_element_type=f32)
        up = lax.dot_general(x, su[...], nt, preferred_element_type=f32)
        hidden = (jax.nn.silu(gate) * up).astype(bf)
        for n in range(4):
            cols = pl.ds(n * 512, 512)
            o = jnp.dot(hidden, sd[:, cols], preferred_element_type=f32).astype(bf)
            part[2 * h : 2 * h + 2, :, cols] = o.reshape(2, rows, 512)
    gcopy(part.at[xor(g, 3, 2)], parts.at[3], 6, other).start()
    gcopy(part.at[other], parts.at[1], 5, other).start()

    lax.fori_loop(2, 3, expert, 0)
    gcopy(parts.at[3], parts.at[3], 6, other).wait_recv()
    parts[0] = (part[far].astype(f32) + parts[3].astype(f32)).astype(bf)
    lax.fori_loop(3, 4, expert, 0)
    gcopy(parts.at[0], parts.at[2], 7, far).start()
    width = HEADS * HD
    swaps = [
        gcopy(k_turned, partner_ref.at[:, pl.ds(0, width)], 11, far),
        gcopy(v_ref, partner_ref.at[:, pl.ds(width, width)], 4, far),
    ]
    for d in swaps:
        d.start()
    for d in home:
        d.wait()
    for s in (1, 2):
        gcopy(parts.at[s], parts.at[s], 4 + s if s == 1 else 7, other).wait_recv()
    for n in range(4):
        cols = pl.ds(n * 512, 512)
        total = (part[g, :, cols].astype(f32) + parts[1, :, cols].astype(f32)) + parts[2, :, cols].astype(f32)
        acc[:, cols] = state_ref[:, cols] + scale * total

    def gather(k, _):
        plane = xor(y, k, 2)

        def got(m, _):
            e = plane * 16 + xor(low, m, 4)
            for d in pair(retb, retc, e, retb, retc, e, 128 + k * 16 + m, e):
                d.wait_recv()
            return 0

        lax.fori_loop(jnp.where(k == 0, 1, 0), 16, got, 0)
        hi = mix_hi[plane]
        lo = mix_lo[plane]
        for n in range(4):
            cols = pl.ds(n * 512, 512)
            v = jnp.concatenate(
                [retb[pl.ds(plane * 16, 16), :, cols].reshape(16 * MAIN, 512),
                 retc[pl.ds(plane * 16, 16), :, cols].reshape(16 * MORE, 512)],
                axis=0,
            )
            acc[:, cols] += jnp.dot(hi, v, preferred_element_type=f32) + jnp.dot(lo, v, preferred_element_type=f32)
        return 0

    lax.fori_loop(0, 4, gather, 0)
    out_ref[...] = acc[...].astype(bf)

    def sent(s, _):
        for d in pair(outb, outc, 0, arrb, arrc, 0, s, r) + pair(finb, finc, 0, retb, retc, 0, 128 + s, r):
            d.wait_send()
        return 0

    lax.fori_loop(1, NREQ, sent, 0)
    for s in range(1, 4):
        gcopy(normed_ref, shard.at[g], s, g).wait_send()
        gcopy(part.at[0], parts.at[g], 4 + s, g).wait_send()
        gcopy(wd.at[piece(g)], wd.at[piece(g)], 7 + s, g).wait_send()
    for d in swaps:
        d.wait()
    finish()


def layer(blocks, lengths, bulk):
    rows = blocks[0].shape[0]
    vm = pl.BlockSpec(memory_space=pltpu.VMEM)
    hb = pl.BlockSpec(memory_space=pltpu.HBM)
    bf = jnp.bfloat16
    wide = (4 * bulk[0].shape[0], D)
    return pl.pallas_call(
        layer_kernel,
        out_shape=(jax.ShapeDtypeStruct((rows, D), bf),) * 3,
        in_specs=[vm] * len(blocks) + [pl.BlockSpec(memory_space=pltpu.SMEM)] + [hb] * len(bulk),
        out_specs=(vm, hb, hb),
        scratch_shapes=[
            pltpu.VMEM((rows, D), jnp.float32),
            pltpu.VMEM((rows, D), bf),
            pltpu.VMEM((4, PLANE, rows), bf),
            pltpu.VMEM((4, rows, PLANE), bf),
            pltpu.VMEM((4, rows, PLANE), bf),
        ] + [
            pltpu.VMEM((NREQ, few, D), bf) for _ in range(4) for few in (MAIN, MORE)
        ] + [
            pltpu.VMEM((4, rows, D), bf),
            pltpu.VMEM((4, rows, D), bf),
            pltpu.VMEM((4, rows, D), bf),
            pltpu.VMEM((rows, D), jnp.float32),
        ] + [
            pltpu.VMEM(wide, bf) for _ in range(6)
        ] + [
            pltpu.SemaphoreType.DMA((4 * NREQ,)),
            pltpu.SemaphoreType.DMA((4 * NREQ,)),
            pltpu.SemaphoreType.DMA((12,)),
            pltpu.SemaphoreType.DMA((12,)),
            pltpu.SemaphoreType.DMA((12,)),
            pltpu.VMEM((rows, HEADS * HD), bf),
            pltpu.VMEM((rows, HEADS * HD), bf),
            pltpu.VMEM((8, 8, HD), bf),
            pltpu.VMEM((2, 16, D // 2), bf),
            pltpu.VMEM((8, rows, HD), bf),
            pltpu.VMEM((16, 2 * rows, HD), bf),
            pltpu.VMEM((8, 8, HD), bf),
            pltpu.VMEM((8, 8, 8, HD), bf),
            pltpu.VMEM((8, rows, HD), bf),
            pltpu.VMEM((8, rows, HD), bf),
            pltpu.VMEM((4, 16, D // 2), bf),
            pltpu.VMEM((2, HEADS * HD, D // 2), bf),
            pltpu.VMEM((256, HD), bf),
            pltpu.VMEM((256, HD), bf),
            pltpu.SemaphoreType.DMA((NSEM,)),
            pltpu.SemaphoreType.DMA((NSEM,)),
            pltpu.SemaphoreType.DMA((10,)),
        ],
        compiler_params=pltpu.CompilerParams(
            collective_id=0, has_side_effects=True, vmem_limit_bytes=63 << 20
        ),
        cost_estimate=pl.CostEstimate(flops=16_000_000_000, bytes_accessed=60_000_000, transcendentals=3_000_000),
        name="layer",
    )(*blocks, lengths, *bulk)


def local(
    suffix_queries,
    suffix_keys,
    suffix_values,
    prefix_cache,
    residual,
    out_weight,
    norm_gain,
    routes,
    route_weights,
    lengths,
    migrate,
    expert_gate,
    expert_up,
    expert_down,
    shared_gate,
    shared_up,
    shared_down,
    shared_router,
):
    grp = lax.axis_index("grp")
    half = jnp.arange(HD // 2, dtype=jnp.float32)
    freq = jnp.power(ROPE_BASE, -2.0 * half / HD)
    blocks = (
        suffix_queries[0], suffix_keys[0], suffix_values[0], prefix_cache[0], out_weight, residual[0],
        norm_gain[None], jnp.concatenate([freq, freq])[None],
        routes[0].T, route_weights[0].T, shared_router.astype(jnp.float32)[None],
    )
    bulk = (
        jnp.swapaxes(expert_gate[0], 0, 1), jnp.swapaxes(expert_up[0], 0, 1), expert_down[0],
        shared_gate.T, shared_up.T, shared_down,
    )
    final, own_cache, partner = layer(blocks, lengths, bulk)
    pair_row = grp // 4 * 2 + grp % 2
    page_flags = jnp.sum(
        jnp.where((jnp.arange(migrate.shape[0], dtype=jnp.int32) == pair_row)[:, None], migrate, 0),
        axis=0,
    )
    page_moved = jnp.repeat(page_flags, PG) == 1
    suffix_cache = jnp.where(page_moved[:, None], partner, own_cache)
    return (final[None], suffix_cache[None])


def solution(mesh):
    placed = (
        P("grp", "req", None),
        P("grp", "req", None),
        P("grp", "req", None),
        P("grp", "req", None),
        P("grp", "req", None),
        P(("req", "grp"), None),
        P(),
        P("grp", "req", None),
        P("grp", "req", None),
        P("grp", None),
        P(None, "req"),
        P("req", None, "grp"),
        P("req", None, "grp"),
        P("req", "grp", None),
        P(None, "grp"),
        P(None, "grp"),
        P("grp", None),
        P(),
    )
    return jax.shard_map(
        local,
        mesh=mesh,
        in_specs=placed,
        out_specs=(P("grp", "req", None), P("grp", "req", None)),
        check_vma=False,
    )
```

```python
import jax
import jax.numpy as jnp
from jax import lax
from jax.experimental import pallas as pl
from jax.experimental.pallas import tpu as pltpu
from jax.sharding import PartitionSpec as P

D = 2048
HD = 128
HEADS = 8
TOP = 4
PG = 16

ROPE_BASE = 1000000.0
EPSILON = 1e-06


MAIN = 8
MORE = 2
NREQ = 64
PLANE = 16 * (MAIN + MORE)
MESH = pl.DeviceIdType.MESH
QS, KS, VS, HK, HV, PB, PX, GS, XS, ZS, YS, CS, OS, WR, WP, WF, NSEM = (
    0, 8, 16, 24, 32, 40, 48, 56, 60, 61, 69, 73, 77, 85, 88, 91, 94)


def attention_part(
    meanwhile, raw_q, raw_k, v_ref, px_ref, ow_ref, resid_ref, gain_ref, len_ref, freq_ref, eg_ref, eu_ref,
    cache_ref, state_ref, normed_ref, wg_ref, wu_ref,
    q_ref, k_ref, pp_ref, wpad_ref, qbuf, kvbuf, pbuf, pfx, obuf, osend, gbuf, wbuf, pk, pv,
    send_sem, recv_sem, local_sem,
):
    r = lax.axis_index("req")
    g = lax.axis_index("grp")
    b = r // HEADS
    j = r % HEADS
    c = g % 2
    xlo = r % 2
    z = (r // 2) % 8
    y = r // 16
    width = HEADS * HD
    rows = q_ref.shape[0]

    def flip(v, s):
        out = 0
        bit = 1
        while bit < 8:
            has = (v // bit) % 2
            out = out + bit * ((1 - has) if s & bit else has)
            bit *= 2
        return out

    def copy(src, dst, idx, req, grp):
        return pltpu.make_async_remote_copy(
            src_ref=src, dst_ref=dst, send_sem=send_sem.at[idx], recv_sem=recv_sem.at[idx],
            device_id=(req, grp), device_id_type=MESH)

    def lanes(h):
        return pl.ds(pl.multiple_of(h * HD, HD), HD)

    up = (b + 1) % 8

    at = lax.broadcasted_iota(jnp.int32, (16, width), 0)
    at8 = lax.broadcasted_iota(jnp.int32, (8, width), 0)
    few = px_ref.shape[0]
    pieces = jnp.zeros((8, width), jnp.float32)
    left = jnp.zeros((16, width), jnp.float32)
    right = jnp.zeros((16, width), jnp.float32)
    for n in range(few):
        pieces = jnp.where(at8 == n, px_ref[n : n + 1, :width].astype(jnp.float32), pieces)
        pieces = jnp.where(at8 == few + n, px_ref[n : n + 1, width:].astype(jnp.float32), pieces)
        left = jnp.where(at == few * g + n, ow_ref[n : n + 1, :width].astype(jnp.float32), left)
        right = jnp.where(at == few * g + n, ow_ref[n : n + 1, width:].astype(jnp.float32), right)
    for h in range(HEADS):
        pp_ref[h] = pieces[:, h * HD : (h + 1) * HD].astype(jnp.bfloat16)
    wpad_ref[0] = left.astype(jnp.bfloat16)
    wpad_ref[1] = right.astype(jnp.bfloat16)

    def openings(ids):
        opening = jnp.zeros(ids.shape, jnp.int32)
        end = 0
        for n in range(len_ref.shape[1]):
            end = end + len_ref[0, n]
            opening = jnp.where(ids >= end, end, opening)
        return opening

    ids = r * rows + lax.broadcasted_iota(jnp.int32, (rows, 1), 0)
    position = (few * NREQ + ids - openings(ids)).astype(jnp.float32)
    angle = position * freq_ref[...]
    cosine = jnp.cos(angle)
    sine = jnp.sin(angle)
    sine = jnp.where(lax.broadcasted_iota(jnp.int32, (rows, HD), 1) < HD // 2, -sine, sine)
    for raw, turned in ((raw_k, k_ref), (raw_q, q_ref)):
        for h in range(HEADS):
            part = raw[:, h * HD : (h + 1) * HD].astype(jnp.float32)
            turned[:, h * HD : (h + 1) * HD] = (
                part * cosine + pltpu.roll(part, HD // 2, 1) * sine
            ).astype(jnp.bfloat16)
    kept = [
        pltpu.make_async_copy(k_ref, cache_ref.at[:, pl.ds(0, width)], local_sem.at[8]),
        pltpu.make_async_copy(v_ref, cache_ref.at[:, pl.ds(width, width)], local_sem.at[9]),
    ]
    for d in kept:
        d.start()
    meanwhile()

    pl.semaphore_wait(pltpu.get_barrier_semaphore(), NREQ - 1 + 3)

    started = []

    def start(*a):
        d = copy(*a)
        d.start()
        started.append(d)

    for s in range(1, 4):
        og = flip(g, s)
        start(wpad_ref.at[og % 2], gbuf.at[g], GS + s, r, og)
    for s in range(1, 8):
        t = flip(j, s)
        start(pp_ref.at[t], pbuf.at[j], PB + s, b * 8 + t, g)
    mine = [
        pltpu.make_async_copy(q_ref.at[:, lanes(j)], qbuf.at[j], local_sem.at[0]),
        pltpu.make_async_copy(k_ref.at[:, lanes(j)], kvbuf.at[8 + j, pl.ds(0, rows)], local_sem.at[1]),
        pltpu.make_async_copy(v_ref.at[:, lanes(j)], kvbuf.at[8 + j, pl.ds(rows, rows)], local_sem.at[2]),
        pltpu.make_async_copy(pp_ref.at[j], pbuf.at[j], local_sem.at[3]),
        pltpu.make_async_copy(wpad_ref.at[c], gbuf.at[g], local_sem.at[4]),
    ]
    for d in mine:
        d.start()
    shards = (eg_ref, eu_ref)
    wholes = (wg_ref, wu_ref)

    def piece(owner):
        return pl.ds(pl.multiple_of(owner * eg_ref.shape[0], 16), eg_ref.shape[0])

    take = [pltpu.make_async_copy(shards[n], wholes[n].at[piece(g)], local_sem.at[6 + n]) for n in range(2)]
    for d in take:
        d.start()

    def history(which):
        for s in which:
            t = flip(j, s)
            start(k_ref.at[:, lanes(t)], kvbuf.at[j, pl.ds(0, rows)], HK + s, up * 8 + t, g)
            start(v_ref.at[:, lanes(t)], kvbuf.at[j, pl.ds(rows, rows)], HV + s, up * 8 + t, g)

    history((0, 2, 4, 6))
    mine[4].wait()
    for s in range(1, 4):
        og = flip(g, s)
        copy(gbuf.at[og], gbuf.at[og], GS + s, r, og).wait_recv()
    w16 = (gbuf[0].astype(jnp.float32) + gbuf[1].astype(jnp.float32)) + (
        gbuf[2].astype(jnp.float32) + gbuf[3].astype(jnp.float32))
    my16 = pl.ds(pl.multiple_of(r * 16, 16), 16)
    wbuf[c, my16, :] = w16.astype(jnp.bfloat16)
    mine[3].wait()
    for s in range(1, 8):
        t = flip(j, s)
        copy(pp_ref.at[t], pbuf.at[t], PB + s, b * 8 + t, g).wait_recv()
    rx = flip(j, 1) + b * 8
    start(wbuf.at[c, my16], wbuf.at[c, my16], XS, rx, g)
    for s in range(1, 8):
        start(pbuf, pfx.at[b], PX + s, flip(b, s) * 8 + j, g)
    keep = pltpu.make_async_copy(pbuf, pfx.at[b], local_sem.at[5])
    keep.start()
    ox16 = pl.ds(pl.multiple_of(rx * 16, 16), 16)
    copy(wbuf.at[c, ox16], wbuf.at[c, ox16], XS, rx, g).wait_recv()
    my32 = pl.ds(pl.multiple_of((r // 2) * 32, 32), 32)
    for s in range(1, 8):
        start(wbuf.at[c, my32], wbuf.at[c, my32], ZS + s, y * 16 + flip(z, s) * 2 + xlo, g)
    history((1, 3, 5, 7))
    for s in range(1, 8):
        t = flip(j, s)
        start(q_ref.at[:, lanes(t)], qbuf.at[j], QS + s, b * 8 + t, g)
        start(k_ref.at[:, lanes(t)], kvbuf.at[8 + j, pl.ds(0, rows)], KS + s, b * 8 + t, g)
        start(v_ref.at[:, lanes(t)], kvbuf.at[8 + j, pl.ds(rows, rows)], VS + s, b * 8 + t, g)
    for n in range(2):
        take[n].wait()
        mypiece = wholes[n].at[piece(g)]
        start(mypiece, mypiece, WR + n, r, flip(g, 2))
        start(mypiece, mypiece, WP + n, r, flip(g, 1))
    for s in range(1, 8):
        oz = pl.ds(pl.multiple_of((y * 8 + flip(z, s)) * 32, 32), 32)
        copy(wbuf.at[c, oz], wbuf.at[c, oz], ZS + s, r, g).wait_recv()
    my256 = pl.ds(pl.multiple_of(y * 256, 256), 256)
    for s in range(1, 4):
        start(wbuf.at[c, my256], wbuf.at[c, my256], YS + s, flip(y, s) * 16 + z * 2 + xlo, g)
    start(wbuf.at[c, my256], wbuf.at[c, my256], CS, r, flip(g, 1))

    def hand_over(q):
        oy = pl.ds(pl.multiple_of(flip(y, q) * 256, 256), 256)
        copy(wbuf.at[c, oy], wbuf.at[c, oy], YS + q, r, g).wait_recv()
        start(wbuf.at[c, oy], wbuf.at[c, oy], CS + q, r, flip(g, 1))

    def pass_on(n):
        far = piece(flip(g, 2))
        copy(wholes[n].at[far], wholes[n].at[far], WR + n, r, g).wait_recv()
        start(wholes[n].at[far], wholes[n].at[far], WF + n, r, flip(g, 1))

    keep.wait()
    for s in range(1, 8):
        ob = flip(b, s)
        copy(pbuf, pfx.at[ob], PX + s, r, g).wait_recv()
    pieces = pfx[...].reshape(8 * 8 * 8, HD)
    ii = lax.broadcasted_iota(jnp.int32, (256, 512), 0)
    cc = lax.broadcasted_iota(jnp.int32, (256, 512), 1)
    at = (ii // 4) * 8 + ii % 4
    pk[...] = jnp.dot((cc == at).astype(jnp.bfloat16), pieces, preferred_element_type=jnp.float32).astype(jnp.bfloat16)
    pv[...] = jnp.dot((cc == at + 4).astype(jnp.bfloat16), pieces, preferred_element_type=jnp.float32).astype(jnp.bfloat16)
    for d in mine[:3]:
        d.wait()
    for s in range(1, 8):
        t = flip(j, s)
        copy(qbuf.at[t], qbuf.at[t], QS + s, r, g).wait_recv()
        copy(kvbuf.at[8 + t, pl.ds(0, rows)], kvbuf.at[8 + t, pl.ds(0, rows)], KS + s, r, g).wait_recv()
        copy(kvbuf.at[8 + t, pl.ds(rows, rows)], kvbuf.at[8 + t, pl.ds(rows, rows)], VS + s, r, g).wait_recv()
    for s in range(8):
        t = flip(j, s)
        copy(kvbuf.at[t, pl.ds(0, rows)], kvbuf.at[t, pl.ds(0, rows)], HK + s, r, g).wait_recv()
        copy(kvbuf.at[t, pl.ds(rows, rows)], kvbuf.at[t, pl.ds(rows, rows)], HV + s, r, g).wait_recv()

    span = rows * HEADS
    nwin = span + rows

    def attend(t):
        q_id = b * span + t * rows + lax.broadcasted_iota(jnp.int32, (rows, 1), 0)
        opening = openings(q_id)
        first = b * span - span + t * rows
        k_id = first + lax.broadcasted_iota(jnp.int32, (rows, nwin), 1)
        q = qbuf[t]
        kw = kvbuf[pl.ds(t, 9), pl.ds(0, rows), :].reshape(nwin, HD)
        vw = kvbuf[pl.ds(t, 9), pl.ds(rows, rows), :].reshape(nwin, HD)
        dims = (((1,), (1,)), ((), ()))
        s1 = lax.dot_general(q, pk[...], dims, preferred_element_type=jnp.float32) * HD ** (-0.5)
        s2 = lax.dot_general(q, kw, dims, preferred_element_type=jnp.float32) * HD ** (-0.5)
        s2 = jnp.where((k_id >= opening) & (k_id <= q_id), s2, -1e30)
        top = jnp.maximum(jnp.max(s1, axis=1, keepdims=True), jnp.max(s2, axis=1, keepdims=True))
        w1 = jnp.exp(s1 - top)
        w2 = jnp.exp(s2 - top)
        total = jnp.sum(w1, axis=1, keepdims=True) + jnp.sum(w2, axis=1, keepdims=True)
        o = jnp.dot(w1.astype(jnp.bfloat16), pv[...], preferred_element_type=jnp.float32)
        o = o + jnp.dot(w2.astype(jnp.bfloat16), vw, preferred_element_type=jnp.float32)
        return (o / total).astype(jnp.bfloat16)

    for s in range(1, 8):
        if s in (5, 6, 7):
            hand_over(s - 4)
        t = flip(j, s)
        osend[t] = attend(t)
        start(osend.at[t], obuf.at[j], OS + s, b * 8 + t, g)
    obuf[j] = attend(j)
    for s in range(1, 8):
        t = flip(j, s)
        copy(obuf.at[t], obuf.at[t], OS + s, r, g).wait_recv()
    pass_on(0)
    for q in range(4):
        oy = pl.ds(pl.multiple_of(flip(y, q) * 256, 256), 256)
        copy(wbuf.at[1 - c, oy], wbuf.at[1 - c, oy], CS + q, r, g).wait_recv()

    attn = jnp.concatenate([obuf[h] for h in range(HEADS)], axis=1)
    wide = 256
    per = wbuf.shape[2] // wide
    total = jnp.zeros((rows, 1), jnp.float32)
    for n in range(2 * per):
        cols = pl.ds(n * wide, wide)
        part = jnp.dot(attn, wbuf[n // per, :, pl.ds((n % per) * wide, wide)], preferred_element_type=jnp.float32)
        part = resid_ref[:, cols].astype(jnp.float32) + part
        state_ref[:, cols] = part
        total = total + jnp.sum(part * part, axis=1, keepdims=True)
    inv = lax.rsqrt(total / D + EPSILON)
    for n in range(2 * per):
        cols = pl.ds(n * wide, wide)
        normed_ref[:, cols] = (state_ref[:, cols] * inv * gain_ref[:, cols]).astype(jnp.bfloat16)
    pass_on(1)

    def weights_in():
        for n in range(2):
            near = piece(flip(g, 1))
            copy(wholes[n].at[near], wholes[n].at[near], WP + n, r, g).wait_recv()
            last = piece(flip(g, 3))
            copy(wholes[n].at[last], wholes[n].at[last], WF + n, r, g).wait_recv()

    def finish():
        for d in kept:
            d.wait()
        for d in started:
            d.wait_send()

    return weights_in, finish


def layer_kernel(
    raw_q, raw_k, v_ref, px_ref, ow_ref, resid_ref, gain_ref, freq_ref,
    rcols_ref, rw_ref, router_ref, len_ref,
    egate_ref, eup_ref, edown_ref, sgate_ref, sup_ref, sdown_ref,
    out_ref, cache_ref, partner_ref,
    state_ref, normed_ref,
    hit_t, mix_hi, mix_lo, outb, outc, arrb, arrc, finb, finc, retb, retc, shard, part, parts, acc,
    wg, wu, wd, sg, su, sd,
    send_sem, recv_sem, grp_send, grp_recv, local_sem,
    k_turned, *attention_scratch,
):
    r = lax.axis_index("req")
    g = lax.axis_index("grp")
    y = r // 16
    low = r % 16
    rows = normed_ref.shape[0]
    bf = jnp.bfloat16
    f32 = jnp.float32

    def slot_maps(shape, axis, p):
        i = lax.broadcasted_iota(jnp.int32, shape, axis)
        first = i < 16 * MAIN
        rest = i - 16 * MAIN
        return (p * 16 + jnp.where(first, i // MAIN, rest // MORE),
                jnp.where(first, i % MAIN, MAIN + rest % MORE))

    def xor(a, b, bits):
        out = 0
        bit = 1
        for _ in range(bits):
            out = out + bit * (((a // bit) % 2 + (b // bit) % 2) % 2)
            bit *= 2
        return out

    span = edown_ref.shape[0]

    def piece(owner):
        return pl.ds(pl.multiple_of(owner * span, 16), span)

    barrier = pltpu.get_barrier_semaphore()

    def greet(s, _):
        peer = xor(y, s // 16, 2) * 16 + xor(low, s % 16, 4)
        pl.semaphore_signal(barrier, inc=1, device_id=(peer, g), device_id_type=MESH)
        return 0

    lax.fori_loop(1, NREQ, greet, 0)
    for s in range(1, 4):
        pl.semaphore_signal(barrier, inc=1, device_id=(r, xor(g, s, 2)), device_id_type=MESH)

    loads = [
        pltpu.make_async_copy(src, dst, local_sem.at[n])
        for n, (src, dst) in enumerate(
            [(edown_ref, wd.at[piece(g)]), (sgate_ref, sg), (sup_ref, su), (sdown_ref, sd)]
        )
    ]
    for d in loads:
        d.start()
    maps = []

    def places():
        ei = lax.broadcasted_iota(jnp.int32, (NREQ, rows), 0)
        named_t = jnp.zeros((NREQ, rows), f32)
        for k in range(TOP):
            named_t = named_t + (rcols_ref[k : k + 1, :] == ei).astype(f32)
        ti = lax.broadcasted_iota(jnp.int32, (rows, rows), 0)
        tj = lax.broadcasted_iota(jnp.int32, (rows, rows), 1)
        slot_t = jnp.dot(named_t.astype(bf), (ti < tj).astype(bf), preferred_element_type=f32)
        for p in range(4):
            expert_of = slot_maps((PLANE, NREQ), 0, p)[0]
            widen_t = (expert_of == lax.broadcasted_iota(jnp.int32, (PLANE, NREQ), 1)).astype(bf)
            mine = jnp.dot(widen_t, named_t.astype(bf), preferred_element_type=f32)
            spot = jnp.dot(widen_t, slot_t.astype(bf), preferred_element_type=f32)
            want = slot_maps((PLANE, rows), 0, p)[1].astype(f32)
            hit_t[p] = jnp.where(spot == want, mine, 0.0).astype(bf)
        maps.extend((ei, ti, slot_t))

    weights_in, finish = attention_part(
        places, raw_q, raw_k, v_ref, px_ref, ow_ref, resid_ref, gain_ref, len_ref, freq_ref, egate_ref, eup_ref,
        cache_ref, state_ref, normed_ref, wg, wu,
        attention_scratch[0], k_turned, *attention_scratch[1:],
    )
    ei, ti, slot_t = maps

    def rcopy(src, dst, idx, req):
        return pltpu.make_async_remote_copy(
            src_ref=src, dst_ref=dst, send_sem=send_sem.at[idx], recv_sem=recv_sem.at[idx],
            device_id=(req, g), device_id_type=MESH)

    def gcopy(src, dst, idx, grp):
        return pltpu.make_async_remote_copy(
            src_ref=src, dst_ref=dst, send_sem=grp_send.at[idx], recv_sem=grp_recv.at[idx],
            device_id=(r, grp), device_id_type=MESH)

    def pair(b8, b2, i, to8, to2, o, idx, req):
        return (rcopy(b8.at[i], to8.at[o], idx, req), rcopy(b2.at[i], to2.at[o], idx + NREQ, req))

    def halves(v):
        cut = 16 * MAIN
        return v[:cut].reshape(16, MAIN, v.shape[1]), v[cut:].reshape(16, MORE, v.shape[1])

    def dispatch(k, _):
        plane = xor(y, k, 2)
        put = hit_t[plane]
        for n in range(4):
            cols = pl.ds(n * 512, 512)
            block = jnp.dot(put, normed_ref[:, cols], preferred_element_type=f32).astype(bf)
            outb[pl.ds(plane * 16, 16), :, cols], outc[pl.ds(plane * 16, 16), :, cols] = halves(block)

        def one(m, _):
            e = plane * 16 + xor(low, m, 4)
            for d in pair(outb, outc, e, arrb, arrc, r, k * 16 + m, e):
                d.start()
            return 0

        lax.fori_loop(jnp.where(k == 0, 1, 0), 16, one, 0)
        return 0

    lax.fori_loop(0, 2, dispatch, 0)
    far = xor(g, 2, 2)
    other = xor(g, 1, 2)
    loads[0].wait()
    gcopy(wd.at[piece(g)], wd.at[piece(g)], 8, far).start()
    gcopy(wd.at[piece(g)], wd.at[piece(g)], 9, other).start()
    own = [
        pltpu.make_async_copy(outb.at[r], arrb.at[r], local_sem.at[6]),
        pltpu.make_async_copy(outc.at[r], arrc.at[r], local_sem.at[10]),
    ]
    for d in own:
        d.start()
    gcopy(normed_ref, shard.at[g], 2, xor(g, 2, 2)).start()
    gcopy(normed_ref, shard.at[g], 1, xor(g, 1, 2)).start()
    keep = pltpu.make_async_copy(normed_ref, shard.at[g], local_sem.at[7])
    keep.start()
    lax.fori_loop(2, 4, dispatch, 0)

    heft = jnp.zeros((NREQ, rows), f32)
    for k in range(TOP):
        heft = heft + jnp.where(rcols_ref[k : k + 1, :] == ei, rw_ref[k : k + 1, :], 0.0)
    heft_hi = heft.astype(bf)
    heft_lo = (heft - heft_hi.astype(f32)).astype(bf)
    tn = (((0,), (0,)), ((), ()))
    for p in range(4):
        expert_of = slot_maps((NREQ, PLANE), 1, p)[0]
        widen = (expert_of == lax.broadcasted_iota(jnp.int32, (NREQ, PLANE), 0)).astype(bf)
        spot = lax.dot_general(slot_t.astype(bf), widen, tn, preferred_element_type=f32)
        hit = spot == slot_maps((rows, PLANE), 1, p)[1].astype(f32)
        mix_hi[p] = jnp.where(hit, lax.dot_general(heft_hi, widen, tn, preferred_element_type=f32), 0.0).astype(bf)
        mix_lo[p] = jnp.where(hit, lax.dot_general(heft_lo, widen, tn, preferred_element_type=f32), 0.0).astype(bf)
    scale = jax.nn.sigmoid(
        jnp.sum(normed_ref[...].astype(f32) * router_ref[...].astype(f32), axis=1, keepdims=True)
    )
    gcopy(wd.at[piece(far)], wd.at[piece(far)], 8, far).wait_recv()
    gcopy(wd.at[piece(far)], wd.at[piece(far)], 10, other).start()
    gcopy(shard.at[far], shard.at[far], 2, far).wait_recv()
    gcopy(shard.at[far], shard.at[far], 3, other).start()
    weights_in()
    gcopy(wd.at[piece(other)], wd.at[piece(other)], 9, other).wait_recv()
    last = piece(xor(g, 3, 2))
    gcopy(wd.at[last], wd.at[last], 10, other).wait_recv()
    for d in own:
        d.wait()
    nt = (((1,), (1,)), ((), ()))

    def expert(k, _):
        plane = xor(y, k, 2)

        def got(m, _):
            e = plane * 16 + xor(low, m, 4)
            for d in pair(arrb, arrc, e, arrb, arrc, e, k * 16 + m, e):
                d.wait_recv()
            return 0

        lax.fori_loop(jnp.where(k == 0, 1, 0), 16, got, 0)
        x = jnp.concatenate(
            [arrb[pl.ds(plane * 16, 16)].reshape(16 * MAIN, D), arrc[pl.ds(plane * 16, 16)].reshape(16 * MORE, D)],
            axis=0,
        )
        gate = lax.dot_general(x, wg[...], nt, preferred_element_type=f32)
        up = lax.dot_general(x, wu[...], nt, preferred_element_type=f32)
        hidden = (jax.nn.silu(gate) * up).astype(bf)
        for n in range(4):
            cols = pl.ds(n * 512, 512)
            o = jnp.dot(hidden, wd[:, cols], preferred_element_type=f32).astype(bf)
            finb[pl.ds(plane * 16, 16), :, cols], finc[pl.ds(plane * 16, 16), :, cols] = halves(o)

        def back(m, _):
            e = plane * 16 + xor(low, m, 4)
            for d in pair(finb, finc, e, retb, retc, r, 128 + k * 16 + m, e):
                d.start()
            return 0

        lax.fori_loop(jnp.where(k == 0, 1, 0), 16, back, 0)
        return 0

    lax.fori_loop(0, 2, expert, 0)
    home = [
        pltpu.make_async_copy(finb.at[r], retb.at[r], local_sem.at[8]),
        pltpu.make_async_copy(finc.at[r], retc.at[r], local_sem.at[11]),
    ]
    for d in home:
        d.start()

    for d in loads[1:]:
        d.wait()
    keep.wait()
    for s in (1, 3):
        og = xor(g, s, 2)
        gcopy(shard.at[og], shard.at[og], s, og).wait_recv()
    for h in range(2):
        x = shard[2 * h : 2 * h + 2].reshape(2 * rows, D)
        gate = lax.dot_general(x, sg[...], nt, preferred_element_type=f32)
        up = lax.dot_general(x, su[...], nt, preferred_element_type=f32)
        hidden = (jax.nn.silu(gate) * up).astype(bf)
        for n in range(4):
            cols = pl.ds(n * 512, 512)
            o = jnp.dot(hidden, sd[:, cols], preferred_element_type=f32).astype(bf)
            part[2 * h : 2 * h + 2, :, cols] = o.reshape(2, rows, 512)
    gcopy(part.at[xor(g, 3, 2)], parts.at[3], 6, other).start()
    gcopy(part.at[other], parts.at[1], 5, other).start()

    lax.fori_loop(2, 3, expert, 0)
    gcopy(parts.at[3], parts.at[3], 6, other).wait_recv()
    parts[0] = (part[far].astype(f32) + parts[3].astype(f32)).astype(bf)
    lax.fori_loop(3, 4, expert, 0)
    gcopy(parts.at[0], parts.at[2], 7, far).start()
    width = HEADS * HD
    swaps = [
        gcopy(k_turned, partner_ref.at[:, pl.ds(0, width)], 11, far),
        gcopy(v_ref, partner_ref.at[:, pl.ds(width, width)], 4, far),
    ]
    for d in swaps:
        d.start()
    for d in home:
        d.wait()
    for s in (1, 2):
        gcopy(parts.at[s], parts.at[s], 4 + s if s == 1 else 7, other).wait_recv()
    for n in range(4):
        cols = pl.ds(n * 512, 512)
        total = (part[g, :, cols].astype(f32) + parts[1, :, cols].astype(f32)) + parts[2, :, cols].astype(f32)
        acc[:, cols] = state_ref[:, cols] + scale * total

    def gather(k, _):
        plane = xor(y, k, 2)

        def got(m, _):
            e = plane * 16 + xor(low, m, 4)
            for d in pair(retb, retc, e, retb, retc, e, 128 + k * 16 + m, e):
                d.wait_recv()
            return 0

        lax.fori_loop(jnp.where(k == 0, 1, 0), 16, got, 0)
        hi = mix_hi[plane]
        lo = mix_lo[plane]
        for n in range(4):
            cols = pl.ds(n * 512, 512)
            v = jnp.concatenate(
                [retb[pl.ds(plane * 16, 16), :, cols].reshape(16 * MAIN, 512),
                 retc[pl.ds(plane * 16, 16), :, cols].reshape(16 * MORE, 512)],
                axis=0,
            )
            acc[:, cols] += jnp.dot(hi, v, preferred_element_type=f32) + jnp.dot(lo, v, preferred_element_type=f32)
        return 0

    lax.fori_loop(0, 4, gather, 0)
    out_ref[...] = acc[...].astype(bf)

    def sent(s, _):
        for d in pair(outb, outc, 0, arrb, arrc, 0, s, r) + pair(finb, finc, 0, retb, retc, 0, 128 + s, r):
            d.wait_send()
        return 0

    lax.fori_loop(1, NREQ, sent, 0)
    for s in range(1, 4):
        gcopy(normed_ref, shard.at[g], s, g).wait_send()
        gcopy(part.at[0], parts.at[g], 4 + s, g).wait_send()
        gcopy(wd.at[piece(g)], wd.at[piece(g)], 7 + s, g).wait_send()
    for d in swaps:
        d.wait()
    finish()


def layer(blocks, lengths, bulk):
    rows = blocks[0].shape[0]
    vm = pl.BlockSpec(memory_space=pltpu.VMEM)
    hb = pl.BlockSpec(memory_space=pltpu.HBM)
    bf = jnp.bfloat16
    wide = (4 * bulk[0].shape[0], D)
    return pl.pallas_call(
        layer_kernel,
        out_shape=(jax.ShapeDtypeStruct((rows, D), bf),) * 3,
        in_specs=[vm] * len(blocks) + [pl.BlockSpec(memory_space=pltpu.SMEM)] + [hb] * len(bulk),
        out_specs=(vm, hb, hb),
        scratch_shapes=[
            pltpu.VMEM((rows, D), jnp.float32),
            pltpu.VMEM((rows, D), bf),
            pltpu.VMEM((4, PLANE, rows), bf),
            pltpu.VMEM((4, rows, PLANE), bf),
            pltpu.VMEM((4, rows, PLANE), bf),
        ] + [
            pltpu.VMEM((NREQ, few, D), bf) for _ in range(4) for few in (MAIN, MORE)
        ] + [
            pltpu.VMEM((4, rows, D), bf),
            pltpu.VMEM((4, rows, D), bf),
            pltpu.VMEM((4, rows, D), bf),
            pltpu.VMEM((rows, D), jnp.float32),
        ] + [
            pltpu.VMEM(wide, bf) for _ in range(6)
        ] + [
            pltpu.SemaphoreType.DMA((4 * NREQ,)),
            pltpu.SemaphoreType.DMA((4 * NREQ,)),
            pltpu.SemaphoreType.DMA((12,)),
            pltpu.SemaphoreType.DMA((12,)),
            pltpu.SemaphoreType.DMA((12,)),
            pltpu.VMEM((rows, HEADS * HD), bf),
            pltpu.VMEM((rows, HEADS * HD), bf),
            pltpu.VMEM((8, 8, HD), bf),
            pltpu.VMEM((2, 16, D // 2), bf),
            pltpu.VMEM((8, rows, HD), bf),
            pltpu.VMEM((16, 2 * rows, HD), bf),
            pltpu.VMEM((8, 8, HD), bf),
            pltpu.VMEM((8, 8, 8, HD), bf),
            pltpu.VMEM((8, rows, HD), bf),
            pltpu.VMEM((8, rows, HD), bf),
            pltpu.VMEM((4, 16, D // 2), bf),
            pltpu.VMEM((2, HEADS * HD, D // 2), bf),
            pltpu.VMEM((256, HD), bf),
            pltpu.VMEM((256, HD), bf),
            pltpu.SemaphoreType.DMA((NSEM,)),
            pltpu.SemaphoreType.DMA((NSEM,)),
            pltpu.SemaphoreType.DMA((10,)),
        ],
        compiler_params=pltpu.CompilerParams(
            collective_id=0, has_side_effects=True, vmem_limit_bytes=63 << 20
        ),
        cost_estimate=pl.CostEstimate(flops=16_000_000_000, bytes_accessed=60_000_000, transcendentals=3_000_000),
        name="layer",
    )(*blocks, lengths, *bulk)


def local(
    suffix_queries,
    suffix_keys,
    suffix_values,
    prefix_cache,
    residual,
    out_weight,
    norm_gain,
    routes,
    route_weights,
    lengths,
    migrate,
    expert_gate,
    expert_up,
    expert_down,
    shared_gate,
    shared_up,
    shared_down,
    shared_router,
):
    grp = lax.axis_index("grp")
    half = jnp.arange(HD // 2, dtype=jnp.float32)
    freq = jnp.power(ROPE_BASE, -2.0 * half / HD)
    blocks = (
        suffix_queries[0], suffix_keys[0], suffix_values[0], prefix_cache[0], out_weight, residual[0],
        norm_gain[None], jnp.concatenate([freq, freq])[None],
        routes[0].T, route_weights[0].T, shared_router.astype(jnp.float32)[None],
    )
    bulk = (
        jnp.swapaxes(expert_gate[0], 0, 1), jnp.swapaxes(expert_up[0], 0, 1), expert_down[0],
        shared_gate.T, shared_up.T, shared_down,
    )
    final, own_cache, partner = layer(blocks, lengths, bulk)
    pair_row = grp // 4 * 2 + grp % 2
    page_flags = jnp.sum(
        jnp.where((jnp.arange(migrate.shape[0], dtype=jnp.int32) == pair_row)[:, None], migrate, 0),
        axis=0,
    )
    page_moved = jnp.repeat(page_flags, PG) == 1
    suffix_cache = jnp.where(page_moved[:, None], partner, own_cache)
    return (final[None], suffix_cache[None])


def solution(mesh):
    placed = (
        P("grp", "req", None),
        P("grp", "req", None),
        P("grp", "req", None),
        P("grp", "req", None),
        P("grp", "req", None),
        P(("req", "grp"), None),
        P(),
        P("grp", "req", None),
        P("grp", "req", None),
        P("grp", None),
        P(None, "req"),
        P("req", None, "grp"),
        P("req", None, "grp"),
        P("req", "grp", None),
        P(None, "grp"),
        P(None, "grp"),
        P("grp", None),
        P(),
    )
    return jax.shard_map(
        local,
        mesh=mesh,
        in_specs=placed,
        out_specs=(P("grp", "req", None), P("grp", "req", None)),
        check_vma=False,
    )
```
